32 devices in a mesh: clip: 4 (over y, x), blk: 8 (over z, core).
Axes of the slice: x: 2, y: 2, z: 4, core: 2. Of those that a mesh axis runs over, the one named last changes fastest.
Arguments:
- frames: bfloat16 [4, 2048, 1024], P('clip', 'blk'), may hold values from -6 to 6
- text_states: bfloat16 [4, 256, 1024], P('clip'), may hold values from -6 to 6
- prompt_lengths: int32 [4], P('clip'), may hold values from 1 to 256, as said below
- cotangent: bfloat16 [4, 2048, 1024], P('clip', 'blk'), may hold values from -6 to 6
- self_query: bfloat16 [1024, 1024], replicated, may hold values from -0.1875 to 0.1875
- self_key: bfloat16 [1024, 1024], replicated, may hold values from -0.1875 to 0.1875
- self_value: bfloat16 [1024, 1024], replicated, may hold values from -0.1875 to 0.1875
- self_out: bfloat16 [1024, 1024], replicated, may hold values from -1 to 1
- cross_query: bfloat16 [1024, 1024], replicated, may hold values from -0.1875 to 0.1875
- cross_key: bfloat16 [1024, 1024], replicated, may hold values from -0.1875 to 0.1875
- cross_value: bfloat16 [1024, 1024], replicated, may hold values from -0.1875 to 0.1875
- cross_out: bfloat16 [1024, 1024], replicated, may hold values from -0.75 to 0.75
- hidden_in: bfloat16 [1024, 4096], replicated, may hold values from -0.1875 to 0.1875
- hidden_out: bfloat16 [4096, 1024], replicated, may hold values from -0.09375 to 0.09375
- first_gain: float32 [1024], replicated, may hold values from 0.25 to 1.75
- first_shift: float32 [1024], replicated, may hold values from -3 to 3
- second_gain: float32 [1024], replicated, may hold values from 0.25 to 1.75
- second_shift: float32 [1024], replicated, may hold values from -3 to 3
- third_gain: float32 [1024], replicated, may hold values from 0.25 to 1.75
- third_shift: float32 [1024], replicated, may hold values from -3 to 3
Outputs:
- output_frames: bfloat16 [4, 2048, 1024], P('clip', 'blk')
- frames_grad: float32 [4, 2048, 1024], P('clip', 'blk')
- text_grad: float32 [4, 256, 1024], P('clip', 'blk')
- self_query_grad: float32 [1024, 1024], P(('clip', 'blk'))
- self_key_grad: float32 [1024, 1024], P(('clip', 'blk'))
- self_value_grad: float32 [1024, 1024], P(('clip', 'blk'))
- self_out_grad: float32 [1024, 1024], P(('clip', 'blk'))
- cross_query_grad: float32 [1024, 1024], P(('clip', 'blk'))
- cross_key_grad: float32 [1024, 1024], P(('clip', 'blk'))
- cross_value_grad: float32 [1024, 1024], P(('clip', 'blk'))
- cross_out_grad: float32 [1024, 1024], P(('clip', 'blk'))
- hidden_in_grad: float32 [1024, 4096], P(('clip', 'blk'))
- hidden_out_grad: float32 [4096, 1024], P(('clip', 'blk'))
- first_gain_grad: float32 [1024], P(('clip', 'blk'))
- first_shift_grad: float32 [1024], P(('clip', 'blk'))
- second_gain_grad: float32 [1024], P(('clip', 'blk'))
- second_shift_grad: float32 [1024], P(('clip', 'blk'))
- third_gain_grad: float32 [1024], P(('clip', 'blk'))
- third_shift_grad: float32 [1024], P(('clip', 'blk'))
The draws below stay inside these ranges and needn't reach their ends.
Inputs may be any that keep to these rules, and one draw needn't show every extreme that they name: Each clip's prompt fills its first prompt_lengths tokens of the 256 padded ones. In every draw one clip's prompt fills all 256; the others are at most 64.
All inputs are finite; a program needn't handle non-finite values.
Results may differ from the reference program's by a relative error of at most 0.025.
Values may be sent and summed in bfloat16 or wider, within the bound.
A program may use at most 256 MiB of HBM per device.

```python
import math
import jax
import jax.numpy as jnp
from jax import lax

D = 1024
HEADS = 16
HEAD = 64
FF = 4096
TEXT = 256
CLIPS = 4
SEQ = 2048


def draw_prompt_lengths(key, part):
    shorter = jax.random.randint(jax.random.fold_in(key, 11), (CLIPS,), 1, TEXT // 4 + 1)
    filled = jax.random.randint(jax.random.fold_in(key, 12), (), 0, CLIPS)
    return jnp.where(jnp.arange(CLIPS) == filled, TEXT, shorter).astype(jnp.int32)


def block_scale(stream_key, dims, cuts, least, high):
    def one(position, parts):
        draws = jax.random.uniform(jax.random.fold_in(jax.random.fold_in(stream_key, 6), position), (parts,), jnp.float32, least / len(cuts), high / len(cuts))
        return jnp.repeat(jnp.exp(draws), dims[position] // parts).reshape((-1,) + (1,) * (len(dims) - position - 1))

    gain = one(*cuts[0])
    for cut in cuts[1:]:
        gain = gain * one(*cut)
    return gain


def bell_draw(key, dims, deviation, most, shards=(), kind=jnp.bfloat16):
    array = jax.random.normal(key, dims, jnp.float32) * deviation
    if len(shards) > 0:
        array = block_scale(key, dims, shards, -0.22, 0.18) * array
    return jnp.clip(array, min=-most, max=most).astype(kind)


def setup_inputs(seed: int = 0) -> dict:
    key_of = jax.random.split(jax.random.key(seed), 21)
    return {
        "frames": bell_draw(key_of[0], (CLIPS, SEQ, D), 1.0, 6.0, ((0, 4), (1, 8))),
        "text_states": bell_draw(key_of[1], (CLIPS, TEXT, D), 1.0, 6.0, ((0, 4),)),
        "prompt_lengths": draw_prompt_lengths(jax.random.fold_in(key_of[20], 71), 0),
        "cotangent": bell_draw(key_of[3], (CLIPS, SEQ, D), 1.0, 6.0, ((0, 4), (1, 8))),
        "self_query": bell_draw(key_of[4], (D, D), D ** -0.5, 0.1875),
        "self_key": bell_draw(key_of[5], (D, D), D ** -0.5, 0.1875),
        "self_value": bell_draw(key_of[6], (D, D), D ** -0.5, 0.1875),
        "self_out": bell_draw(key_of[7], (D, D), (HEAD // 2) ** -0.5, 1.0),
        "cross_query": bell_draw(key_of[8], (D, D), D ** -0.5, 0.1875),
        "cross_key": bell_draw(key_of[9], (D, D), D ** -0.5, 0.1875),
        "cross_value": bell_draw(key_of[10], (D, D), D ** -0.5, 0.1875),
        "cross_out": bell_draw(key_of[11], (D, D), HEAD ** -0.5, 0.75),
        "hidden_in": bell_draw(key_of[12], (D, FF), D ** -0.5, 0.1875),
        "hidden_out": bell_draw(key_of[13], (FF, D), FF ** -0.5, 0.09375),
        "first_gain": jnp.clip(1.0 + 0.15 * jax.random.normal(key_of[14], (D,), jnp.float32), 0.25, 1.75),
        "first_shift": bell_draw(key_of[15], (D,), 0.5, 3.0, (), jnp.float32),
        "second_gain": jnp.clip(1.0 + 0.15 * jax.random.normal(key_of[16], (D,), jnp.float32), 0.25, 1.75),
        "second_shift": bell_draw(key_of[17], (D,), 0.5, 3.0, (), jnp.float32),
        "third_gain": jnp.clip(1.0 + 0.15 * jax.random.normal(key_of[18], (D,), jnp.float32), 0.25, 1.75),
        "third_shift": bell_draw(key_of[19], (D,), 0.5, 3.0, (), jnp.float32),
    }


highest = lax.Precision.HIGHEST

@jax.custom_vjp
def low(v):
    return lax.optimization_barrier(v.astype(jnp.bfloat16)).astype(jnp.float32)

@jax.custom_vjp
def low_back(v):
    return v

def low_keep(v):
    return (low(v), None)

def low_pass(kept, grad):
    return (grad,)

def back_keep(v):
    return (v, None)

def back_low(kept, grad):
    return (low(grad),)
low.defvjp(low_keep, low_pass)
low_back.defvjp(back_keep, back_low)

def layer_norm(inputs, gain_vec, shift_vec):
    centred = inputs - lax.optimization_barrier(jnp.mean(inputs, axis=-1, keepdims=True))
    variance = lax.optimization_barrier(jnp.mean(centred * centred, axis=-1, keepdims=True))
    return centred * lax.rsqrt(variance + 1e-05) * gain_vec + shift_vec

def rounded(inputs):
    return low_back(low(inputs))

def matmul(left, right):
    return jnp.dot(left, right, precision=highest, preferred_element_type=jnp.float32)

def softmax_rows(scores):
    top_score = lax.optimization_barrier(jnp.max(scores, axis=-1, keepdims=True))
    weights = jnp.exp(scores - top_score)
    return weights / lax.optimization_barrier(jnp.sum(weights, axis=-1, keepdims=True))

def self_attention(queries, keys_in, values_in):
    block_rows = math.gcd(512, SEQ)
    block_count = SEQ // block_rows
    query_blocks = queries.reshape(block_count, block_rows, HEADS, HEAD)
    key_heads = keys_in.reshape(SEQ, HEADS, HEAD)
    value_heads = values_in.reshape(SEQ, HEADS, HEAD)
    block_starts = jnp.arange(block_count, dtype=jnp.int32) * block_rows
    key_index = jnp.arange(SEQ, dtype=jnp.int32)

    def one_block(block_item):
        query_block, start_row = block_item
        row_index = start_row + jnp.arange(block_rows, dtype=jnp.int32)
        scores = jnp.einsum('qhd,khd->hqk', query_block, key_heads, precision=highest) * 0.125
        allowed = key_index[None, :] <= row_index[:, None]
        scores = low_back(jnp.where(allowed[None], scores, -1e+30))
        weights = low(softmax_rows(scores))
        return jnp.einsum('hqk,khd->qhd', weights, value_heads, precision=highest)
    attended = lax.map(jax.checkpoint(one_block), (query_blocks, block_starts))
    return attended.reshape(SEQ, D)

def cross_attention(queries, keys_in, values_in, prompt_len):
    scores = jnp.einsum('qhd,khd->hqk', queries.reshape(SEQ, HEADS, HEAD), keys_in.reshape(TEXT, HEADS, HEAD), precision=highest) * 0.125
    visible = jnp.arange(TEXT, dtype=jnp.int32) < prompt_len
    scores = low_back(jnp.where(visible[None, None, :], scores, -1e+30))
    weights = low(softmax_rows(scores))
    attended = jnp.einsum('hqk,khd->qhd', weights, values_in.reshape(TEXT, HEADS, HEAD), precision=highest)
    return attended.reshape(SEQ, D)

def clip_layer(clip_frames, clip_text, weight_set, prompt_len):
    self_query, self_key, self_value, self_out, cross_query, cross_key, cross_value, cross_out, hidden_in, hidden_out, first_gain, first_shift, second_gain, second_shift, third_gain, third_shift = weight_set
    normed_one = low(layer_norm(clip_frames, first_gain, first_shift))
    queries = rounded(matmul(normed_one, self_query))
    keys_in = rounded(matmul(normed_one, self_key))
    values_in = rounded(matmul(normed_one, self_value))
    attended = self_attention(queries, keys_in, values_in)
    after_self = clip_frames + low_back(matmul(rounded(attended), self_out))
    normed_two = low(layer_norm(after_self, second_gain, second_shift))
    cross_queries = rounded(matmul(normed_two, cross_query))
    text_keys = rounded(matmul(clip_text, cross_key))
    text_values = rounded(matmul(clip_text, cross_value))
    mixed = cross_attention(cross_queries, text_keys, text_values, prompt_len)
    after_cross = after_self + low_back(matmul(rounded(mixed), cross_out))
    normed_three = low(layer_norm(after_cross, third_gain, third_shift))
    hidden = low(jax.nn.gelu(low_back(matmul(normed_three, hidden_in)), approximate=False))
    return after_cross + low_back(matmul(hidden, hidden_out))

def reference(frames, text_states, prompt_lengths, cotangent, self_query, self_key, self_value, self_out, cross_query, cross_key, cross_value, cross_out, hidden_in, hidden_out, first_gain, first_shift, second_gain, second_shift, third_gain, third_shift):
    weight_set = (self_query.astype(jnp.float32), self_key.astype(jnp.float32), self_value.astype(jnp.float32), self_out.astype(jnp.float32), cross_query.astype(jnp.float32), cross_key.astype(jnp.float32), cross_value.astype(jnp.float32), cross_out.astype(jnp.float32), hidden_in.astype(jnp.float32), hidden_out.astype(jnp.float32), first_gain.astype(jnp.float32), first_shift.astype(jnp.float32), second_gain.astype(jnp.float32), second_shift.astype(jnp.float32), third_gain.astype(jnp.float32), third_shift.astype(jnp.float32))

    def one_clip(totals, clip_item):
        clip_frames, clip_text, prompt_len, clip_cot = clip_item

        def forward(frames_in, text_in, weights_in):
            return clip_layer(frames_in, text_in, weights_in, prompt_len)
        result, pullback = jax.vjp(forward, clip_frames.astype(jnp.float32), clip_text.astype(jnp.float32), weight_set)
        frame_grad, text_grad, weight_grads = pullback(clip_cot.astype(jnp.float32))
        totals = jax.tree.map(jnp.add, totals, weight_grads)
        return (totals, (result.astype(jnp.bfloat16), frame_grad, text_grad))
    zero_set = jax.tree.map(jnp.zeros_like, weight_set)
    totals, (outputs, frame_grads, text_grads) = lax.scan(one_clip, zero_set, (frames, text_states, prompt_lengths, cotangent))
    return (outputs, frame_grads, text_grads, totals[0], totals[1], totals[2], totals[3], totals[4], totals[5], totals[6], totals[7], totals[8], totals[9], totals[10], totals[11], totals[12], totals[13], totals[14], totals[15])
```

```python
from functools import partial
import math

import jax
import jax.numpy as jnp
from jax import lax
from jax.experimental import pallas as pl
from jax.experimental.pallas import tpu as pltpu
from jax.sharding import PartitionSpec as P

D = 1024
HEADS = 16
HEAD = 64
TEXT = 256
MESH = pl.DeviceIdType.MESH


def shifted(block, axis, distance):
    devices = range(lax.axis_size(axis))
    route = [((i - distance) % len(devices), i) for i in devices]
    return lax.ppermute(block, axis, route)


def shifted_2(block, axis, distance):
    devices = range(lax.axis_size(axis))
    route = [(i - distance, i) for i in devices if i - distance in devices]
    return lax.ppermute(block, axis, route)


def layer_norm(inputs, gain_vec, shift_vec):
    centred = inputs - jnp.mean(inputs, axis=-1, keepdims=True)
    variance = jnp.mean(centred * centred, axis=-1, keepdims=True)
    return centred * lax.rsqrt(variance + 1e-05) * gain_vec + shift_vec


def project(left, right):
    return jnp.dot(left, right, preferred_element_type=jnp.float32)


def weight_term(left, right):
    return jnp.einsum("td,te->de", left, right, preferred_element_type=jnp.float32)


def back_project(left, right):
    return jnp.einsum("te,de->td", left, right, preferred_element_type=jnp.float32)


def bits_of(size):
    return size.bit_length() - 1


def stage_orders(clips, blks):
    clip_bits = [("clip", k) for k in range(bits_of(clips))]
    blk_bits = [("blk", k) for k in range(bits_of(blks))]
    return (blk_bits[:1] + clip_bits + blk_bits[1:], blk_bits[:1] + clip_bits[::-1] + blk_bits[1:])


def post_of(order, stage, clips, blks):
    left = [("clip", k) for k in range(bits_of(clips))][::-1] + [("blk", k) for k in range(bits_of(blks))][::-1]
    for done in order[:stage]:
        left.remove(done)
    return 1 << (len(left) - 1 - left.index(order[stage]))


class Scatter:
    def __init__(self, order, clips, blks, source, window, own, recvs, send_sems, recv_sems, own_sem):
        self.order, self.clips, self.blks = order, clips, blks
        self.source, self.window, self.own, self.recvs = source, window, own, recvs
        self.send_sems, self.recv_sems, self.own_sem = send_sems, recv_sems, own_sem

    def parts(self, stage):
        axis, bit = self.order[stage]
        me = lax.axis_index(axis)
        mine = (me // (1 << bit)) % 2
        partner = me + (1 << bit) * (1 - 2 * mine)
        post = post_of(self.order, stage, self.clips, self.blks)
        ref = self.source if stage == 0 else self.recvs[stage - 1]
        return {axis: partner}, mine, post, ref

    def half(self, stage, which, post, ref):
        count, rows, width = ref.shape
        window = self.window if stage == 0 else slice(None)
        return ref.reshape(count // (2 * post), 2, post, rows, width).at[:, which, :, :, window]

    def copy(self, stage):
        partner, mine, post, ref = self.parts(stage)
        out = self.half(stage, 1 - mine, post, ref)
        into = self.recvs[stage]
        into = into.reshape(into.shape[0] // post, post, *into.shape[1:])
        return pltpu.make_async_remote_copy(
            src_ref=out,
            dst_ref=into,
            send_sem=self.send_sems.at[stage],
            recv_sem=self.recv_sems.at[stage],
            device_id=partner,
            device_id_type=MESH,
        )

    def load(self):
        _, mine, post, ref = self.parts(0)
        kept = self.half(0, mine, post, ref)
        into = self.own.reshape(self.own.shape[0] // post, post, *self.own.shape[1:])
        return pltpu.make_async_copy(kept, into, self.own_sem)

    def add(self, stage):
        _, mine, post, ref = self.parts(stage)
        into = self.recvs[stage]
        count = into.shape[0]

        def one(i, carry):
            at = i if stage == 0 else ((i // post) * 2 + mine) * post + i % post
            base = self.own if stage == 0 else ref
            into[i] = into[i] + base[at]
            return carry

        lax.fori_loop(0, count, one, 0)

    def last(self, out):
        stage = len(self.order) - 1
        _, mine, _, ref = self.parts(stage)
        out[...] = self.recvs[stage][0].astype(jnp.float32) + ref[mine].astype(jnp.float32)


def scatter_kernel(clips, blks, kinds, *refs):
    orders = stage_orders(clips, blks)
    stages = len(orders[0])
    count = len(kinds)
    n_kind = max(k for k, _, _ in kinds) + 1
    arrays = refs[: len(set((k, a) for k, a, _ in kinds))]
    refs = refs[len(arrays) :]
    vec, refs = refs[0], refs[1:]
    outs, refs = refs[: len(arrays)], refs[len(arrays) :]
    vec_out, refs = refs[0], refs[1:]
    owns, refs = refs[:n_kind], refs[n_kind:]
    recvs, refs = refs[: n_kind * stages], refs[n_kind * stages :]
    vec_in, send_sems, recv_sems, own_sems, vec_send, vec_recv = refs

    barrier = pltpu.get_barrier_semaphore()
    for axis, bit in orders[0]:
        me = lax.axis_index(axis)
        partner = me + (1 << bit) * (1 - 2 * ((me // (1 << bit)) % 2))
        pl.semaphore_signal(barrier, inc=1, device_id={axis: partner}, device_id_type=MESH)
    pl.semaphore_wait(barrier, stages)

    pieces, targets = [], []
    seen = [0] * n_kind
    slots = [owns[k].shape[0] for k in range(n_kind)]
    for p, (kind, array, part) in enumerate(kinds):
        width = recvs[kind * stages].shape[-1]
        window = pl.ds(part * width, width)
        slot = seen[kind]
        seen[kind] += 1
        pieces.append(
            Scatter(
                orders[p % 2], clips, blks,
                arrays[array], window,
                owns[kind].at[slot % slots[kind]],
                [recvs[kind * stages + s].at[slot] for s in range(stages)],
                send_sems.at[p], recv_sems.at[p], own_sems.at[p],
            )
        )
        targets.append(outs[array].at[:, window])

    def vec_copy(stage):
        axis, bit = orders[0][stage]
        me = lax.axis_index(axis)
        partner = me + (1 << bit) * (1 - 2 * ((me // (1 << bit)) % 2))
        return pltpu.make_async_remote_copy(
            src_ref=vec_in.at[0, stage],
            dst_ref=vec_in.at[1, stage],
            send_sem=vec_send.at[stage],
            recv_sem=vec_recv.at[stage],
            device_id={axis: partner},
            device_id_type=MESH,
        )

    vec_in[0, 0] = vec[...]
    vec_copy(0).start()
    for piece in pieces:
        piece.copy(0).start()
    held = {}
    for p, (kind, _, _) in enumerate(kinds):
        ahead = [q for q in range(count) if kinds[q][0] == kind]
        held[p] = ahead
    started = set()

    def load_ahead(kind, upto):
        queue = [q for q in range(count) if kinds[q][0] == kind]
        for q in queue[:upto]:
            if q not in started:
                started.add(q)
                pieces[q].load().start()

    for kind in range(n_kind):
        load_ahead(kind, slots[kind])
    done = [0] * n_kind
    for stage in range(stages):
        for p, piece in enumerate(pieces):
            piece.copy(stage).wait()
            if stage == 0:
                piece.load().wait()
            if stage == stages - 1:
                piece.last(targets[p])
                continue
            piece.add(stage)
            piece.copy(stage + 1).start()
            if stage == 0:
                kind = kinds[p][0]
                done[kind] += 1
                load_ahead(kind, slots[kind] + done[kind])
        vec_copy(stage).wait()
        summed = vec_in[0, stage] + vec_in[1, stage]
        if stage == stages - 1:
            vec_out[...] = summed
        else:
            vec_in[0, stage + 1] = summed
            vec_copy(stage + 1).start()


def reduce_scatter(arrays, kinds, vec, clips, blks):
    orders = stage_orders(clips, blks)
    stages = len(orders[0])
    devices = clips * blks
    count = len(kinds)
    n_kind = max(k for k, _, _ in kinds) + 1
    shapes, totals = [None] * n_kind, [0] * n_kind
    parts_of = {}
    for kind, array, part in kinds:
        totals[kind] += 1
        parts_of[array] = max(parts_of.get(array, 0), part + 1)
    for kind, array, _ in kinds:
        shapes[kind] = (arrays[array].shape[1], arrays[array].shape[2] // parts_of[array])
    any_spec = pl.BlockSpec(memory_space=pltpu.MemorySpace.HBM)
    vmem = pl.BlockSpec(memory_space=pltpu.VMEM)
    scratch = [pltpu.VMEM((min(3, totals[k]), devices // 2, *shapes[k]), jnp.bfloat16) for k in range(n_kind)]
    for k in range(n_kind):
        for s in range(stages):
            scratch.append(pltpu.VMEM((totals[k], devices >> (s + 1), *shapes[k]), jnp.bfloat16))
    dma = pltpu.SemaphoreType.DMA
    scratch += [
        pltpu.VMEM((2, stages, *vec.shape), jnp.float32),
        dma((count, stages)), dma((count, stages)), dma((count,)), dma((stages,)), dma((stages,)),
    ]
    return pl.pallas_call(
        partial(scatter_kernel, clips, blks, kinds),
        out_shape=[jax.ShapeDtypeStruct(a.shape[1:], jnp.float32) for a in arrays] + [jax.ShapeDtypeStruct(vec.shape, jnp.float32)],
        in_specs=[any_spec] * len(arrays) + [vmem],
        out_specs=[vmem] * (len(arrays) + 1),
        scratch_shapes=scratch,
        compiler_params=pltpu.CompilerParams(collective_id=0, has_side_effects=True, vmem_limit_bytes=56 << 20),
    )(*arrays, vec)


def body(
    frames,
    text_states,
    prompt_lengths,
    cotangent,
    self_query,
    self_key,
    self_value,
    self_out,
    cross_query,
    cross_key,
    cross_value,
    cross_out,
    hidden_in,
    hidden_out,
    first_gain,
    first_shift,
    second_gain,
    second_shift,
    third_gain,
    third_shift,
):
    block_total = lax.axis_size("blk")
    block_rank = lax.axis_index("blk")
    local_frames = frames[0].astype(jnp.float32)
    row_count = local_frames.shape[0]
    normed_one, norm_back_one = jax.vjp(layer_norm, local_frames, first_gain, first_shift)
    act_one = normed_one.astype(jnp.bfloat16)
    queries = project(act_one, self_query).astype(jnp.bfloat16)
    keys_local = project(act_one, self_key).astype(jnp.bfloat16)
    values_local = project(act_one, self_value).astype(jnp.bfloat16)
    query_heads = queries.reshape(row_count, HEADS, HEAD)
    query_index = block_rank * row_count + jnp.arange(row_count, dtype=jnp.int32)
    query_limit = (block_rank + 1) * row_count
    start_state = (
        jnp.full((HEADS, row_count), -1e30, jnp.float32),
        jnp.zeros((HEADS, row_count), jnp.float32),
        jnp.zeros((HEADS, row_count, HEAD), jnp.float32),
    )
    piece_keys = lax.all_gather(keys_local, "blk", axis=0, tiled=True)
    piece_values = lax.all_gather(values_local, "blk", axis=0, tiled=True)
    step_rows = math.gcd(row_count, piece_keys.shape[0])

    def one_step(step_index, running):
        first_key = step_index * step_rows

        def attend(running_in):
            run_peak, run_total, weighted = running_in
            key_block = lax.dynamic_slice_in_dim(piece_keys, step_index * step_rows, step_rows, 0)
            value_block = lax.dynamic_slice_in_dim(
                piece_values, step_index * step_rows, step_rows, 0
            )
            key_block = key_block.reshape(step_rows, HEADS, HEAD)
            value_block = value_block.reshape(step_rows, HEADS, HEAD)
            scores = (
                jnp.einsum(
                    "qhd,khd->hqk", query_heads, key_block, preferred_element_type=jnp.float32
                )
                * 0.125
            )
            key_index = first_key + jnp.arange(step_rows, dtype=jnp.int32)
            allowed = (key_index[None, :] <= query_index[:, None])[None]
            scores = jnp.where(allowed, scores, -1e30)
            new_peak = jnp.maximum(run_peak, jnp.max(scores, axis=-1))
            weights = jnp.where(allowed, jnp.exp(scores - new_peak[..., None]), 0.0)
            rescale = jnp.exp(run_peak - new_peak)
            run_total = run_total * rescale + jnp.sum(weights, axis=-1)
            weighted = weighted * rescale[..., None] + jnp.einsum(
                "hqk,khd->hqd",
                weights.astype(jnp.bfloat16),
                value_block,
                preferred_element_type=jnp.float32,
            )
            return (new_peak, run_total, weighted)

        return lax.cond(first_key < query_limit, attend, lambda running_in: running_in, running)

    run_peak, run_total, weighted = lax.fori_loop(
        0, piece_keys.shape[0] // step_rows, one_step, start_state
    )
    attended = (weighted / run_total[..., None]).transpose(1, 0, 2).reshape(row_count, D)
    log_sum = run_peak + jnp.log(run_total)
    att_low = attended.astype(jnp.bfloat16)
    after_self = local_frames + project(att_low, self_out)
    normed_two, norm_back_two = jax.vjp(layer_norm, after_self, second_gain, second_shift)
    act_two = normed_two.astype(jnp.bfloat16)
    local_text = text_states[0]
    cross_queries = (
        project(act_two, cross_query).astype(jnp.bfloat16).reshape(row_count, HEADS, HEAD)
    )
    text_keys = project(local_text, cross_key).astype(jnp.bfloat16).reshape(TEXT, HEADS, HEAD)
    text_values = project(local_text, cross_value).astype(jnp.bfloat16).reshape(TEXT, HEADS, HEAD)
    visible = (jnp.arange(TEXT, dtype=jnp.int32) < prompt_lengths[0])[None, None, :]
    cross_scores = (
        jnp.einsum("qhd,khd->hqk", cross_queries, text_keys, preferred_element_type=jnp.float32)
        * 0.125
    )
    cross_scores = jnp.where(visible, cross_scores, -1e30)
    cross_exp = jnp.exp(cross_scores - jnp.max(cross_scores, axis=-1, keepdims=True))
    cross_prob = cross_exp / jnp.sum(cross_exp, axis=-1, keepdims=True)
    cross_low = cross_prob.astype(jnp.bfloat16)
    cross_mixed = (
        jnp.einsum("hqk,khd->qhd", cross_low, text_values, preferred_element_type=jnp.float32)
        .reshape(row_count, D)
        .astype(jnp.bfloat16)
    )
    after_cross = after_self + project(cross_mixed, cross_out)
    normed_three, norm_back_three = jax.vjp(layer_norm, after_cross, third_gain, third_shift)
    act_three = normed_three.astype(jnp.bfloat16)
    pre_act = project(act_three, hidden_in)
    hidden, gelu_back = jax.vjp(partial(jax.nn.gelu, approximate=False), pre_act)
    hidden_low = hidden.astype(jnp.bfloat16)
    output_frames = (after_cross + project(hidden_low, hidden_out)).astype(jnp.bfloat16)[None]
    grad_out = cotangent[0]
    hidden_out_term = weight_term(hidden_low, grad_out)
    (pre_grad,) = gelu_back(back_project(grad_out, hidden_out))
    pre_low = pre_grad.astype(jnp.bfloat16)
    hidden_in_term = weight_term(act_three, pre_low)
    grad_norm_three, third_gain_term, third_shift_term = norm_back_three(
        back_project(pre_low, hidden_in)
    )
    grad_two = grad_out.astype(jnp.float32) + grad_norm_three
    grad_two_low = grad_two.astype(jnp.bfloat16)
    cross_out_term = weight_term(cross_mixed, grad_two_low)
    mixed_grad = (
        back_project(grad_two_low, cross_out).astype(jnp.bfloat16).reshape(row_count, HEADS, HEAD)
    )
    cross_dprob = jnp.einsum(
        "qhd,khd->hqk", mixed_grad, text_values, preferred_element_type=jnp.float32
    )
    cross_dscore = cross_prob * (
        cross_dprob - jnp.sum(cross_prob * cross_dprob, axis=-1, keepdims=True)
    )
    cross_dscore = cross_dscore.astype(jnp.bfloat16)
    cq_grad = (
        (
            jnp.einsum("hqk,khd->qhd", cross_dscore, text_keys, preferred_element_type=jnp.float32)
            * 0.125
        )
        .reshape(row_count, D)
        .astype(jnp.bfloat16)
    )
    key_part = (
        jnp.einsum(
            "hqk,qhd->khd", cross_dscore, cross_queries, preferred_element_type=jnp.float32
        ).reshape(TEXT, D)
        * 0.125
    )
    value_part = jnp.einsum(
        "hqk,qhd->khd", cross_low, mixed_grad, preferred_element_type=jnp.float32
    ).reshape(TEXT, D)
    key_summed, value_summed = (
        lax.psum_scatter(
            key_part.astype(jnp.bfloat16), "blk", scatter_dimension=0, tiled=True
        ).astype(jnp.float32),
        lax.psum_scatter(
            value_part.astype(jnp.bfloat16), "blk", scatter_dimension=0, tiled=True
        ).astype(jnp.float32),
    )
    text_rows = key_summed.shape[0]
    key_summed_low = key_summed.astype(jnp.bfloat16)
    value_summed_low = value_summed.astype(jnp.bfloat16)
    own_text = lax.dynamic_slice_in_dim(local_text, block_rank * text_rows, text_rows, 0)
    cross_key_term = weight_term(own_text, key_summed_low)
    cross_value_term = weight_term(own_text, value_summed_low)
    text_grad = (
        back_project(key_summed_low, cross_key) + back_project(value_summed_low, cross_value)
    )[None]
    cross_query_term = weight_term(act_two, cq_grad)
    grad_norm_two, second_gain_term, second_shift_term = norm_back_two(
        back_project(cq_grad, cross_query)
    )
    grad_one = grad_two + grad_norm_two
    grad_one_low = grad_one.astype(jnp.bfloat16)
    self_out_term = weight_term(att_low, grad_one_low)
    att_grad = back_project(grad_one_low, self_out).astype(jnp.bfloat16)
    grad_heads = att_grad.reshape(row_count, HEADS, HEAD)
    delta_rows = jnp.sum(
        (att_grad.astype(jnp.float32) * attended).reshape(row_count, HEADS, HEAD), axis=-1
    ).T

    def block_terms(held_keys, held_values, source_block):
        key_block = held_keys.reshape(row_count, HEADS, HEAD)
        value_block = held_values.reshape(row_count, HEADS, HEAD)
        key_index = source_block * row_count + jnp.arange(row_count, dtype=jnp.int32)
        allowed = (key_index[None, :] <= query_index[:, None])[None]
        scores = (
            jnp.einsum("qhd,khd->hqk", query_heads, key_block, preferred_element_type=jnp.float32)
            * 0.125
        )
        scores = jnp.where(allowed, scores, -1e30)
        probs = jnp.where(allowed, jnp.exp(scores - log_sum[..., None]), 0.0)
        dprobs = jnp.einsum(
            "qhd,khd->hqk", grad_heads, value_block, preferred_element_type=jnp.float32
        )
        dscores = (probs * (dprobs - delta_rows[..., None])).astype(jnp.bfloat16)
        query_term = (
            jnp.einsum("hqk,khd->hqd", dscores, key_block, preferred_element_type=jnp.float32)
            * 0.125
        )
        key_term = (
            jnp.einsum(
                "hqk,qhd->khd", dscores, query_heads, preferred_element_type=jnp.float32
            ).reshape(row_count, D)
            * 0.125
        )
        value_term = jnp.einsum(
            "hqk,qhd->khd",
            probs.astype(jnp.bfloat16),
            grad_heads,
            preferred_element_type=jnp.float32,
        ).reshape(row_count, D)
        return (key_term, value_term, query_term)

    def block_grads(held_state, source_block):

        def compute(state_in):
            held_keys, held_values, key_grads, value_grads, query_grads = state_in
            key_term, value_term, query_term = block_terms(held_keys, held_values, source_block)
            return (
                held_keys,
                held_values,
                key_grads + key_term,
                value_grads + value_term,
                query_grads + query_term,
            )

        return lax.cond(source_block <= block_rank, compute, lambda state_in: state_in, held_state)

    def pass_grads(held_state):
        held_keys, held_values, key_grads, value_grads, query_grads = held_state
        key_grads, value_grads = (
            shifted(key_grads.astype(jnp.bfloat16), "blk", 1).astype(key_grads.dtype),
            shifted(value_grads.astype(jnp.bfloat16), "blk", 1).astype(value_grads.dtype),
        )
        return (held_keys, held_values, key_grads, value_grads, query_grads)

    def block_turn(turn, held_state):
        held_state = block_grads(held_state, (block_rank - turn) % block_total)
        held_keys, held_values, key_grads, value_grads, query_grads = pass_grads(held_state)
        held_keys, held_values = shifted_2((held_keys, held_values), "blk", 1)
        return (held_keys, held_values, key_grads, value_grads, query_grads)

    held_state = (
        keys_local,
        values_local,
        jnp.zeros((row_count, D), jnp.float32),
        jnp.zeros((row_count, D), jnp.float32),
        jnp.zeros((HEADS, row_count, HEAD), jnp.float32),
    )
    held_state = lax.fori_loop(0, block_total - 1, block_turn, held_state)
    held_state = block_grads(held_state, (block_rank + 1) % block_total)
    held_state = pass_grads(held_state)
    key_grads, value_grads, query_grads = (held_state[2], held_state[3], held_state[4])
    query_low = query_grads.transpose(1, 0, 2).reshape(row_count, D).astype(jnp.bfloat16)
    key_low = key_grads.astype(jnp.bfloat16)
    value_low = value_grads.astype(jnp.bfloat16)
    self_query_term = weight_term(act_one, query_low)
    self_key_term = weight_term(act_one, key_low)
    self_value_term = weight_term(act_one, value_low)
    grad_act_one = (
        back_project(query_low, self_query)
        + back_project(key_low, self_key)
        + back_project(value_low, self_value)
    )
    grad_norm_one, first_gain_term, first_shift_term = norm_back_one(grad_act_one)
    frames_grad = (grad_one + grad_norm_one)[None]
    clip_total = lax.axis_size("clip")
    devices = clip_total * block_total
    matrices = [
        self_query_term, self_key_term, self_value_term, self_out_term, cross_query_term, cross_key_term, cross_value_term, cross_out_term,
        hidden_in_term, hidden_out_term,
    ]
    matrices = [m.astype(jnp.bfloat16).reshape(devices, m.shape[0] // devices, m.shape[1]) for m in matrices]
    kinds = [(1, 9, j) for j in range(4)] + [(0, 8, j) for j in range(4)] + [(0, j, 0) for j in range(8)]
    vectors = [first_gain_term, first_shift_term, second_gain_term, second_shift_term, third_gain_term, third_shift_term]
    stacked = jnp.stack(vectors + [jnp.zeros_like(first_gain_term)] * 2)
    *summed, vec_sum = reduce_scatter(matrices, kinds, stacked, clip_total, block_total)
    own = D // devices
    vec_own = lax.dynamic_slice_in_dim(vec_sum, (lax.axis_index("clip") * block_total + block_rank) * own, own, 1)
    summed = list(summed) + [vec_own[j] for j in range(6)]
    return (
        output_frames,
        frames_grad,
        text_grad,
        summed[0],
        summed[1],
        summed[2],
        summed[3],
        summed[4],
        summed[5],
        summed[6],
        summed[7],
        summed[8],
        summed[9],
        summed[10],
        summed[11],
        summed[12],
        summed[13],
        summed[14],
        summed[15],
    )


def solution(mesh):
    in_specs = (
        P("clip", "blk", None),
        P("clip", None, None),
        P("clip"),
        P("clip", "blk", None),
        P(),
        P(),
        P(),
        P(),
        P(),
        P(),
        P(),
        P(),
        P(),
        P(),
        P(),
        P(),
        P(),
        P(),
        P(),
        P(),
    )
    out_specs = (
        P("clip", "blk", None),
        P("clip", "blk", None),
        P("clip", "blk", None),
        P(("clip", "blk"), None),
        P(("clip", "blk"), None),
        P(("clip", "blk"), None),
        P(("clip", "blk"), None),
        P(("clip", "blk"), None),
        P(("clip", "blk"), None),
        P(("clip", "blk"), None),
        P(("clip", "blk"), None),
        P(("clip", "blk"), None),
        P(("clip", "blk"), None),
        P(("clip", "blk")),
        P(("clip", "blk")),
        P(("clip", "blk")),
        P(("clip", "blk")),
        P(("clip", "blk")),
        P(("clip", "blk")),
    )
    return jax.shard_map(body, mesh=mesh, in_specs=in_specs, out_specs=out_specs, check_vma=False)
```

```python
from functools import partial
import math

import jax
import jax.numpy as jnp
from jax import lax
from jax.experimental import pallas as pl
from jax.experimental.pallas import tpu as pltpu
from jax.sharding import PartitionSpec as P

D = 1024
HEADS = 16
HEAD = 64
TEXT = 256
MESH = pl.DeviceIdType.MESH


def bits_of(size):
    return size.bit_length() - 1


def stage_orders(clips, blks):
    clip_bits = [("clip", k) for k in range(bits_of(clips))]
    blk_bits = [("blk", k) for k in range(bits_of(blks))]
    return (blk_bits[:1] + clip_bits + blk_bits[1:], blk_bits[:1] + clip_bits[::-1] + blk_bits[1:])


def post_of(order, stage, clips, blks):
    left = [("clip", k) for k in range(bits_of(clips))][::-1] + [("blk", k) for k in range(bits_of(blks))][::-1]
    for done in order[:stage]:
        left.remove(done)
    return 1 << (len(left) - 1 - left.index(order[stage]))


class Scatter:
    def __init__(self, order, clips, blks, source, window, own, recvs, send_sems, recv_sems, own_sem):
        self.order, self.clips, self.blks = order, clips, blks
        self.source, self.window, self.own, self.recvs = source, window, own, recvs
        self.send_sems, self.recv_sems, self.own_sem = send_sems, recv_sems, own_sem

    def parts(self, stage):
        axis, bit = self.order[stage]
        me = lax.axis_index(axis)
        mine = (me // (1 << bit)) % 2
        partner = me + (1 << bit) * (1 - 2 * mine)
        post = post_of(self.order, stage, self.clips, self.blks)
        ref = self.source if stage == 0 else self.recvs[stage - 1]
        return {axis: partner}, mine, post, ref

    def half(self, stage, which, post, ref):
        count, rows, width = ref.shape
        window = self.window if stage == 0 else slice(None)
        return ref.reshape(count // (2 * post), 2, post, rows, width).at[:, which, :, :, window]

    def copy(self, stage):
        partner, mine, post, ref = self.parts(stage)
        out = self.half(stage, 1 - mine, post, ref)
        into = self.recvs[stage]
        into = into.reshape(into.shape[0] // post, post, *into.shape[1:])
        return pltpu.make_async_remote_copy(
            src_ref=out,
            dst_ref=into,
            send_sem=self.send_sems.at[stage],
            recv_sem=self.recv_sems.at[stage],
            device_id=partner,
            device_id_type=MESH,
        )

    def load(self):
        _, mine, post, ref = self.parts(0)
        kept = self.half(0, mine, post, ref)
        into = self.own.reshape(self.own.shape[0] // post, post, *self.own.shape[1:])
        return pltpu.make_async_copy(kept, into, self.own_sem)

    def add(self, stage):
        _, mine, post, ref = self.parts(stage)
        into = self.recvs[stage]
        count = into.shape[0]

        def one(i, carry):
            at = i if stage == 0 else ((i // post) * 2 + mine) * post + i % post
            base = self.own if stage == 0 else ref
            into[i] = into[i] + base[at]
            return carry

        lax.fori_loop(0, count, one, 0)

    def last(self, out):
        stage = len(self.order) - 1
        _, mine, _, ref = self.parts(stage)
        out[...] = self.recvs[stage][0].astype(jnp.float32) + ref[mine].astype(jnp.float32)


def scatter_kernel(clips, blks, kinds, *refs):
    orders = stage_orders(clips, blks)
    stages = len(orders[0])
    count = len(kinds)
    head_w, refs = refs[0], refs[1:]
    n_kind = max(k for k, _, _ in kinds) + 1
    arrays = refs[: len(set((k, a) for k, a, _ in kinds))]
    refs = refs[len(arrays) :]
    vec, refs = refs[0], refs[1:]
    outs, refs = refs[: len(arrays)], refs[len(arrays) :]
    (vec_out, head_out), refs = refs[:2], refs[2:]
    clip_stages = bits_of(clips)
    head_own, refs = refs[0], refs[1:]
    head_recvs, refs = refs[:clip_stages], refs[clip_stages:]
    (head_send, head_recv, head_sem, swap_send, swap_recv), refs = refs[:5], refs[5:]
    owns, refs = refs[:n_kind], refs[n_kind:]
    recvs, refs = refs[: n_kind * stages], refs[n_kind * stages :]
    vec_in, send_sems, recv_sems, own_sems, vec_send, vec_recv = refs

    for axis, bit in orders[0]:
        if axis == "clip":
            me = lax.axis_index(axis)
            partner = me + (1 << bit) * (1 - 2 * ((me // (1 << bit)) % 2))
            pl.semaphore_signal(pltpu.get_barrier_semaphore(), inc=1, device_id={axis: partner}, device_id_type=MESH)
    greet("blk", clip_stages)

    pieces, targets = [], []
    seen = [0] * n_kind
    slots = [owns[k].shape[0] for k in range(n_kind)]
    for p, (kind, array, part) in enumerate(kinds):
        width = recvs[kind * stages].shape[-1]
        window = pl.ds(part * width, width)
        slot = seen[kind]
        seen[kind] += 1
        pieces.append(
            Scatter(
                orders[p % 2], clips, blks,
                arrays[array], window,
                owns[kind].at[slot % slots[kind]],
                [recvs[kind * stages + s].at[slot] for s in range(stages)],
                send_sems.at[p], recv_sems.at[p], own_sems.at[p],
            )
        )
        targets.append(outs[array].at[:, window])

    def vec_copy(stage):
        axis, bit = orders[0][stage]
        me = lax.axis_index(axis)
        partner = me + (1 << bit) * (1 - 2 * ((me // (1 << bit)) % 2))
        return pltpu.make_async_remote_copy(
            src_ref=vec_in.at[0, stage],
            dst_ref=vec_in.at[1, stage],
            send_sem=vec_send.at[stage],
            recv_sem=vec_recv.at[stage],
            device_id={axis: partner},
            device_id_type=MESH,
        )

    everything = slice(None)
    heads = Scatter(
        [("clip", k) for k in range(clip_stages)], clips, blks, head_w, everything, head_own, list(head_recvs),
        head_send, head_recv, head_sem,
    )
    rank = lax.axis_index("blk")

    def swap(peer, source):
        return pltpu.make_async_remote_copy(
            src_ref=head_recvs[-1].at[peer], dst_ref=head_out.at[source], send_sem=swap_send.at[peer],
            recv_sem=swap_recv.at[source], device_id={"blk": peer}, device_id_type=MESH,
        )

    vec_in[0, 0] = vec[...]
    vec_copy(0).start()
    heads.copy(0).start()
    heads.load().start()
    for piece in pieces:
        piece.copy(0).start()
    held = {}
    for p, (kind, _, _) in enumerate(kinds):
        ahead = [q for q in range(count) if kinds[q][0] == kind]
        held[p] = ahead
    started = set()

    def load_ahead(kind, upto):
        queue = [q for q in range(count) if kinds[q][0] == kind]
        for q in queue[:upto]:
            if q not in started:
                started.add(q)
                pieces[q].load().start()

    for kind in range(n_kind):
        load_ahead(kind, slots[kind])
    done = [0] * n_kind
    for stage in range(stages):
        for p, piece in enumerate(pieces):
            piece.copy(stage).wait()
            if stage == 0:
                piece.load().wait()
            if stage == stages - 1:
                piece.last(targets[p])
                continue
            piece.add(stage)
            piece.copy(stage + 1).start()
            if stage == 0:
                kind = kinds[p][0]
                done[kind] += 1
                load_ahead(kind, slots[kind] + done[kind])
        if stage < clip_stages:
            heads.copy(stage).wait()
            if stage == 0:
                heads.load().wait()
            heads.add(stage)
            if stage + 1 < clip_stages:
                heads.copy(stage + 1).start()
            else:
                head_out[rank] = head_recvs[-1][rank]
                for step in range(1, blks):
                    swap((rank + step) % blks, rank).start()
        vec_copy(stage).wait()
        summed = vec_in[0, stage] + vec_in[1, stage]
        if stage == stages - 1:
            vec_out[...] = summed
        else:
            vec_in[0, stage + 1] = summed
            vec_copy(stage + 1).start()
    for step in range(1, blks):
        peer = (rank + step) % blks
        swap(peer, rank).wait_send()
        swap(peer, peer).wait_recv()


def reduce_scatter(head_w, arrays, kinds, vec, clips, blks):
    orders = stage_orders(clips, blks)
    stages = len(orders[0])
    devices = clips * blks
    count = len(kinds)
    n_kind = max(k for k, _, _ in kinds) + 1
    shapes, totals = [None] * n_kind, [0] * n_kind
    parts_of = {}
    for kind, array, part in kinds:
        totals[kind] += 1
        parts_of[array] = max(parts_of.get(array, 0), part + 1)
    for kind, array, _ in kinds:
        shapes[kind] = (arrays[array].shape[1], arrays[array].shape[2] // parts_of[array])
    any_spec = pl.BlockSpec(memory_space=pltpu.MemorySpace.HBM)
    vmem = pl.BlockSpec(memory_space=pltpu.VMEM)
    clip_stages = bits_of(clips)
    dma = pltpu.SemaphoreType.DMA
    head_shape = head_w.shape[1:]
    scratch = [pltpu.VMEM((devices // 2, *head_shape), jnp.bfloat16)]
    scratch += [pltpu.VMEM((devices >> (s + 1), *head_shape), jnp.bfloat16) for s in range(clip_stages)]
    scratch += [dma((clip_stages,)), dma((clip_stages,)), dma, dma((blks,)), dma((blks,))]
    scratch += [pltpu.VMEM((min(3, totals[k]), devices // 2, *shapes[k]), jnp.bfloat16) for k in range(n_kind)]
    for k in range(n_kind):
        for s in range(stages):
            scratch.append(pltpu.VMEM((totals[k], devices >> (s + 1), *shapes[k]), jnp.bfloat16))
    scratch += [
        pltpu.VMEM((2, stages, *vec.shape), jnp.float32),
        dma((count, stages)), dma((count, stages)), dma((count,)), dma((stages,)), dma((stages,)),
    ]
    return pl.pallas_call(
        partial(scatter_kernel, clips, blks, kinds),
        out_shape=[jax.ShapeDtypeStruct(a.shape[1:], jnp.float32) for a in arrays]
        + [jax.ShapeDtypeStruct(vec.shape, jnp.float32), jax.ShapeDtypeStruct((blks, *head_shape), jnp.bfloat16)],
        in_specs=[any_spec] * (1 + len(arrays)) + [vmem],
        out_specs=[vmem] * (len(arrays) + 2),
        scratch_shapes=scratch,
        compiler_params=pltpu.CompilerParams(collective_id=0, has_side_effects=True, vmem_limit_bytes=56 << 20),
    )(head_w, *arrays, vec)


def normed(block, gain, shift):
    values = block.astype(jnp.float32)
    centred = values - jnp.mean(values, axis=-1, keepdims=True)
    variance = jnp.mean(centred * centred, axis=-1, keepdims=True)
    return centred * lax.rsqrt(variance + 1e-05) * gain + shift


def matmul(left, right, over=(1, 0)):
    return lax.dot_general(left, right, (((over[0],), (over[1],)), ((), ())), preferred_element_type=jnp.float32)


def greet(axis, others):
    me, size = lax.axis_index(axis), lax.axis_size(axis)
    barrier = pltpu.get_barrier_semaphore()
    for step in range(1, size):
        pl.semaphore_signal(barrier, inc=1, device_id={axis: (me + step) % size}, device_id_type=MESH)
    pl.semaphore_wait(barrier, size - 1 + others)


def head_only(block, head):
    lanes = block.shape[-1]
    if lanes == HEAD:
        return block
    lane = lax.broadcasted_iota(jnp.int32, block.shape, 1)
    return jnp.where((lane // HEAD) == head, block, jnp.zeros_like(block))


def causal(rows, transposed):
    row = lax.broadcasted_iota(jnp.int32, (rows, rows), 0)
    column = lax.broadcasted_iota(jnp.int32, (rows, rows), 1)
    return (row <= column) if transposed else (column <= row)


def forward_kernel(
    frames, weight, gain, shift, att_out, act_out, qkv_out, full_out, lse_out, gathered, low, ring_send, ring_recv, core_send, core_recv, out_send, out_recv
):
    blks = lax.axis_size("blk")
    chips = blks // 2
    me = lax.axis_index("blk")
    chip, core = me // 2, me % 2
    rows, width = low.shape[1:]
    heads = width // HEAD

    greet("blk", 0)
    gathered[me] = frames[...]

    def ring(slot, way):
        return pltpu.make_async_remote_copy(
            src_ref=gathered.at[slot], dst_ref=gathered.at[slot], send_sem=ring_send.at[0 if way > 0 else 1, slot],
            recv_sem=ring_recv.at[slot], device_id={"blk": me + 2 * way}, device_id_type=MESH,
        )

    def across(slot):
        return pltpu.make_async_remote_copy(
            src_ref=gathered.at[slot], dst_ref=gathered.at[slot], send_sem=core_send.at[slot],
            recv_sem=core_recv.at[slot], device_id={"blk": chip * 2 + 1 - core}, device_id_type=MESH,
        )

    def project_block(slot):
        act = normed(gathered[slot], gain[...], shift[...]).astype(jnp.bfloat16)
        act_out[slot] = act
        made = matmul(act, weight[...]).astype(jnp.bfloat16)
        qkv_out[slot, :, :width] = made[:, :width] * jnp.bfloat16(0.125)
        qkv_out[slot, :, width:] = made[:, width:]

    @pl.when(chip + 1 < chips)
    def _():
        ring(me, 1).start()

    @pl.when(chip > 0)
    def _():
        ring(me, -1).start()

    across(me).start()
    project_block(me)
    other = chip * 2 + 1 - core
    across(other).wait_recv()
    project_block(other)

    for step in range(1, chips):
        for way in (1, -1):
            source = chip - way * step

            @pl.when((source >= 0) & (source < chips))
            def _():
                slot = source * 2 + core
                ring(slot, way).wait_recv()

                @pl.when((chip + way >= 0) & (chip + way < chips))
                def _():
                    ring(slot, way).start()

                across(slot).start()

        for way in (1, -1):
            source = chip - way * step

            @pl.when((source >= 0) & (source < chips))
            def _():
                project_block(source * 2 + core)
                across(source * 2 + 1 - core).wait_recv()
                project_block(source * 2 + 1 - core)

    mask = causal(rows, False)

    def send(block):
        return pltpu.make_async_remote_copy(
            src_ref=low.at[block], dst_ref=att_out.at[me], send_sem=out_send.at[block],
            recv_sem=out_recv.at[me], device_id={"blk": block}, device_id_type=MESH,
        )

    def query_block(i, carry):
        queries = qkv_out[i, :, :width]
        split = [head_only(queries, h) for h in range(heads)]

        def update(j, state, masked):
            keys = qkv_out[j, :, width : 2 * width]
            values = qkv_out[j, :, 2 * width :]
            new = []
            for h in range(heads):
                peak, total, acc = state[3 * h : 3 * h + 3]
                scores = matmul(split[h], keys, (1, 1))
                if masked:
                    scores = jnp.where(mask, scores, -1e30)
                top = jnp.maximum(peak, jnp.max(scores, axis=-1, keepdims=True))
                weights = jnp.exp(scores - top)
                rescale = jnp.exp(peak - top)
                total = total * rescale + jnp.sum(weights, axis=-1, keepdims=True)
                acc = acc * rescale + matmul(weights.astype(jnp.bfloat16), values)
                new += [top, total, acc]
            return tuple(new)

        start = []
        for _ in range(heads):
            start += [jnp.full((rows, 1), -1e30, jnp.float32), jnp.zeros((rows, 1), jnp.float32), jnp.zeros((rows, width), jnp.float32)]
        state = update(i, tuple(start), True)
        state = lax.fori_loop(0, i, lambda j, held: update(j, held, False), state)
        lane = lax.broadcasted_iota(jnp.int32, (rows, width), 1) // HEAD
        full = state[2] / state[1]
        stat = jnp.broadcast_to(state[0] + jnp.log(state[1]), (rows, width))
        for h in range(1, heads):
            full = jnp.where(lane == h, state[3 * h + 2] / state[3 * h + 1], full)
            stat = jnp.where(lane == h, state[3 * h] + jnp.log(state[3 * h + 1]), stat)
        full_out[i] = full
        lse_out[i] = stat
        low[i] = full.astype(jnp.bfloat16)

        @pl.when(i != me)
        def _():
            send(i).start()

        return carry

    lax.fori_loop(0, blks, query_block, 0)
    att_out[me] = low[me]

    def finish(i, carry):
        @pl.when(i != me)
        def _():
            send(i).wait_send()
            pltpu.make_async_remote_copy(
                src_ref=low.at[i], dst_ref=att_out.at[i], send_sem=out_send.at[i],
                recv_sem=out_recv.at[i], device_id={"blk": i}, device_id_type=MESH,
            ).wait_recv()

        return carry

    lax.fori_loop(0, blks, finish, 0)

    @pl.when(chip + 1 < chips)
    def _():
        ring(me, 1).wait_send()

    @pl.when(chip > 0)
    def _():
        ring(me, -1).wait_send()

    across(me).wait_send()
    for step in range(1, chips):
        for way in (1, -1):
            source = chip - way * step

            @pl.when((source >= 0) & (source < chips))
            def _():
                slot = source * 2 + core

                @pl.when((chip + way >= 0) & (chip + way < chips))
                def _():
                    ring(slot, way).wait_send()

                across(slot).wait_send()


def attention_forward(frames, weight, gain, shift, blks):
    rows, depth = frames.shape
    width = weight.shape[1] // 3
    vmem = pl.BlockSpec(memory_space=pltpu.VMEM)
    dma = pltpu.SemaphoreType.DMA
    return pl.pallas_call(
        forward_kernel,
        out_shape=[
            jax.ShapeDtypeStruct((blks, rows, width), jnp.bfloat16),
            jax.ShapeDtypeStruct((blks, rows, depth), jnp.bfloat16),
            jax.ShapeDtypeStruct((blks, rows, 3 * width), jnp.bfloat16),
            jax.ShapeDtypeStruct((blks, rows, width), jnp.float32),
            jax.ShapeDtypeStruct((blks, rows, width), jnp.float32),
        ],
        in_specs=[vmem] * 4,
        out_specs=[vmem] * 5,
        scratch_shapes=[
            pltpu.VMEM((blks, rows, depth), jnp.bfloat16), pltpu.VMEM((blks, rows, width), jnp.bfloat16),
            dma((2, blks)), dma((blks,)), dma((blks,)), dma((blks,)), dma((blks,)), dma((blks,)),
        ],
        compiler_params=pltpu.CompilerParams(collective_id=1, has_side_effects=True, vmem_limit_bytes=48 << 20),
    )(frames, weight, gain, shift)


def backward_kernel(
    grads, qkv, full, lse, act, mine_out, weight_low, weight_out, grad_all, lse_rows, delta_rows, sums, query_sum, in_send, in_recv, out_send, out_recv
):
    blks = lax.axis_size("blk")
    me = lax.axis_index("blk")
    rows, width = full.shape[1:]
    heads = width // HEAD
    greet("blk", 0)

    def fetch(peer, source):
        return pltpu.make_async_remote_copy(
            src_ref=grads.at[peer], dst_ref=grad_all.at[source], send_sem=in_send.at[peer],
            recv_sem=in_recv.at[source], device_id={"blk": peer}, device_id_type=MESH,
        )

    def give(block, source):
        return pltpu.make_async_remote_copy(
            src_ref=sums.at[block], dst_ref=mine_out.at[source], send_sem=out_send.at[block],
            recv_sem=out_recv.at[source], device_id={"blk": block}, device_id_type=MESH,
        )

    for step in range(1, blks):
        fetch((me + step) % blks, me).start()
    grad_all[me] = grads[me]
    for i in range(blks):
        stat = lse[i].T
        for h in range(heads):
            lse_rows[i, h : h + 1, :] = stat[h * HEAD : h * HEAD + 1, :]
        query_sum[i] = jnp.zeros_like(query_sum[i])
    for step in range(1, blks):
        fetch((me + step) % blks, (me + step) % blks).wait_recv()
    for i in range(blks):
        product = (grad_all[i].astype(jnp.float32) * full[i]).T
        for h in range(heads):
            delta_rows[i, h : h + 1, :] = jnp.sum(product[h * HEAD : (h + 1) * HEAD], axis=0, keepdims=True)

    mask = causal(rows, True)

    def key_block(j, carry):
        keys = qkv[j, :, width : 2 * width]
        values = qkv[j, :, 2 * width :]
        key_split = [head_only(keys, h) for h in range(heads)]

        def update(i, state, masked):
            key_sum, value_sum = state
            queries = qkv[i, :, :width]
            grad = grad_all[i]
            total = None
            for h in range(heads):
                query_h, grad_h = head_only(queries, h), head_only(grad, h)
                scores = matmul(keys, query_h, (1, 1))
                probs = jnp.exp(scores - lse_rows[i, h : h + 1, :])
                if masked:
                    probs = jnp.where(mask, probs, 0.0)
                dprobs = matmul(values, grad_h, (1, 1))
                dscores = (probs * (dprobs - delta_rows[i, h : h + 1, :])).astype(jnp.bfloat16)
                value_sum = value_sum + matmul(probs.astype(jnp.bfloat16), grad_h)
                key_sum = key_sum + matmul(dscores, query_h)
                term = matmul(dscores, key_split[h], (0, 0))
                total = term if total is None else total + term
            query_sum[i] = query_sum[i] + total
            return key_sum, value_sum

        zero = jnp.zeros((rows, width), jnp.float32)
        state = update(j, (zero, zero), True)
        key_sum, value_sum = lax.fori_loop(j + 1, blks, lambda i, held: update(i, held, False), state)
        sums[j, :, :width] = (query_sum[j] * 0.125).astype(jnp.bfloat16)
        sums[j, :, width : 2 * width] = key_sum.astype(jnp.bfloat16)
        sums[j, :, 2 * width :] = value_sum.astype(jnp.bfloat16)

        @pl.when(j != me)
        def _():
            give(j, me).start()

        return carry

    lax.fori_loop(0, blks, key_block, 0)
    mine_out[me] = sums[me]
    depth = act.shape[-1]

    def weight_block(j, carry):
        weight_out[...] += matmul(act[j], sums[j], (0, 0))
        return carry

    weight_out[...] = jnp.zeros_like(weight_out)
    lax.fori_loop(0, blks, weight_block, 0)
    weight_low[...] = weight_out[...].astype(jnp.bfloat16)
    for step in range(1, blks):
        peer = (me + step) % blks
        fetch(peer, me).wait_send()
        give(peer, me).wait_send()
        give(peer, peer).wait_recv()


def attention_backward(grads, qkv, full, lse, act):
    blks, rows, width = grads.shape
    depth = act.shape[-1]
    vmem = pl.BlockSpec(memory_space=pltpu.VMEM)
    dma = pltpu.SemaphoreType.DMA
    heads = width // HEAD
    return pl.pallas_call(
        backward_kernel,
        out_shape=[
            jax.ShapeDtypeStruct((blks, rows, 3 * width), jnp.bfloat16),
            jax.ShapeDtypeStruct((depth, 3 * width), jnp.bfloat16),
        ],
        in_specs=[vmem] * 5,
        out_specs=[vmem] * 2,
        scratch_shapes=[
            pltpu.VMEM((depth, 3 * width), jnp.float32),
            pltpu.VMEM((blks, rows, width), jnp.bfloat16),
            pltpu.VMEM((blks, max(8, heads), rows), jnp.float32), pltpu.VMEM((blks, max(8, heads), rows), jnp.float32),
            pltpu.VMEM((blks, rows, 3 * width), jnp.bfloat16), pltpu.VMEM((blks, rows, width), jnp.float32),
            dma((blks,)), dma((blks,)), dma((blks,)), dma((blks,)),
        ],
        compiler_params=pltpu.CompilerParams(collective_id=2, has_side_effects=True, vmem_limit_bytes=48 << 20),
    )(grads, qkv, full, lse, act)


def layer_norm(inputs, gain_vec, shift_vec):
    centred = inputs - jnp.mean(inputs, axis=-1, keepdims=True)
    variance = jnp.mean(centred * centred, axis=-1, keepdims=True)
    return centred * lax.rsqrt(variance + 1e-05) * gain_vec + shift_vec


def project(left, right):
    return jnp.dot(left, right, preferred_element_type=jnp.float32)


def weight_term(left, right):
    return jnp.einsum("td,te->de", left, right, preferred_element_type=jnp.float32)


def back_project(left, right):
    return jnp.einsum("te,de->td", left, right, preferred_element_type=jnp.float32)


def body(
    frames,
    text_states,
    prompt_lengths,
    cotangent,
    self_query,
    self_key,
    self_value,
    self_out,
    cross_query,
    cross_key,
    cross_value,
    cross_out,
    hidden_in,
    hidden_out,
    first_gain,
    first_shift,
    second_gain,
    second_shift,
    third_gain,
    third_shift,
):
    block_total = lax.axis_size("blk")
    block_rank = lax.axis_index("blk")
    local_frames = frames[0].astype(jnp.float32)
    row_count = local_frames.shape[0]
    _, norm_back_one = jax.vjp(layer_norm, local_frames, first_gain, first_shift)
    clip_total = lax.axis_size("clip")
    devices = clip_total * block_total
    head_width = D // block_total
    own_weight = jnp.concatenate(
        [
            lax.dynamic_slice_in_dim(matrix, block_rank * head_width, head_width, 1)
            for matrix in (self_query, self_key, self_value)
        ],
        axis=1,
    )
    att_parts, act_all, qkv, att_full, log_sums = attention_forward(
        frames[0], own_weight, first_gain[None], first_shift[None], block_total
    )
    att_low = att_parts.transpose(1, 0, 2).reshape(row_count, D)
    after_self = local_frames + project(att_low, self_out)
    normed_two, norm_back_two = jax.vjp(layer_norm, after_self, second_gain, second_shift)
    act_two = normed_two.astype(jnp.bfloat16)
    local_text = text_states[0]
    cross_queries = (
        project(act_two, cross_query).astype(jnp.bfloat16).reshape(row_count, HEADS, HEAD)
    )
    text_keys = project(local_text, cross_key).astype(jnp.bfloat16).reshape(TEXT, HEADS, HEAD)
    text_values = project(local_text, cross_value).astype(jnp.bfloat16).reshape(TEXT, HEADS, HEAD)
    visible = (jnp.arange(TEXT, dtype=jnp.int32) < prompt_lengths[0])[None, None, :]
    cross_scores = (
        jnp.einsum("qhd,khd->hqk", cross_queries, text_keys, preferred_element_type=jnp.float32)
        * 0.125
    )
    cross_scores = jnp.where(visible, cross_scores, -1e30)
    cross_exp = jnp.exp(cross_scores - jnp.max(cross_scores, axis=-1, keepdims=True))
    cross_prob = cross_exp / jnp.sum(cross_exp, axis=-1, keepdims=True)
    cross_low = cross_prob.astype(jnp.bfloat16)
    cross_mixed = (
        jnp.einsum("hqk,khd->qhd", cross_low, text_values, preferred_element_type=jnp.float32)
        .reshape(row_count, D)
        .astype(jnp.bfloat16)
    )
    after_cross = after_self + project(cross_mixed, cross_out)
    normed_three, norm_back_three = jax.vjp(layer_norm, after_cross, third_gain, third_shift)
    act_three = normed_three.astype(jnp.bfloat16)
    pre_act = project(act_three, hidden_in)
    hidden, gelu_back = jax.vjp(partial(jax.nn.gelu, approximate=False), pre_act)
    hidden_low = hidden.astype(jnp.bfloat16)
    output_frames = (after_cross + project(hidden_low, hidden_out)).astype(jnp.bfloat16)[None]
    grad_out = cotangent[0]
    hidden_out_term = weight_term(hidden_low, grad_out)
    (pre_grad,) = gelu_back(back_project(grad_out, hidden_out))
    pre_low = pre_grad.astype(jnp.bfloat16)
    hidden_in_term = weight_term(act_three, pre_low)
    grad_norm_three, third_gain_term, third_shift_term = norm_back_three(
        back_project(pre_low, hidden_in)
    )
    grad_two = grad_out.astype(jnp.float32) + grad_norm_three
    grad_two_low = grad_two.astype(jnp.bfloat16)
    cross_out_term = weight_term(cross_mixed, grad_two_low)
    mixed_grad = (
        back_project(grad_two_low, cross_out).astype(jnp.bfloat16).reshape(row_count, HEADS, HEAD)
    )
    cross_dprob = jnp.einsum(
        "qhd,khd->hqk", mixed_grad, text_values, preferred_element_type=jnp.float32
    )
    cross_dscore = cross_prob * (
        cross_dprob - jnp.sum(cross_prob * cross_dprob, axis=-1, keepdims=True)
    )
    cross_dscore = cross_dscore.astype(jnp.bfloat16)
    cq_grad = (
        (
            jnp.einsum("hqk,khd->qhd", cross_dscore, text_keys, preferred_element_type=jnp.float32)
            * 0.125
        )
        .reshape(row_count, D)
        .astype(jnp.bfloat16)
    )
    key_part = (
        jnp.einsum(
            "hqk,qhd->khd", cross_dscore, cross_queries, preferred_element_type=jnp.float32
        ).reshape(TEXT, D)
        * 0.125
    )
    value_part = jnp.einsum(
        "hqk,qhd->khd", cross_low, mixed_grad, preferred_element_type=jnp.float32
    ).reshape(TEXT, D)
    key_summed, value_summed = (
        lax.psum_scatter(
            key_part.astype(jnp.bfloat16), "blk", scatter_dimension=0, tiled=True
        ).astype(jnp.float32),
        lax.psum_scatter(
            value_part.astype(jnp.bfloat16), "blk", scatter_dimension=0, tiled=True
        ).astype(jnp.float32),
    )
    text_rows = key_summed.shape[0]
    key_summed_low = key_summed.astype(jnp.bfloat16)
    value_summed_low = value_summed.astype(jnp.bfloat16)
    own_text = lax.dynamic_slice_in_dim(local_text, block_rank * text_rows, text_rows, 0)
    cross_key_term = weight_term(own_text, key_summed_low)
    cross_value_term = weight_term(own_text, value_summed_low)
    text_grad = (
        back_project(key_summed_low, cross_key) + back_project(value_summed_low, cross_value)
    )[None]
    cross_query_term = weight_term(act_two, cq_grad)
    grad_norm_two, second_gain_term, second_shift_term = norm_back_two(
        back_project(cq_grad, cross_query)
    )
    grad_one = grad_two + grad_norm_two
    grad_one_low = grad_one.astype(jnp.bfloat16)
    self_out_term = weight_term(att_low, grad_one_low)
    att_grad = back_project(grad_one_low, self_out).astype(jnp.bfloat16)
    grad_parts = att_grad.reshape(row_count, block_total, head_width).transpose(1, 0, 2)
    own_grads, head_weight = attention_backward(grad_parts, qkv, att_full, log_sums, act_all)
    own_grads = own_grads.reshape(block_total, row_count, 3, head_width).transpose(2, 1, 0, 3)
    query_low, key_low, value_low = own_grads.reshape(3, row_count, D)
    grad_act_one = (
        back_project(query_low, self_query)
        + back_project(key_low, self_key)
        + back_project(value_low, self_value)
    )
    grad_norm_one, first_gain_term, first_shift_term = norm_back_one(grad_act_one)
    frames_grad = (grad_one + grad_norm_one)[None]
    matrices = [self_out_term, cross_query_term, cross_key_term, cross_value_term, cross_out_term, hidden_in_term, hidden_out_term]
    matrices = [m.astype(jnp.bfloat16).reshape(devices, m.shape[0] // devices, m.shape[1]) for m in matrices]
    kinds = [(1, 6, j) for j in range(4)] + [(0, 5, j) for j in range(4)] + [(0, j, 0) for j in range(5)]
    vectors = [first_gain_term, first_shift_term, second_gain_term, second_shift_term, third_gain_term, third_shift_term]
    stacked = jnp.stack(vectors + [jnp.zeros_like(first_gain_term)] * 2)
    own = D // devices
    *matrix_sums, vec_sum, head_sums = reduce_scatter(
        head_weight.reshape(devices, own, 3 * head_width), matrices, kinds, stacked, clip_total, block_total
    )
    vec_own = lax.dynamic_slice_in_dim(vec_sum, (lax.axis_index("clip") * block_total + block_rank) * own, own, 1)
    head_sums = head_sums.reshape(block_total, own, 3, head_width).transpose(2, 1, 0, 3).reshape(3, own, D).astype(jnp.float32)
    summed = [head_sums[j] for j in range(3)] + list(matrix_sums) + [vec_own[j] for j in range(6)]
    return (
        output_frames,
        frames_grad,
        text_grad,
        summed[0],
        summed[1],
        summed[2],
        summed[3],
        summed[4],
        summed[5],
        summed[6],
        summed[7],
        summed[8],
        summed[9],
        summed[10],
        summed[11],
        summed[12],
        summed[13],
        summed[14],
        summed[15],
    )


def solution(mesh):
    in_specs = (
        P("clip", "blk", None),
        P("clip", None, None),
        P("clip"),
        P("clip", "blk", None),
        P(),
        P(),
        P(),
        P(),
        P(),
        P(),
        P(),
        P(),
        P(),
        P(),
        P(),
        P(),
        P(),
        P(),
        P(),
        P(),
    )
    out_specs = (
        P("clip", "blk", None),
        P("clip", "blk", None),
        P("clip", "blk", None),
        P(("clip", "blk"), None),
        P(("clip", "blk"), None),
        P(("clip", "blk"), None),
        P(("clip", "blk"), None),
        P(("clip", "blk"), None),
        P(("clip", "blk"), None),
        P(("clip", "blk"), None),
        P(("clip", "blk"), None),
        P(("clip", "blk"), None),
        P(("clip", "blk"), None),
        P(("clip", "blk")),
        P(("clip", "blk")),
        P(("clip", "blk")),
        P(("clip", "blk")),
        P(("clip", "blk")),
        P(("clip", "blk")),
    )
    return jax.shard_map(body, mesh=mesh, in_specs=in_specs, out_specs=out_specs, check_vma=False)
```

```python
from functools import partial
import math
from types import SimpleNamespace

import jax
import jax.numpy as jnp
from jax import lax
from jax.experimental import pallas as pl
from jax.experimental.pallas import tpu as pltpu
from jax.sharding import PartitionSpec as P

D = 1024
HEADS = 16
HEAD = 64
TEXT = 256
MESH = pl.DeviceIdType.MESH


def normed(block, gain, shift):
    values = block.astype(jnp.float32)
    centred = values - jnp.mean(values, axis=-1, keepdims=True)
    variance = jnp.mean(centred * centred, axis=-1, keepdims=True)
    return centred * lax.rsqrt(variance + 1e-05) * gain + shift


def matmul(left, right, over=(1, 0)):
    return lax.dot_general(left, right, (((over[0],), (over[1],)), ((), ())), preferred_element_type=jnp.float32)


def greet(axis, others):
    me, size = lax.axis_index(axis), lax.axis_size(axis)
    barrier = pltpu.get_barrier_semaphore()
    for step in range(1, size):
        pl.semaphore_signal(barrier, inc=1, device_id={axis: (me + step) % size}, device_id_type=MESH)
    pl.semaphore_wait(barrier, size - 1 + others)


def head_only(block, head):
    lanes = block.shape[-1]
    if lanes == HEAD:
        return block
    lane = lax.broadcasted_iota(jnp.int32, block.shape, 1)
    return jnp.where((lane // HEAD) == head, block, jnp.zeros_like(block))


def causal(rows, transposed):
    row = lax.broadcasted_iota(jnp.int32, (rows, rows), 0)
    column = lax.broadcasted_iota(jnp.int32, (rows, rows), 1)
    return (row <= column) if transposed else (column <= row)


def forward_kernel(
    frames, weight, gain, shift, att_out, act_out, qkv_out, full_out, lse_out, gathered, low, ring_send, ring_recv, core_send, core_recv, out_send, out_recv
):
    blks = lax.axis_size("blk")
    chips = blks // 2
    me = lax.axis_index("blk")
    chip, core = me // 2, me % 2
    rows, width = low.shape[1:]
    heads = width // HEAD

    greet("blk", 0)
    gathered[me] = frames[...]

    def ring(slot, way):
        return pltpu.make_async_remote_copy(
            src_ref=gathered.at[slot], dst_ref=gathered.at[slot], send_sem=ring_send.at[0 if way > 0 else 1, slot],
            recv_sem=ring_recv.at[slot], device_id={"blk": me + 2 * way}, device_id_type=MESH,
        )

    def across(slot):
        return pltpu.make_async_remote_copy(
            src_ref=gathered.at[slot], dst_ref=gathered.at[slot], send_sem=core_send.at[slot],
            recv_sem=core_recv.at[slot], device_id={"blk": chip * 2 + 1 - core}, device_id_type=MESH,
        )

    def project_block(slot):
        act = normed(gathered[slot], gain[...], shift[...]).astype(jnp.bfloat16)
        act_out[slot] = act
        made = matmul(act, weight[...]).astype(jnp.bfloat16)
        qkv_out[slot, :, :width] = made[:, :width] * jnp.bfloat16(0.125)
        qkv_out[slot, :, width:] = made[:, width:]

    @pl.when(chip + 1 < chips)
    def _():
        ring(me, 1).start()

    @pl.when(chip > 0)
    def _():
        ring(me, -1).start()

    across(me).start()
    project_block(me)
    other = chip * 2 + 1 - core
    across(other).wait_recv()
    project_block(other)

    for step in range(1, chips):
        for way in (1, -1):
            source = chip - way * step

            @pl.when((source >= 0) & (source < chips))
            def _():
                slot = source * 2 + core
                ring(slot, way).wait_recv()

                @pl.when((chip + way >= 0) & (chip + way < chips))
                def _():
                    ring(slot, way).start()

                across(slot).start()

        for way in (1, -1):
            source = chip - way * step

            @pl.when((source >= 0) & (source < chips))
            def _():
                project_block(source * 2 + core)
                across(source * 2 + 1 - core).wait_recv()
                project_block(source * 2 + 1 - core)

    mask = causal(rows, False)

    def send(block):
        return pltpu.make_async_remote_copy(
            src_ref=low.at[block], dst_ref=att_out.at[me], send_sem=out_send.at[block],
            recv_sem=out_recv.at[me], device_id={"blk": block}, device_id_type=MESH,
        )

    def query_block(i, carry):
        queries = qkv_out[i, :, :width]
        split = [head_only(queries, h) for h in range(heads)]

        def update(j, state, masked):
            keys = qkv_out[j, :, width : 2 * width]
            values = qkv_out[j, :, 2 * width :]
            new = []
            for h in range(heads):
                peak, total, acc = state[3 * h : 3 * h + 3]
                scores = matmul(split[h], keys, (1, 1))
                if masked:
                    scores = jnp.where(mask, scores, -1e30)
                top = jnp.maximum(peak, jnp.max(scores, axis=-1, keepdims=True))
                weights = jnp.exp(scores - top)
                rescale = jnp.exp(peak - top)
                total = total * rescale + jnp.sum(weights, axis=-1, keepdims=True)
                acc = acc * rescale + matmul(weights.astype(jnp.bfloat16), values)
                new += [top, total, acc]
            return tuple(new)

        start = []
        for _ in range(heads):
            start += [jnp.full((rows, 1), -1e30, jnp.float32), jnp.zeros((rows, 1), jnp.float32), jnp.zeros((rows, width), jnp.float32)]
        state = update(i, tuple(start), True)
        state = lax.fori_loop(0, i, lambda j, held: update(j, held, False), state)
        lane = lax.broadcasted_iota(jnp.int32, (rows, width), 1) // HEAD
        full = state[2] / state[1]
        stat = jnp.broadcast_to(state[0] + jnp.log(state[1]), (rows, width))
        for h in range(1, heads):
            full = jnp.where(lane == h, state[3 * h + 2] / state[3 * h + 1], full)
            stat = jnp.where(lane == h, state[3 * h] + jnp.log(state[3 * h + 1]), stat)
        full_out[i] = full
        stat = stat.T
        for h in range(heads):
            lse_out[i, h : h + 1, :] = stat[h * HEAD : h * HEAD + 1, :]
        low[i] = full.astype(jnp.bfloat16)

        @pl.when(i != me)
        def _():
            send(i).start()

        return carry

    lax.fori_loop(0, blks, query_block, 0)
    att_out[me] = low[me]

    def finish(i, carry):
        @pl.when(i != me)
        def _():
            send(i).wait_send()
            pltpu.make_async_remote_copy(
                src_ref=low.at[i], dst_ref=att_out.at[i], send_sem=out_send.at[i],
                recv_sem=out_recv.at[i], device_id={"blk": i}, device_id_type=MESH,
            ).wait_recv()

        return carry

    lax.fori_loop(0, blks, finish, 0)

    @pl.when(chip + 1 < chips)
    def _():
        ring(me, 1).wait_send()

    @pl.when(chip > 0)
    def _():
        ring(me, -1).wait_send()

    across(me).wait_send()
    for step in range(1, chips):
        for way in (1, -1):
            source = chip - way * step

            @pl.when((source >= 0) & (source < chips))
            def _():
                slot = source * 2 + core

                @pl.when((chip + way >= 0) & (chip + way < chips))
                def _():
                    ring(slot, way).wait_send()

                across(slot).wait_send()


def attention_forward(frames, weight, gain, shift, blks):
    rows, depth = frames.shape
    width = weight.shape[1] // 3
    vmem = pl.BlockSpec(memory_space=pltpu.VMEM)
    dma = pltpu.SemaphoreType.DMA
    return pl.pallas_call(
        forward_kernel,
        out_shape=[
            jax.ShapeDtypeStruct((blks, rows, width), jnp.bfloat16),
            jax.ShapeDtypeStruct((blks, rows, depth), jnp.bfloat16),
            jax.ShapeDtypeStruct((blks, rows, 3 * width), jnp.bfloat16),
            jax.ShapeDtypeStruct((blks, rows, width), jnp.float32),
            jax.ShapeDtypeStruct((blks, 8, rows), jnp.float32),
        ],
        in_specs=[vmem] * 4,
        out_specs=[vmem] * 5,
        scratch_shapes=[
            pltpu.VMEM((blks, rows, depth), jnp.bfloat16), pltpu.VMEM((blks, rows, width), jnp.bfloat16),
            dma((2, blks)), dma((blks,)), dma((blks,)), dma((blks,)), dma((blks,)), dma((blks,)),
        ],
        compiler_params=pltpu.CompilerParams(collective_id=1, has_side_effects=True, vmem_limit_bytes=48 << 20),
    )(frames, weight, gain, shift)


PLAN = ((), (), ((-1, 0), ), (), ((-1, 1), ), (), ((-1, 2), ), ((0, 0), (-1, 3)), (), ((-1, 4), (-1, 5), (-1, 6)), ((0, 1), ), ((-1, 7), ), ((1, 0), (0, 2)), (), ((2, 0), ), (), ((3, 0), ), ((0, 3), (0, 4)), ((-1, 8), ), (), (), ((0, 5), (0, 6)), ((-1, 9), (-1, 10)), ((1, 1), (1, 3), (0, 7)), ((1, 2), ), ((2, 1), (2, 3), (1, 4), (0, 8)), ((2, 2), ), ((3, 1), (1, 5), (1, 6)), ((3, 3), ), ((2, 4), ), (), ((3, 2), (3, 4), (2, 5), (2, 6), (1, 7), (1, 8), (0, 9), (0, 10)), ((3, 5), ), ())


def bits_of(size):
    return size.bit_length() - 1


class Halving:
    def __init__(self, left, order, bufs, sems):
        self.order, self.bufs, self.sems = order, bufs, sems
        self.posts, held = [], list(left)
        for split in order:
            self.posts.append(1 << (len(held) - 1 - held.index(split)))
            held.remove(split)

    def parts(self, stage):
        axis, bit = self.order[stage]
        me = lax.axis_index(axis)
        mine = (me // (1 << bit)) % 2
        return {axis: me + (1 << bit) * (1 - 2 * mine)}, mine

    def half(self, stage, which):
        ref, post = self.bufs[stage], self.posts[stage]
        return ref.reshape(ref.shape[0] // (2 * post), 2, post, *ref.shape[1:]), which

    def copy(self, stage):
        partner, mine = self.parts(stage)
        into = self.bufs[stage + 1]
        view, which = self.half(stage, 1 - mine)
        return pltpu.make_async_remote_copy(
            src_ref=view.at[:, which],
            dst_ref=into.reshape(into.shape[0] // self.posts[stage], self.posts[stage], *into.shape[1:]),
            send_sem=self.sems.at[0, stage],
            recv_sem=self.sems.at[1, stage],
            device_id=partner,
            device_id_type=MESH,
        )

    def start(self, stage=0):
        self.copy(stage).start()

    def turn(self, stage):
        self.copy(stage).wait()
        _, mine = self.parts(stage)
        into, ref, post = self.bufs[stage + 1], self.bufs[stage], self.posts[stage]

        def one(i, carry):
            into[i] = into[i] + ref[((i // post) * 2 + mine) * post + i % post]
            return carry

        lax.fori_loop(0, into.shape[0], one, 0)
        if stage + 1 < len(self.order):
            self.start(stage + 1)


def columns(axis_sum):
    return jnp.sum(axis_sum.reshape(-1, 8, axis_sum.shape[-1]), axis=0)


def norm_back(value, grad, gain, base, write, vec, row):
    rows, width = grad.shape
    step = min(64, rows)

    def chunk(i, sums):
        at = pl.ds(pl.multiple_of(i * step, step), step)
        centred = value[at, :].astype(jnp.float32)
        centred = centred - jnp.mean(centred, axis=-1, keepdims=True)
        scale = lax.rsqrt(jnp.mean(centred * centred, axis=-1, keepdims=True) + 1e-05)
        unit = centred * scale
        error = grad[at, :]
        term = error * gain
        back = scale * (term - jnp.mean(term, axis=-1, keepdims=True) - unit * jnp.mean(term * unit, axis=-1, keepdims=True))
        write(at, base[at, :].astype(jnp.float32) + back)
        return sums[0] + columns(error * unit), sums[1] + columns(error)

    zero = jnp.zeros((8, width), jnp.float32)
    gain_sum, shift_sum = lax.fori_loop(0, rows // step, chunk, (zero, zero))
    vec[row : row + 1, :] = jnp.sum(gain_sum, axis=0, keepdims=True)
    vec[row + 1 : row + 2, :] = jnp.sum(shift_sum, axis=0, keepdims=True)


def tail_kernel(names, clip_stages, blk_stages, *refs):
    r = SimpleNamespace(**dict(zip(names, refs)))
    rest = list(refs[len(names) :])
    stages = clip_stages + blk_stages - 1
    r.wide, rest = rest[:stages], rest[stages:]
    r.tall, rest = rest[:stages], rest[stages:]
    r.kv, rest = rest[:blk_stages], rest[blk_stages:]
    r.head_w, r.text_w = rest[:clip_stages], rest[clip_stages:]
    clips, blks = lax.axis_size("clip"), lax.axis_size("blk")
    me, clip = lax.axis_index("blk"), lax.axis_index("clip")
    core = me % 2
    pair = {"blk": me + 1 - 2 * core}
    devices = clips * blks
    rows, depth = r.frames.shape
    half = depth // 2
    width = depth // blks
    heads = width // HEAD
    tokens = r.text.shape[0]
    chunk = r.first.shape[-1]
    chunks = r.hidden_in.shape[1] // chunk
    bf16, f32 = jnp.bfloat16, jnp.float32
    gains = r.gains
    vec = r.vec

    barrier = pltpu.get_barrier_semaphore()
    for step in range(1, clips):
        pl.semaphore_signal(barrier, inc=1, device_id={"clip": (clip + step) % clips}, device_id_type=MESH)
    greet("blk", clips - 1)

    sem_at = [0]

    def sem():
        sem_at[0] += 1
        return r.sems.at[sem_at[0] - 1]

    def local(source, target):
        return pltpu.make_async_copy(source, target, sem())

    def remote(source, target, where):
        return pltpu.make_async_remote_copy(
            src_ref=source, dst_ref=target, send_sem=sem(), recv_sem=sem(), device_id=where, device_id_type=MESH
        )

    own, other = pl.ds(0, rows), pl.ds(rows, rows)
    my_half = pl.ds(pl.multiple_of(core * half, half), half)
    its_half = pl.ds(pl.multiple_of((1 - core) * half, half), half)


    def hidden_loads(j):
        at = pl.ds(j * chunk, chunk)
        return (
            local(r.hidden_in.at[:, at], r.first.at[j % 2]),
            local(r.hidden_out.at[at, :], r.second.at[j % 2]),
        )

    act_here = local(r.act_three, r.cat_three.at[own])
    grad_here = local(r.cotangent, r.dy)
    act_here.start()
    grad_here.start()
    weights = {j: hidden_loads(j) for j in range(min(2, chunks))}
    for copies in weights.values():
        for copy in copies:
            copy.start()
    exchanged = {}
    three, mixed, two, att, grads = range(5)
    for name, (source, cat) in enumerate(((r.act_three, r.cat_three), (r.mixed, r.cat_mixed), (r.act_two, r.cat_two), (r.att, r.cat_att))):
        exchanged[name] = [remote(source, cat.at[other], pair)]
        if name != three:
            exchanged[name].append(local(source, cat.at[own]))
    exchanged[grads] = [
        remote(r.cotangent.at[:, its_half], r.cat_dy.at[other], pair),
        local(r.cotangent.at[:, my_half], r.cat_dy.at[own]),
    ]
    for name in (three, grads, mixed, two, att):
        for copy in exchanged[name]:
            copy.start()
    small = [
        local(source, into)
        for source, into in ((r.after_cross, r.value), (r.text_keys, r.tk), (r.text_values, r.tv), (r.cross_queries, r.cq))
    ]
    for copy in small:
        copy.start()
    act_here.wait()
    grad_here.wait()

    clip_bits = [("clip", k) for k in range(bits_of(clips))]
    blk_bits = [("blk", k) for k in range(bits_of(blks))]
    left = clip_bits[::-1] + blk_bits[::-1]
    orders = (clip_bits + blk_bits[1:], clip_bits[::-1] + blk_bits[1:])
    pieces = []
    for p in range(2 * chunks + 3):
        wide = p < chunks or p >= 2 * chunks
        held = [r.wide_own, *r.wide] if wide else [r.tall_own, *r.tall]
        nth = (p if p < chunks else p - chunks) if wide else p - chunks
        pieces.append(
            Halving(left, orders[p % 2], [held[0].at[nth % chunks]] + [level.at[nth] for level in held[1:]], r.piece_sems.at[p])
        )

    def finish(p, out, column, rows_out):
        piece = pieces[p]
        size = piece.bufs[-1].shape[-1]
        base = core * half + column if p >= chunks and p < 2 * chunks else column + core * half
        at = pl.ds(pl.multiple_of(base, size), size)
        tall_piece = chunks <= p < 2 * chunks
        stage = r.tall_fix.at[p - chunks] if tall_piece else r.wide_fix.at[p if p < chunks else p - chunks]
        stage[...] = piece.bufs[-1][1 - core].astype(f32)
        copy = remote(stage, out.at[:, at], pair)
        copy.start()
        out[:, at] = piece.bufs[-1][core].astype(f32)
        return copy

    fixes = []

    def task(stage, p):
        if stage < stages:
            pieces[p].turn(stage)
        if stage == stages - 1:
            if p < chunks:
                fixes.append((p, finish(p, r.hidden_in_out, p * chunk, None)))
            elif p < 2 * chunks:
                fixes.append((p, finish(p, r.hidden_out_out, (p - chunks) * (half // chunks), None)))
            else:
                fixes.append((p, finish(p, (r.cross_out_out, r.cross_query_out, r.self_out_out)[p - 2 * chunks], 0, None)))

    total = len(pieces)
    at_point, reached = [0], [-2] * total

    def reach(stage, p):
        while reached[p] < stage:
            reached[p] += 1
            if reached[p] < 0:
                pieces[p].start()
            else:
                task(reached[p], p)

    def point():
        if at_point[0] < len(PLAN):
            for stage, p in PLAN[at_point[0]]:
                if p < total:
                    reach(stage, p)
        at_point[0] += 1

    def outer(cat_left, cat_right, into):
        entries, block = into.shape[:2]
        group = max(1, 256 // block)

        def part(m, carry):
            at = pl.ds(pl.multiple_of(m * group * block, group * block), group * block)
            made = matmul(cat_left[:, at], cat_right[...], (0, 0))
            into[pl.ds(m * group, group)] = made.reshape(group, block, made.shape[-1]).astype(bf16)
            return carry

        lax.fori_loop(0, entries // group, part, 0)

    swaps = {}
    sub = min(256, chunk)
    for j in range(chunks):
        for copy in weights[j]:
            copy.wait()
        first, second = r.first.at[j % 2], r.second.at[j % 2]
        pre_low = r.pre_low.at[j % 2]
        hidden = r.cat_hidden.at[own, pl.ds(j * chunk, chunk)]
        if j >= 2:
            swaps[j - 2][0].wait_send()

        def part(u, carry):
            at = pl.ds(pl.multiple_of(u * sub, sub), sub)
            pre = matmul(r.cat_three[own, :], first[:, at])
            grad = matmul(r.dy[...], second[at, :], (1, 1))
            phi = 0.5 * (1.0 + lax.erf(pre * math.sqrt(0.5)))
            slope = phi + pre * (jnp.exp(-0.5 * pre * pre) * (1.0 / math.sqrt(2.0 * math.pi)))
            hidden[:, at] = (pre * phi).astype(bf16)
            pre_low[:, at] = (grad * slope).astype(bf16)
            return carry

        lax.fori_loop(0, chunk // sub, part, 0)
        swaps[j] = (
            remote(pre_low.at[:, pl.ds(pl.multiple_of((1 - core) * (chunk // 2), chunk // 2), chunk // 2)], r.cat_pre.at[j, other], pair),
            remote(hidden, r.cat_hidden.at[other, pl.ds(j * chunk, chunk)], pair),
        )
        for copy in swaps[j]:
            copy.start()
        r.cat_pre[j, own, :] = pre_low[:, pl.ds(pl.multiple_of(core * (chunk // 2), chunk // 2), chunk // 2)]
        made = matmul(hidden[...], second[...])
        back = matmul(pre_low[...], first[...], (1, 1))
        if j == 0:
            r.total[...] = made
            r.grad[...] = back
        else:
            r.total[...] += made
            r.grad[...] += back
        if j + 2 < chunks:
            weights[j + 2] = hidden_loads(j + 2)
            for copy in weights[j + 2]:
                copy.start()
        point()
        if j == 0:
            for copy in exchanged[three]:
                copy.wait()
        else:
            swaps[j - 1][0].wait_recv()
            outer(r.cat_three, r.cat_pre.at[j - 1], pieces[j - 1].bufs[0])
            point()
    for j in (chunks - 2, chunks - 1):
        swaps[j][0].wait_send()
    later = [
        local(source, into.at[slot])
        for source, into, slot in ((r.cross_out, r.first, 0), (r.cross_query, r.second, 0), (r.self_out, r.first, 1))
    ]
    for copy in later:
        copy.start()
    swaps[chunks - 1][0].wait_recv()
    outer(r.cat_three, r.cat_pre.at[chunks - 1], pieces[chunks - 1].bufs[0])
    point()
    for copy in small:
        copy.wait()
    r.mixed_grad[...] = (r.value[...] + r.total[...]).astype(bf16)
    output_copy = local(r.mixed_grad, r.output)
    output_copy.start()
    for copy in exchanged[grads]:
        copy.wait()
    for j in range(chunks):
        swaps[j][1].wait()
    tall = half // chunks
    block = r.tall_own.shape[2]
    group = max(1, 512 // block)

    def tall_part(m, carry):
        at = pl.ds(pl.multiple_of(m * group * block, group * block), group * block)
        made = matmul(r.cat_hidden[:, at], r.cat_dy[...], (0, 0))
        for w in range(chunks):
            r.tall_own[w, pl.ds(m * group, group)] = made[:, w * tall : (w + 1) * tall].reshape(group, block, tall).astype(bf16)
        return carry

    turns = devices // group
    lax.fori_loop(0, turns // 2, tall_part, 0)
    point()
    lax.fori_loop(turns // 2, turns, tall_part, 0)
    point()

    def keep_two(at, value):
        r.total[at, :] = value
        r.low[0, at, :] = value.astype(bf16)

    norm_back(r.value, r.grad, gains[2:3, :], r.dy, keep_two, vec, 4)
    second_value = local(r.after_self, r.value)
    second_value.start()

    def share(which):
        copy = remote(r.low.at[which, :, its_half], r.cat_low.at[which, other], pair)
        copy.start()
        r.cat_low[which, own, :] = r.low[which, :, my_half]
        return copy

    shared = [share(0)]
    later[0].wait()
    output_copy.wait()
    r.mixed_grad[...] = matmul(r.low[0], r.first[0], (1, 1)).astype(bf16)
    point()
    lanes = min(128, depth)
    groups = lanes // width

    def cross(t, carry):
        at = pl.ds(pl.multiple_of(t * lanes, lanes), lanes)
        queries, keys, values, grads = r.cq[:, at], r.tk[:, at], r.tv[:, at], r.mixed_grad[:, at]
        query_sum = jnp.zeros((rows, lanes), f32)
        key_sum, value_sum = jnp.zeros((tokens, lanes), f32), jnp.zeros((tokens, lanes), f32)
        for h in range(lanes // HEAD):
            query_h, grad_h, key_h = head_only(queries, h), head_only(grads, h), head_only(keys, h)
            scores = matmul(keys, query_h, (1, 1)) * 0.125 + r.hidden_tokens[:, :1]
            scores = jnp.exp(scores - jnp.max(scores, axis=0, keepdims=True))
            prob = scores / jnp.sum(scores, axis=0, keepdims=True)
            dprob = matmul(values, grad_h, (1, 1))
            dscore = (prob * (dprob - jnp.sum(prob * dprob, axis=0, keepdims=True))).astype(bf16)
            query_sum = query_sum + matmul(dscore, key_h, (0, 0))
            key_sum = key_sum + matmul(dscore, query_h)
            value_sum = value_sum + matmul(prob.astype(bf16), grad_h)
        r.low[1, :, at] = (query_sum * 0.125).astype(bf16)
        for g in range(groups):
            r.kv_own[t * groups + g, :, :width] = (key_sum[:, g * width : (g + 1) * width] * 0.125).astype(bf16)
            r.kv_own[t * groups + g, :, width:] = value_sum[:, g * width : (g + 1) * width].astype(bf16)
        return carry

    turns = depth // lanes
    for quarter in range(4):
        lax.fori_loop(turns * quarter // 4, turns * (quarter + 1) // 4, cross, 0)
        point()
    text_load = local(r.text, r.tk)
    text_load.start()
    text_sum = Halving(blk_bits[::-1], blk_bits, [r.kv_own, *r.kv], r.kv_sems)
    text_sum.start()
    shared.append(share(1))
    point()
    later[1].wait()
    r.grad[...] = matmul(r.low[1], r.second[0], (1, 1))
    second_value.wait()
    shared[0].wait_send()

    def keep_one(at, value):
        r.total[at, :] = value
        r.low[0, at, :] = value.astype(bf16)

    norm_back(r.value, r.grad, gains[1:2, :], r.total, keep_one, vec, 2)
    point()
    for copy in (share_one := [remote(r.low.at[0, :, its_half], r.cat_low.at[2, other], pair)]):
        copy.start()
    r.cat_low[2, own, :] = r.low[0, :, my_half]
    later[2].wait()
    att_grad = matmul(r.low[0], r.first[1], (1, 1)).astype(bf16)
    for s in range(blks):
        r.grad_own[s] = att_grad[:, s * width : (s + 1) * width]

    block_sems = r.block_sems

    def fetch(peer, source):
        return pltpu.make_async_remote_copy(
            src_ref=r.grad_own.at[peer], dst_ref=r.grad_all.at[source], send_sem=block_sems.at[0, peer],
            recv_sem=block_sems.at[1, source], device_id={"blk": peer}, device_id_type=MESH,
        )

    def give(peer, source):
        return pltpu.make_async_remote_copy(
            src_ref=r.qkv_here.at[peer], dst_ref=r.sums_in.at[source], send_sem=block_sems.at[2, peer],
            recv_sem=block_sems.at[3, source], device_id={"blk": peer}, device_id_type=MESH,
        )

    for step in range(1, blks):
        fetch((me + step) % blks, me).start()
    r.grad_all[me] = r.grad_own[me]
    attention_inputs = [local(source, into) for source, into in ((r.qkv, r.qkv_here), (r.full, r.full_here), (r.lse, r.lse_rows))]
    for copy in attention_inputs:
        copy.start()
    projections = [
        local(source, into.at[slot])
        for source, into, slot in ((r.self_query, r.first, 0), (r.self_key, r.second, 0), (r.self_value, r.second, 1))
    ]
    for copy in projections:
        copy.start()
    point()
    text_sum.turn(0)

    def last_pieces():
        for n, (name, cat, wait) in enumerate(((mixed, r.cat_mixed, shared[0]), (two, r.cat_two, shared[1]), (att, r.cat_att, share_one[0]))):
            for copy in exchanged[name]:
                copy.wait()
            wait.wait_recv() if n == 0 else wait.wait()
            if n < chunks:
                reach(0, n)
            outer(cat, r.cat_low.at[n], pieces[2 * chunks + n].bufs[0])
            point()

    last_pieces()
    text_done = text_sum.bufs[-1].at[0]
    text_rows = tokens // blks

    def swap_text(peer, source):
        return pltpu.make_async_remote_copy(
            src_ref=text_done.at[pl.ds(pl.multiple_of(peer * text_rows, text_rows), text_rows)], dst_ref=r.text_out.at[source],
            send_sem=block_sems.at[4, peer], recv_sem=block_sems.at[5, source], device_id={"blk": peer}, device_id_type=MESH,
        )

    clip_left = clip_bits[::-1] + blk_bits[::-1]
    text_w = Halving(clip_left, clip_bits[::-1], [r.text_w_own, *r.text_w], r.clip_sems.at[0])
    head_w = Halving(clip_left, clip_bits, [r.head_w_own, *r.head_w], r.clip_sems.at[1])

    def text_ready():
        for step in range(1, blks):
            swap_text((me + step) % blks, me).start()
        r.text_out[me] = text_done[pl.ds(pl.multiple_of(me * text_rows, text_rows), text_rows), :]
        text_load.wait()
        outer(r.tk, text_done, r.text_w_own)
        text_w.start()

    for copy in attention_inputs:
        copy.wait()
    qkv, full = r.qkv_here, r.full_here
    for step in range(1, blks):
        fetch((me + step) % blks, (me + step) % blks).wait_recv()
    text_sum.turn(1)
    point()
    for i in range(blks):
        product = (r.grad_all[i].astype(f32) * full[i]).T
        for h in range(heads):
            r.delta_rows[i, h : h + 1, :] = jnp.sum(product[h * HEAD : (h + 1) * HEAD], axis=0, keepdims=True)

    full[...] = jnp.zeros_like(full)
    point()
    mask = causal(rows, True)

    def act_load(j):
        return pltpu.make_async_copy(r.act_all.at[j], r.low.at[j % 2], block_sems.at[6, j])

    act_load(0).start()
    act_load(1).start()

    def key_block(j):
        keys = qkv[j, :, width : 2 * width]
        values = qkv[j, :, 2 * width :]

        def update(i, state, masked):
            key_sum, value_sum = state
            queries = qkv[i, :, :width]
            grad = r.grad_all[i]
            summed = None
            for h in range(heads):
                query_h, grad_h, key_h = head_only(queries, h), head_only(grad, h), head_only(keys, h)
                scores = matmul(keys, query_h, (1, 1))
                probs = jnp.exp(scores - r.lse_rows[i, h : h + 1, :])
                if masked:
                    probs = jnp.where(mask, probs, 0.0)
                dprobs = matmul(values, grad_h, (1, 1))
                dscores = (probs * (dprobs - r.delta_rows[i, h : h + 1, :])).astype(bf16)
                value_sum = value_sum + matmul(probs.astype(bf16), grad_h)
                key_sum = key_sum + matmul(dscores, query_h)
                term = matmul(dscores, key_h, (0, 0))
                summed = term if summed is None else summed + term
            full[i] += summed
            return key_sum, value_sum

        zero = jnp.zeros((rows, width), f32)
        state = update(j, (zero, zero), True)
        if j + 1 < blks:
            state = lax.fori_loop(j + 1, blks, lambda i, held: update(i, held, False), state)
        r.qkv_here[j, :, :width] = (full[j] * 0.125).astype(bf16)
        r.qkv_here[j, :, width : 2 * width] = state[0].astype(bf16)
        r.qkv_here[j, :, 2 * width :] = state[1].astype(bf16)

        @pl.when(j != me)
        def _():
            give(j, me).start()

        act_load(j).wait()
        made = matmul(r.low[j % 2], r.qkv_here[j], (0, 0))
        if j == 0:
            r.head_sum[...] = made
        else:
            r.head_sum[...] += made
        if j + 2 < blks:
            act_load(j + 2).start()

    for j in range(blks):
        key_block(j)
        if j == 1:
            for stage in range(2, len(blk_bits)):
                text_sum.turn(stage)
            text_ready()
        if j == min(4, blks - 2):
            text_w.turn(0)
        point()
    for stage in range(1, len(clip_bits)):
        text_w.turn(stage)
    r.sums_in[me] = r.qkv_here[me]
    r.head_w_own[...] = r.head_sum[...].reshape(r.head_w_own.shape).astype(bf16)
    head_w.start()

    def swap_w(summed, out, base, peer, source):
        return pltpu.make_async_remote_copy(
            src_ref=summed.bufs[-1].at[peer], dst_ref=out.at[source], send_sem=block_sems.at[base, peer],
            recv_sem=block_sems.at[base + 1, source], device_id={"blk": peer}, device_id_type=MESH,
        )

    for step in range(1, blks):
        swap_w(text_w, r.text_w_out, 7, (me + step) % blks, me).start()
    r.text_w_out[me] = text_w.bufs[-1][me]
    for copy in projections:
        copy.wait()
    first_value = local(r.frames, r.mixed_grad)
    first_value.start()
    for step in range(1, blks):
        give((me + step) % blks, (me + step) % blks).wait_recv()
    grad_rows = [r.low.at[0], r.low.at[1], r.cq]
    for s in range(blks):
        for t in range(3):
            grad_rows[t][:, s * width : (s + 1) * width] = r.sums_in[s, :, t * width : (t + 1) * width]
    point()
    head_w.turn(0)
    r.grad[...] = matmul(grad_rows[0][...], r.first[0], (1, 1))
    r.grad[...] += matmul(grad_rows[1][...], r.second[0], (1, 1))
    r.grad[...] += matmul(grad_rows[2][...], r.second[1], (1, 1))
    first_value.wait()
    point()

    def keep_frames(at, value):
        r.value[at, :] = value

    norm_back(r.mixed_grad, r.grad, gains[0:1, :], r.total, keep_frames, vec, 0)
    frames_copy = local(r.value, r.frames_grad)
    frames_copy.start()
    vec[6:8, :] = jnp.zeros((2, depth), f32)
    part = depth // clips

    def swap_vec(peer, source):
        return pltpu.make_async_remote_copy(
            src_ref=vec.at[:, pl.ds(pl.multiple_of(peer * part, part), part)], dst_ref=r.vec_in.at[source],
            send_sem=r.vec_sems.at[0, peer], recv_sem=r.vec_sems.at[1, source], device_id={"clip": peer}, device_id_type=MESH,
        )

    for step in range(1, clips):
        swap_vec((clip + step) % clips, clip).start()
    r.vec_in[clip] = vec[:, pl.ds(pl.multiple_of(clip * part, part), part)]
    for stage in range(1, len(clip_bits)):
        head_w.turn(stage)
    for step in range(1, blks):
        swap_w(head_w, r.head_w_out, 9, (me + step) % blks, me).start()
    r.head_w_out[me] = head_w.bufs[-1][me]
    point()
    for step in range(1, clips):
        swap_vec((clip + step) % clips, (clip + step) % clips).wait_recv()
    r.vec_sum[me] = jnp.sum(r.vec_in[...], axis=0)

    def share_vec(peer, source):
        return pltpu.make_async_remote_copy(
            src_ref=r.vec_sum.at[me], dst_ref=r.vec_sum.at[source], send_sem=block_sems.at[11, peer],
            recv_sem=block_sems.at[12, source], device_id={"blk": peer}, device_id_type=MESH,
        )

    for step in range(1, blks):
        share_vec((me + step) % blks, me).start()
    for k in range(total + 2 * stages):
        for stage in range(stages):
            if 0 <= k - 2 * stage < total:
                reach(stage, k - 2 * stage)
    for step in range(1, blks):
        share_vec((me + step) % blks, (me + step) % blks).wait_recv()
    r.vec_out[...] = jnp.sum(r.vec_sum[...], axis=0)
    for _, copy in fixes:
        copy.wait()
    frames_copy.wait()
    for step in range(1, clips):
        swap_vec((clip + step) % clips, clip).wait_send()
    for step in range(1, blks):
        peer = (me + step) % blks
        fetch(peer, me).wait_send()
        give(peer, me).wait_send()
        swap_text(peer, me).wait_send()
        swap_text(peer, peer).wait_recv()
        for summed, out, base in ((text_w, r.text_w_out, 7), (head_w, r.head_w_out, 9)):
            swap_w(summed, out, base, peer, me).wait_send()
            swap_w(summed, out, base, peer, peer).wait_recv()
        share_vec(peer, me).wait_send()


def backward(inputs, gains, hidden_tokens, clips, blks):
    rows, depth = inputs["frames"].shape
    tokens = inputs["text"].shape[0]
    hidden = inputs["hidden_in"].shape[1]
    devices, width, half = clips * blks, depth // blks, depth // 2
    chunk = min(1024, hidden)
    chunks = hidden // chunk
    own = depth // devices
    tall = half // chunks
    stages = bits_of(clips) + bits_of(blks) - 1
    bf16, f32 = jnp.bfloat16, jnp.float32
    hbm, vmem = pl.BlockSpec(memory_space=pltpu.MemorySpace.HBM), pl.BlockSpec(memory_space=pltpu.VMEM)
    dma = pltpu.SemaphoreType.DMA
    shape = jax.ShapeDtypeStruct
    outs = dict(
        output=shape((rows, depth), bf16), frames_grad=shape((rows, depth), f32), text_out=shape((blks, tokens // blks, 2 * width), bf16),
        head_w_out=shape((blks, own, 3 * width), bf16), text_w_out=shape((blks, own, 2 * width), bf16),
        hidden_in_out=shape((own, hidden), f32), hidden_out_out=shape((hidden // devices, depth), f32),
        cross_out_out=shape((own, depth), f32), cross_query_out=shape((own, depth), f32), self_out_out=shape((own, depth), f32),
        vec_out=shape((8, depth // clips), f32),
    )
    scratch = dict(
        first=((2, depth, chunk), bf16), second=((2, chunk, depth), bf16),
        cat_three=((2 * rows, depth), bf16), cat_mixed=((2 * rows, depth), bf16), cat_two=((2 * rows, depth), bf16),
        cat_att=((2 * rows, depth), bf16), cat_dy=((2 * rows, half), bf16), dy=((rows, depth), bf16),
        cat_hidden=((2 * rows, hidden), bf16), pre_low=((2, rows, chunk), bf16), cat_pre=((chunks, 2 * rows, chunk // 2), bf16),
        total=((rows, depth), f32), grad=((rows, depth), f32), value=((rows, depth), f32),
        low=((2, rows, depth), bf16), cat_low=((3, 2 * rows, half), bf16), mixed_grad=((rows, depth), bf16),
        cq=((rows, depth), bf16), tk=((tokens, depth), bf16), tv=((tokens, depth), bf16),
        vec=((8, depth), f32), vec_in=((clips, 8, depth // clips), f32), vec_sum=((blks, 8, depth // clips), f32),
        wide_own=((chunks, devices, own, half), bf16), tall_own=((chunks, devices, hidden // devices, tall), bf16),
        wide_fix=((chunks + 3, own, half), f32), tall_fix=((chunks, hidden // devices, tall), f32),
        kv_own=((blks, tokens, 2 * width), bf16),
        head_w_own=((devices, own, 3 * width), bf16), text_w_own=((devices, own, 2 * width), bf16),
        grad_own=((blks, rows, width), bf16), grad_all=((blks, rows, width), bf16), sums_in=((blks, rows, 3 * width), bf16), qkv_here=((blks, rows, 3 * width), bf16), full_here=((blks, rows, width), f32),
        lse_rows=((blks, 8, rows), f32), delta_rows=((blks, 8, rows), f32),
        head_sum=((depth, 3 * width), f32),
    )
    levels = [((chunks + 3, devices >> (s + 1), own, half), bf16) for s in range(stages)]
    levels += [((chunks, devices >> (s + 1), hidden // devices, tall), bf16) for s in range(stages)]
    levels += [((blks >> (s + 1), tokens, 2 * width), bf16) for s in range(bits_of(blks))]
    for parts in (3, 2):
        levels += [((devices >> (s + 1), own, parts * width), bf16) for s in range(bits_of(clips))]
    sems = dict(
        sems=(160,), piece_sems=(2 * chunks + 3, 2, stages), kv_sems=(2, bits_of(blks)), block_sems=(13, blks),
        clip_sems=(2, 2, bits_of(clips)), vec_sems=(2, clips),
    )
    small = dict(gains=gains, hidden_tokens=hidden_tokens)
    names = [*inputs, *small, *outs, *scratch, *sems]
    made = pl.pallas_call(
        partial(tail_kernel, names, bits_of(clips), bits_of(blks)),
        out_shape=list(outs.values()),
        in_specs=[hbm] * len(inputs) + [vmem] * 2,
        out_specs=[hbm if i < 2 else vmem for i in range(len(outs))],
        scratch_shapes=[pltpu.VMEM(*v) for v in scratch.values()] + [dma(v) for v in sems.values()] + [pltpu.VMEM(*v) for v in levels],
        compiler_params=pltpu.CompilerParams(collective_id=3, has_side_effects=True, vmem_limit_bytes=63 << 20),
    )(*inputs.values(), *small.values())
    return SimpleNamespace(**dict(zip(outs, made)))


def layer_norm(inputs, gain_vec, shift_vec):
    centred = inputs - jnp.mean(inputs, axis=-1, keepdims=True)
    variance = jnp.mean(centred * centred, axis=-1, keepdims=True)
    return centred * lax.rsqrt(variance + 1e-05) * gain_vec + shift_vec


def project(left, right):
    return jnp.dot(left, right, preferred_element_type=jnp.float32)


def weight_term(left, right):
    return jnp.einsum("td,te->de", left, right, preferred_element_type=jnp.float32)


def back_project(left, right):
    return jnp.einsum("te,de->td", left, right, preferred_element_type=jnp.float32)


def body(
    frames,
    text_states,
    prompt_lengths,
    cotangent,
    self_query,
    self_key,
    self_value,
    self_out,
    cross_query,
    cross_key,
    cross_value,
    cross_out,
    hidden_in,
    hidden_out,
    first_gain,
    first_shift,
    second_gain,
    second_shift,
    third_gain,
    third_shift,
):
    block_total = lax.axis_size("blk")
    block_rank = lax.axis_index("blk")
    local_frames = frames[0].astype(jnp.float32)
    row_count = local_frames.shape[0]
    clip_total = lax.axis_size("clip")
    devices = clip_total * block_total
    head_width = D // block_total
    own_weight = jnp.concatenate(
        [
            lax.dynamic_slice_in_dim(matrix, block_rank * head_width, head_width, 1)
            for matrix in (self_query, self_key, self_value)
        ],
        axis=1,
    )
    att_parts, act_all, qkv, att_full, log_sums = attention_forward(
        frames[0], own_weight, first_gain[None], first_shift[None], block_total
    )
    att_low = att_parts.transpose(1, 0, 2).reshape(row_count, D)
    after_self = local_frames + project(att_low, self_out)
    normed_two = layer_norm(after_self, second_gain, second_shift)
    act_two = normed_two.astype(jnp.bfloat16)
    local_text = text_states[0]
    cross_queries = (
        project(act_two, cross_query).astype(jnp.bfloat16).reshape(row_count, HEADS, HEAD)
    )
    text_keys = project(local_text, cross_key).astype(jnp.bfloat16).reshape(TEXT, HEADS, HEAD)
    text_values = project(local_text, cross_value).astype(jnp.bfloat16).reshape(TEXT, HEADS, HEAD)
    visible = (jnp.arange(TEXT, dtype=jnp.int32) < prompt_lengths[0])[None, None, :]
    cross_scores = (
        jnp.einsum("qhd,khd->hqk", cross_queries, text_keys, preferred_element_type=jnp.float32)
        * 0.125
    )
    cross_scores = jnp.where(visible, cross_scores, -1e30)
    cross_exp = jnp.exp(cross_scores - jnp.max(cross_scores, axis=-1, keepdims=True))
    cross_prob = cross_exp / jnp.sum(cross_exp, axis=-1, keepdims=True)
    cross_low = cross_prob.astype(jnp.bfloat16)
    cross_mixed = (
        jnp.einsum("hqk,khd->qhd", cross_low, text_values, preferred_element_type=jnp.float32)
        .reshape(row_count, D)
        .astype(jnp.bfloat16)
    )
    after_cross = after_self + project(cross_mixed, cross_out)
    normed_three = layer_norm(after_cross, third_gain, third_shift)
    act_three = normed_three.astype(jnp.bfloat16)
    inputs = dict(
        act_three=act_three, cotangent=cotangent[0], hidden_in=hidden_in, hidden_out=hidden_out, mixed=cross_mixed, act_two=act_two, att=att_low,
        after_cross=after_cross, after_self=after_self, frames=frames[0], text=local_text, text_keys=text_keys.reshape(TEXT, D),
        text_values=text_values.reshape(TEXT, D), cross_queries=cross_queries.reshape(row_count, D), cross_out=cross_out,
        cross_query=cross_query, self_out=self_out, self_query=self_query, self_key=self_key, self_value=self_value,
        qkv=qkv, full=att_full, lse=log_sums, act_all=act_all,
    )
    gains = jnp.stack([first_gain, second_gain, third_gain] + [jnp.zeros_like(first_gain)] * 5)
    hidden_tokens = jnp.where(jnp.arange(TEXT, dtype=jnp.int32) < prompt_lengths[0], 0.0, -1e30).astype(jnp.float32)
    made = backward(inputs, gains, jnp.broadcast_to(hidden_tokens[:, None], (TEXT, 128)), clip_total, block_total)
    output_frames, frames_grad = made.output[None], made.frames_grad[None]
    own = D // devices
    text_parts = made.text_out.reshape(block_total, -1, 2, head_width).transpose(2, 1, 0, 3)
    key_rows, value_rows = text_parts.reshape(2, -1, D)
    text_grad = (back_project(key_rows, cross_key) + back_project(value_rows, cross_value))[None]
    head_sums = made.head_w_out.reshape(block_total, own, 3, head_width).transpose(2, 1, 0, 3).reshape(3, own, D).astype(jnp.float32)
    text_sums = made.text_w_out.reshape(block_total, own, 2, head_width).transpose(2, 1, 0, 3).reshape(2, own, D).astype(jnp.float32)
    vec_own = lax.dynamic_slice_in_dim(made.vec_out, block_rank * own, own, 1)
    summed = [
        head_sums[0], head_sums[1], head_sums[2], made.self_out_out, made.cross_query_out, text_sums[0], text_sums[1],
        made.cross_out_out, made.hidden_in_out, made.hidden_out_out,
    ] + [vec_own[j] for j in range(6)]
    return (
        output_frames,
        frames_grad,
        text_grad,
        summed[0],
        summed[1],
        summed[2],
        summed[3],
        summed[4],
        summed[5],
        summed[6],
        summed[7],
        summed[8],
        summed[9],
        summed[10],
        summed[11],
        summed[12],
        summed[13],
        summed[14],
        summed[15],
    )


def solution(mesh):
    in_specs = (
        P("clip", "blk", None),
        P("clip", None, None),
        P("clip"),
        P("clip", "blk", None),
        P(),
        P(),
        P(),
        P(),
        P(),
        P(),
        P(),
        P(),
        P(),
        P(),
        P(),
        P(),
        P(),
        P(),
        P(),
        P(),
    )
    out_specs = (
        P("clip", "blk", None),
        P("clip", "blk", None),
        P("clip", "blk", None),
        P(("clip", "blk"), None),
        P(("clip", "blk"), None),
        P(("clip", "blk"), None),
        P(("clip", "blk"), None),
        P(("clip", "blk"), None),
        P(("clip", "blk"), None),
        P(("clip", "blk"), None),
        P(("clip", "blk"), None),
        P(("clip", "blk"), None),
        P(("clip", "blk"), None),
        P(("clip", "blk")),
        P(("clip", "blk")),
        P(("clip", "blk")),
        P(("clip", "blk")),
        P(("clip", "blk")),
        P(("clip", "blk")),
    )
    return jax.shard_map(body, mesh=mesh, in_specs=in_specs, out_specs=out_specs, check_vma=False)
```

```python
from functools import partial
import math
from types import SimpleNamespace

import jax
import jax.numpy as jnp
from jax import lax
from jax.experimental import pallas as pl
from jax.experimental.pallas import tpu as pltpu
from jax.sharding import PartitionSpec as P

D = 1024
HEADS = 16
HEAD = 64
TEXT = 256
MESH = pl.DeviceIdType.MESH


def normed(block, gain, shift):
    values = block.astype(jnp.float32)
    centred = values - jnp.mean(values, axis=-1, keepdims=True)
    variance = jnp.mean(centred * centred, axis=-1, keepdims=True)
    return centred * lax.rsqrt(variance + 1e-05) * gain + shift


def matmul(left, right, over=(1, 0)):
    return lax.dot_general(left, right, (((over[0],), (over[1],)), ((), ())), preferred_element_type=jnp.float32)


def greet(axis, others):
    me, size = lax.axis_index(axis), lax.axis_size(axis)
    barrier = pltpu.get_barrier_semaphore()
    for step in range(1, size):
        pl.semaphore_signal(barrier, inc=1, device_id={axis: (me + step) % size}, device_id_type=MESH)
    pl.semaphore_wait(barrier, size - 1 + others)


def head_only(block, head):
    lanes = block.shape[-1]
    if lanes == HEAD:
        return block
    lane = lax.broadcasted_iota(jnp.int32, block.shape, 1)
    return jnp.where((lane // HEAD) == head, block, jnp.zeros_like(block))


def causal(rows, transposed):
    row = lax.broadcasted_iota(jnp.int32, (rows, rows), 0)
    column = lax.broadcasted_iota(jnp.int32, (rows, rows), 1)
    return (row <= column) if transposed else (column <= row)


def token_bias(lengths, tokens):
    token = lax.broadcasted_iota(jnp.int32, (tokens, 1), 0)
    return jnp.where(token < lengths[0], 0.0, -1e30)


def forward_kernel(names, *refs):
    r = SimpleNamespace(**dict(zip(names, refs)))
    blks = lax.axis_size("blk")
    chips = blks // 2
    me = lax.axis_index("blk")
    chip, core = me // 2, me % 2
    rows, width = r.low.shape[1:]
    depth = r.frames_here.shape[1]
    heads = width // HEAD
    bf16, f32 = jnp.bfloat16, jnp.float32
    gathered, qkv = r.gathered, r.qkv
    sem_at = [0]

    def local(source, target):
        sem_at[0] += 1
        return pltpu.make_async_copy(source, target, r.sems.at[sem_at[0] - 1])

    slices = []
    for n, source in enumerate((r.projection_0, r.projection_1, r.projection_2)):
        if source.shape[1] > width:
            source = source.at[:, pl.ds(pl.multiple_of(me * width, width), width)]
        slices.append(local(source, r.weight.at[n]))
    loads = [
        local(source, target)
        for source, target in (
            (r.text, r.text_here), (r.cross_key, r.key_here), (r.cross_value, r.value_here), (r.self_out, r.self_out_here),
            (r.cross_query, r.cross_query_here), (r.cross_out, r.cross_out_here),
        )
    ]
    for copy in slices:
        copy.start()
    greet("blk", 0)
    gathered[me] = r.frames_here[...]
    for copy in loads:
        copy.start()
    hidden_tokens = token_bias(r.lengths, r.tk.shape[0])

    def ring(slot, way):
        return pltpu.make_async_remote_copy(
            src_ref=gathered.at[slot], dst_ref=gathered.at[slot], send_sem=r.ring_send.at[0 if way > 0 else 1, slot],
            recv_sem=r.ring_recv.at[slot], device_id={"blk": me + 2 * way}, device_id_type=MESH,
        )

    def across(slot):
        return pltpu.make_async_remote_copy(
            src_ref=gathered.at[slot], dst_ref=gathered.at[slot], send_sem=r.core_send.at[slot],
            recv_sem=r.core_recv.at[slot], device_id={"blk": chip * 2 + 1 - core}, device_id_type=MESH,
        )

    def send(block):
        return pltpu.make_async_remote_copy(
            src_ref=r.low.at[block], dst_ref=r.att_parts.at[me], send_sem=r.out_send.at[block],
            recv_sem=r.out_recv.at[me], device_id={"blk": block}, device_id_type=MESH,
        )

    def project_block(slot):
        act = normed(gathered[slot], r.gain_0[...], r.shift_0[...]).astype(bf16)
        r.act_all[slot] = act
        qkv[slot, :, :width] = matmul(act, r.weight[0]).astype(bf16) * jnp.bfloat16(0.125)
        qkv[slot, :, width : 2 * width] = matmul(act, r.weight[1]).astype(bf16)
        values = matmul(act, r.weight[2]).astype(bf16)
        qkv[slot, :, 2 * width :] = values
        r.value_rows[slot] = values.T

    mask = causal(rows, True)
    r.peaks[...] = jnp.full_like(r.peaks, -1e30)
    r.totals[...] = jnp.zeros_like(r.totals)
    r.acc[...] = jnp.zeros_like(r.acc)

    def update(i, j):
        def pair(masked):
            keys, queries = qkv[j, :, width : 2 * width], qkv[i, :, :width]
            for h in range(heads):
                own = pl.ds(h * HEAD, HEAD)
                scores = matmul(keys, head_only(queries, h), (1, 1))
                if masked:
                    scores = jnp.where(mask, scores, -1e30)
                peak = r.peaks[i, h : h + 1, :]
                top = jnp.maximum(peak, jnp.max(scores, axis=0, keepdims=True))
                weights = jnp.exp(scores - top)
                rescale = jnp.exp(peak - top)
                r.peaks[i, h : h + 1, :] = top
                r.totals[i, h : h + 1, :] = r.totals[i, h : h + 1, :] * rescale + jnp.sum(weights, axis=0, keepdims=True)
                r.acc[i, own, :] = r.acc[i, own, :] * rescale + matmul(r.value_rows[j, own, :], weights.astype(bf16))

        pl.when(i == j)(lambda: pair(True))
        pl.when(i != j)(lambda: pair(False))

    def settle(i):
        for h in range(heads):
            own = pl.ds(h * HEAD, HEAD)
            r.acc[i, own, :] = r.acc[i, own, :] / r.totals[i, h : h + 1, :]
            r.lse[i, h : h + 1, :] = r.peaks[i, h : h + 1, :] + jnp.log(r.totals[i, h : h + 1, :])
        full = r.acc[i].T
        r.full[i] = full
        r.low[i] = full.astype(bf16)

        @pl.when(i != me)
        def _():
            send(i).start()

    def lower(first, stop):
        def one(i, carry):
            update(i, first)

            @pl.when(i > first)
            def _():
                update(i, first + 1)

            pl.when(first == 0)(lambda: settle(i))
            return carry

        lax.fori_loop(first, stop, one, 0)

    def upper(first, start):
        def one(i, carry):
            lax.fori_loop(start, i + 1, lambda j, held: (update(i, j), held)[1], 0)
            pl.when(start == 0)(lambda: settle(i))
            return carry

        lax.fori_loop(first, first + 2, one, 0)

    @pl.when(chip + 1 < chips)
    def _():
        ring(me, 1).start()

    @pl.when(chip > 0)
    def _():
        ring(me, -1).start()

    across(me).start()
    for copy in slices:
        copy.wait()
    project_block(me)
    other = chip * 2 + 1 - core
    across(other).wait_recv()
    project_block(other)
    upper(chip * 2, chip * 2)
    for copy in loads[:3]:
        copy.wait()
    r.tk[...] = matmul(r.text_here[...], r.key_here[...]).astype(bf16)
    r.tv[...] = matmul(r.text_here[...], r.value_here[...]).astype(bf16)

    for step in range(1, chips):
        for way in (1, -1):
            source = chip - way * step

            @pl.when((source >= 0) & (source < chips))
            def _():
                slot = source * 2 + core
                ring(slot, way).wait_recv()

                @pl.when((chip + way >= 0) & (chip + way < chips))
                def _():
                    ring(slot, way).start()

                across(slot).start()

        for way in (1, -1):
            source = chip - way * step

            @pl.when((source >= 0) & (source < chips))
            def _():
                project_block(source * 2 + core)
                across(source * 2 + 1 - core).wait_recv()
                project_block(source * 2 + 1 - core)
                if way > 0:
                    lower(source * 2, 2 * jnp.minimum(chip + step, chips))
                else:
                    upper(source * 2, 2 * jnp.maximum(chip - step, 0))

    stores = []

    def store(*pairs):
        for source, target in pairs:
            stores.append(local(source, target))
            stores[-1].start()

    store((r.act_all, r.act_all_out), (qkv, r.qkv_out), (r.full, r.full_out), (r.lse, r.lse_out), (r.tk, r.tk_out), (r.tv, r.tv_out))
    r.att_parts[me] = r.low[me]
    for copy in loads[3:]:
        copy.wait()
    for step in range(1, blks):
        peer = (me + step) % blks
        pltpu.make_async_remote_copy(
            src_ref=r.low.at[peer], dst_ref=r.att_parts.at[peer], send_sem=r.out_send.at[peer],
            recv_sem=r.out_recv.at[peer], device_id={"blk": peer}, device_id_type=MESH,
        ).wait_recv()
    for s in range(blks):
        r.att[:, s * width : (s + 1) * width] = r.att_parts[s]

    r.after_self[...] = r.frames_here[...].astype(f32) + matmul(r.att[...], r.self_out_here[...])
    r.act_two[...] = normed(r.after_self[...], r.gain_1[...], r.shift_1[...]).astype(bf16)
    r.cross_queries[...] = matmul(r.act_two[...], r.cross_query_here[...]).astype(bf16)
    lanes = min(128, depth)

    def cross(t, carry):
        at = pl.ds(pl.multiple_of(t * lanes, lanes), lanes)
        queries, keys, values = r.cross_queries[:, at], r.tk[:, at], r.tv[:, at]
        mixed = jnp.zeros((rows, lanes), f32)
        for h in range(lanes // HEAD):
            scores = matmul(keys, head_only(queries, h), (1, 1)) * 0.125 + hidden_tokens
            scores = jnp.exp(scores - jnp.max(scores, axis=0, keepdims=True))
            prob = scores / jnp.sum(scores, axis=0, keepdims=True)
            mixed = mixed + matmul(prob.astype(bf16), head_only(values, h), (0, 0))
        r.mixed[:, at] = mixed.astype(bf16)
        return carry

    lax.fori_loop(0, depth // lanes, cross, 0)
    store((r.att, r.att_out), (r.after_self, r.after_self_out), (r.act_two, r.act_two_out))
    store((r.cross_queries, r.cross_queries_out), (r.mixed, r.mixed_out))
    r.after_cross[...] = r.after_self[...] + matmul(r.mixed[...], r.cross_out_here[...])
    r.act_three[...] = normed(r.after_cross[...], r.gain_2[...], r.shift_2[...]).astype(bf16)

    store((r.after_cross, r.after_cross_out), (r.act_three, r.act_three_out))
    for step in range(1, blks):
        send((me + step) % blks).wait_send()

    @pl.when(chip + 1 < chips)
    def _():
        ring(me, 1).wait_send()

    @pl.when(chip > 0)
    def _():
        ring(me, -1).wait_send()

    across(me).wait_send()
    for step in range(1, chips):
        for way in (1, -1):
            source = chip - way * step

            @pl.when((source >= 0) & (source < chips))
            def _():
                slot = source * 2 + core

                @pl.when((chip + way >= 0) & (chip + way < chips))
                def _():
                    ring(slot, way).wait_send()

                across(slot).wait_send()

    for copy in stores:
        copy.wait()


def forward(frames, projections, norms, lengths, weights, blks):
    rows, depth = frames.shape
    width = depth // blks
    tokens = weights["text"].shape[0]
    bf16, f32 = jnp.bfloat16, jnp.float32
    hbm, vmem = pl.BlockSpec(memory_space=pltpu.MemorySpace.HBM), pl.BlockSpec(memory_space=pltpu.VMEM)
    dma = pltpu.SemaphoreType.DMA
    shape = jax.ShapeDtypeStruct
    small = dict(frames_here=frames)
    for n in range(3):
        small |= {f"gain_{n}": norms[n], f"shift_{n}": norms[3 + n]}
    weights = weights | {f"projection_{n}": projections[n] for n in range(3)}
    kept = dict(
        act_all=((blks, rows, depth), bf16), qkv=((blks, rows, 3 * width), bf16), full=((blks, rows, width), f32),
        lse=((blks, 8, rows), f32), att=((rows, depth), bf16), after_self=((rows, depth), f32), act_two=((rows, depth), bf16),
        cross_queries=((rows, depth), bf16), tk=((tokens, depth), bf16), tv=((tokens, depth), bf16),
        mixed=((rows, depth), bf16), after_cross=((rows, depth), f32), act_three=((rows, depth), bf16),
    )
    outs = {f"{name}_out": shape(*v) for name, v in kept.items()}
    scratch = dict(
        gathered=((blks, rows, depth), bf16), low=((blks, rows, width), bf16), att_parts=((blks, rows, width), bf16),
        value_rows=((blks, width, rows), bf16), peaks=((blks, 8, rows), f32), totals=((blks, 8, rows), f32), acc=((blks, width, rows), f32),
        text_here=((tokens, depth), bf16), key_here=((depth, depth), bf16), value_here=((depth, depth), bf16),
        self_out_here=((depth, depth), bf16), cross_query_here=((depth, depth), bf16), cross_out_here=((depth, depth), bf16),
        weight=((3, depth, width), bf16), **kept,
    )
    sems = dict(ring_send=(2, blks), ring_recv=(blks,), core_send=(blks,), core_recv=(blks,), out_send=(blks,), out_recv=(blks,), sems=(32,))
    names = ["lengths", *small, *weights, *outs, *scratch, *sems]
    made = pl.pallas_call(
        partial(forward_kernel, names),
        out_shape=list(outs.values()),
        in_specs=[pl.BlockSpec(memory_space=pltpu.SMEM)] + [vmem] * len(small) + [hbm] * len(weights),
        out_specs=[hbm] * len(outs),
        scratch_shapes=[pltpu.VMEM(*v) for v in scratch.values()] + [dma(v) for v in sems.values()],
        compiler_params=pltpu.CompilerParams(collective_id=1, has_side_effects=True, vmem_limit_bytes=60 << 20),
    )(lengths, *small.values(), *weights.values())
    return SimpleNamespace(**dict(zip(kept, made)))


EARLY = (0, 2)
PLAN = ((), (), ((-1, 0), ), (), ((-1, 1), ), (), ((-1, 2), ), ((-1, 3), ), ((0, 0), ), ((-1, 4), (-1, 5), (-1, 6), (-1, 7)), ((0, 1), ), (), (), ((0, 2), (0, 3)), ((1, 0), ), (), ((0, 4), ), (), ((0, 5), (-1, 8)), ((-1, 9), ), (), ((2, 0), (1, 2), (1, 3), (0, 6), (0, 7), (-1, 10)), ((1, 1), ), ((1, 4), (1, 5)), (), ((0, 8), ), ((3, 0), (1, 7), (0, 9), (2, 2)), (), ((1, 6), ), (), ((0, 10), ), ((3, 2), (1, 8), (1, 9), (1, 10)), (), ())


def bits_of(size):
    return size.bit_length() - 1


class Halving:
    def __init__(self, left, order, bufs, sems):
        self.order, self.bufs, self.sems = order, bufs, sems
        self.posts, held = [], list(left)
        for split in order:
            self.posts.append(1 << (len(held) - 1 - held.index(split)))
            held.remove(split)

    def parts(self, stage):
        axis, bit = self.order[stage]
        me = lax.axis_index(axis)
        mine = (me // (1 << bit)) % 2
        return {axis: me + (1 << bit) * (1 - 2 * mine)}, mine

    def half(self, stage, which):
        ref, post = self.bufs[stage], self.posts[stage]
        return ref.reshape(ref.shape[0] // (2 * post), 2, post, *ref.shape[1:]), which

    def copy(self, stage):
        partner, mine = self.parts(stage)
        into = self.bufs[stage + 1]
        view, which = self.half(stage, 1 - mine)
        return pltpu.make_async_remote_copy(
            src_ref=view.at[:, which],
            dst_ref=into.reshape(into.shape[0] // self.posts[stage], self.posts[stage], *into.shape[1:]),
            send_sem=self.sems.at[0, stage],
            recv_sem=self.sems.at[1, stage],
            device_id=partner,
            device_id_type=MESH,
        )

    def start(self, stage=0):
        self.copy(stage).start()

    def turn(self, stage):
        self.copy(stage).wait()
        _, mine = self.parts(stage)
        into, ref, post = self.bufs[stage + 1], self.bufs[stage], self.posts[stage]

        def one(i, carry):
            into[i] = into[i] + ref[((i // post) * 2 + mine) * post + i % post]
            return carry

        lax.fori_loop(0, into.shape[0], one, 0)
        if stage + 1 < len(self.order):
            self.start(stage + 1)


def columns(axis_sum):
    return jnp.sum(axis_sum.reshape(-1, 8, axis_sum.shape[-1]), axis=0)


def norm_back(value, grad, gain, base, write, vec, row):
    rows, width = grad.shape
    step = min(64, rows)

    def chunk(i, sums):
        at = pl.ds(pl.multiple_of(i * step, step), step)
        centred = value[at, :].astype(jnp.float32)
        centred = centred - jnp.mean(centred, axis=-1, keepdims=True)
        scale = lax.rsqrt(jnp.mean(centred * centred, axis=-1, keepdims=True) + 1e-05)
        unit = centred * scale
        error = grad[at, :]
        term = error * gain
        back = scale * (term - jnp.mean(term, axis=-1, keepdims=True) - unit * jnp.mean(term * unit, axis=-1, keepdims=True))
        write(at, base[at, :].astype(jnp.float32) + back)
        return sums[0] + columns(error * unit), sums[1] + columns(error)

    zero = jnp.zeros((8, width), jnp.float32)
    gain_sum, shift_sum = lax.fori_loop(0, rows // step, chunk, (zero, zero))
    vec[row : row + 1, :] = jnp.sum(gain_sum, axis=0, keepdims=True)
    vec[row + 1 : row + 2, :] = jnp.sum(shift_sum, axis=0, keepdims=True)


def tail_kernel(names, clip_stages, blk_stages, *refs):
    r = SimpleNamespace(**dict(zip(names, refs)))
    rest = list(refs[len(names) :])
    stages = clip_stages + blk_stages - 1
    r.wide, rest = rest[:stages], rest[stages:]
    r.tall, rest = rest[:stages], rest[stages:]
    r.kv, rest = rest[:blk_stages], rest[blk_stages:]
    r.head_w, r.text_w = rest[:clip_stages], rest[clip_stages:]
    clips, blks = lax.axis_size("clip"), lax.axis_size("blk")
    me, clip = lax.axis_index("blk"), lax.axis_index("clip")
    core = me % 2
    pair = {"blk": me + 1 - 2 * core}
    devices = clips * blks
    rows, depth = r.frames.shape
    half = depth // 2
    width = depth // blks
    heads = width // HEAD
    tokens = r.text.shape[0]
    chunk = r.first.shape[-1]
    chunks = r.hidden_in.shape[1] // chunk
    bf16, f32 = jnp.bfloat16, jnp.float32
    hidden_tokens = token_bias(r.lengths, tokens)
    vec = r.vec

    barrier = pltpu.get_barrier_semaphore()
    for step in range(1, clips):
        pl.semaphore_signal(barrier, inc=1, device_id={"clip": (clip + step) % clips}, device_id_type=MESH)
    greet("blk", clips - 1)

    sem_at = [0]

    def sem():
        sem_at[0] += 1
        return r.sems.at[sem_at[0] - 1]

    def local(source, target):
        return pltpu.make_async_copy(source, target, sem())

    def remote(source, target, where):
        return pltpu.make_async_remote_copy(
            src_ref=source, dst_ref=target, send_sem=sem(), recv_sem=sem(), device_id=where, device_id_type=MESH
        )

    own, other = pl.ds(0, rows), pl.ds(rows, rows)
    my_half = pl.ds(pl.multiple_of(core * half, half), half)
    its_half = pl.ds(pl.multiple_of((1 - core) * half, half), half)


    def hidden_loads(j):
        at = pl.ds(j * chunk, chunk)
        return (
            local(r.hidden_in.at[:, at], r.first.at[j % 2]),
            local(r.hidden_out.at[at, :], r.second.at[j % 2]),
        )

    act_here = local(r.act_three, r.cat_three.at[own])
    grad_here = local(r.cotangent, r.dy)
    act_here.start()
    grad_here.start()
    weights = {j: hidden_loads(j) for j in range(min(2, chunks))}
    for copies in weights.values():
        for copy in copies:
            copy.start()
    exchanged = {}
    three, mixed, two, att, grads = range(5)
    for name, (source, cat) in enumerate(((r.act_three, r.cat_three), (r.mixed, r.cat_mixed), (r.act_two, r.cat_two), (r.att, r.cat_att))):
        exchanged[name] = [remote(source, cat.at[other], pair)]
        if name != three:
            exchanged[name].append(local(source, cat.at[own]))
    exchanged[grads] = [
        remote(r.cotangent.at[:, its_half], r.cat_dy.at[other], pair),
        local(r.cotangent.at[:, my_half], r.cat_dy.at[own]),
    ]
    for name in (three, grads, mixed, two, att):
        for copy in exchanged[name]:
            copy.start()
    small = [
        local(source, into)
        for source, into in ((r.after_cross, r.value), (r.text_keys, r.tk), (r.text_values, r.tv), (r.cross_queries, r.cq))
    ]
    for copy in small:
        copy.start()
    act_here.wait()
    grad_here.wait()

    clip_bits = [("clip", k) for k in range(bits_of(clips))]
    blk_bits = [("blk", k) for k in range(bits_of(blks))]
    left = clip_bits[::-1] + blk_bits[::-1]
    orders = [clip_bits + blk_bits[1:], clip_bits[::-1] + blk_bits[1:]]
    early = [blk_bits[1:] + clip_bits, blk_bits[1:] + clip_bits[::-1]]
    pieces = []
    for p in range(2 * chunks + 3):
        wide = p < chunks or p >= 2 * chunks
        held = [r.wide_own, *r.wide] if wide else [r.tall_own, *r.tall]
        nth = (p if p < chunks else p - chunks) if wide else p - chunks
        order = early[EARLY.index(p) % 2] if p in EARLY else orders[(p - sum(q < p for q in EARLY)) % 2]
        pieces.append(
            Halving(left, order, [held[0].at[nth % chunks]] + [level.at[nth] for level in held[1:]], r.piece_sems.at[p])
        )

    def finish(p, out, column, rows_out):
        piece = pieces[p]
        size = piece.bufs[-1].shape[-1]
        base = core * half + column if p >= chunks and p < 2 * chunks else column + core * half
        at = pl.ds(pl.multiple_of(base, size), size)
        tall_piece = chunks <= p < 2 * chunks
        stage = r.tall_fix.at[p - chunks] if tall_piece else r.wide_fix.at[p if p < chunks else p - chunks]
        stage[...] = piece.bufs[-1][1 - core].astype(f32)
        copy = remote(stage, out.at[:, at], pair)
        copy.start()
        out[:, at] = piece.bufs[-1][core].astype(f32)
        return copy

    fixes = []

    def task(stage, p):
        if stage < stages:
            pieces[p].turn(stage)
        if stage == stages - 1:
            if p < chunks:
                fixes.append((p, finish(p, r.hidden_in_out, p * chunk, None)))
            elif p < 2 * chunks:
                fixes.append((p, finish(p, r.hidden_out_out, (p - chunks) * (half // chunks), None)))
            else:
                fixes.append((p, finish(p, (r.cross_out_out, r.cross_query_out, r.self_out_out)[p - 2 * chunks], 0, None)))

    total = len(pieces)
    at_point, reached = [0], [-2] * total

    def reach(stage, p):
        while reached[p] < stage:
            reached[p] += 1
            if reached[p] < 0:
                pieces[p].start()
            else:
                task(reached[p], p)

    def point():
        if at_point[0] < len(PLAN):
            for stage, p in PLAN[at_point[0]]:
                if p < total:
                    reach(stage, p)
        at_point[0] += 1

    def outer(cat_left, cat_right, into):
        entries, block = into.shape[:2]
        group = max(1, 256 // block)

        def part(m, carry):
            at = pl.ds(pl.multiple_of(m * group * block, group * block), group * block)
            made = matmul(cat_left[:, at], cat_right[...], (0, 0))
            into[pl.ds(m * group, group)] = made.reshape(group, block, made.shape[-1]).astype(bf16)
            return carry

        lax.fori_loop(0, entries // group, part, 0)

    swaps = {}
    sub = min(256, chunk)
    for j in range(chunks):
        for copy in weights[j]:
            copy.wait()
        first, second = r.first.at[j % 2], r.second.at[j % 2]
        pre_low = r.pre_low.at[j % 2]
        hidden = r.cat_hidden.at[own, pl.ds(j * chunk, chunk)]
        if j >= 2:
            swaps[j - 2][0].wait_send()

        def part(u, carry):
            at = pl.ds(pl.multiple_of(u * sub, sub), sub)
            pre = matmul(r.cat_three[own, :], first[:, at])
            grad = matmul(r.dy[...], second[at, :], (1, 1))
            phi = 0.5 * (1.0 + lax.erf(pre * math.sqrt(0.5)))
            slope = phi + pre * (jnp.exp(-0.5 * pre * pre) * (1.0 / math.sqrt(2.0 * math.pi)))
            hidden[:, at] = (pre * phi).astype(bf16)
            pre_low[:, at] = (grad * slope).astype(bf16)
            return carry

        lax.fori_loop(0, chunk // sub, part, 0)
        swaps[j] = (
            remote(pre_low.at[:, pl.ds(pl.multiple_of((1 - core) * (chunk // 2), chunk // 2), chunk // 2)], r.cat_pre.at[j, other], pair),
            remote(hidden, r.cat_hidden.at[other, pl.ds(j * chunk, chunk)], pair),
        )
        for copy in swaps[j]:
            copy.start()
        r.cat_pre[j, own, :] = pre_low[:, pl.ds(pl.multiple_of(core * (chunk // 2), chunk // 2), chunk // 2)]
        made = matmul(hidden[...], second[...])
        back = matmul(pre_low[...], first[...], (1, 1))
        if j == 0:
            r.total[...] = made
            r.grad[...] = back
        else:
            r.total[...] += made
            r.grad[...] += back
        if j + 2 < chunks:
            weights[j + 2] = hidden_loads(j + 2)
            for copy in weights[j + 2]:
                copy.start()
        point()
        if j == 0:
            for copy in exchanged[three]:
                copy.wait()
        else:
            swaps[j - 1][0].wait_recv()
            outer(r.cat_three, r.cat_pre.at[j - 1], pieces[j - 1].bufs[0])
            point()
    for j in (chunks - 2, chunks - 1):
        swaps[j][0].wait_send()
    later = [
        local(source, into.at[slot])
        for source, into, slot in ((r.cross_out, r.first, 0), (r.cross_query, r.second, 0), (r.self_out, r.first, 1))
    ]
    for copy in later:
        copy.start()
    swaps[chunks - 1][0].wait_recv()
    outer(r.cat_three, r.cat_pre.at[chunks - 1], pieces[chunks - 1].bufs[0])
    point()
    for copy in small:
        copy.wait()
    r.mixed_grad[...] = (r.value[...] + r.total[...]).astype(bf16)
    output_copy = local(r.mixed_grad, r.output)
    output_copy.start()
    for copy in exchanged[grads]:
        copy.wait()
    for j in range(chunks):
        swaps[j][1].wait()
    tall = half // chunks
    block = r.tall_own.shape[2]
    group = max(1, 512 // block)

    def tall_part(m, carry):
        at = pl.ds(pl.multiple_of(m * group * block, group * block), group * block)
        made = matmul(r.cat_hidden[:, at], r.cat_dy[...], (0, 0))
        for w in range(chunks):
            r.tall_own[w, pl.ds(m * group, group)] = made[:, w * tall : (w + 1) * tall].reshape(group, block, tall).astype(bf16)
        return carry

    turns = devices // group
    lax.fori_loop(0, turns // 2, tall_part, 0)
    point()
    lax.fori_loop(turns // 2, turns, tall_part, 0)
    point()

    def keep_two(at, value):
        r.total[at, :] = value
        r.low[0, at, :] = value.astype(bf16)

    norm_back(r.value, r.grad, r.gain_2[...], r.dy, keep_two, vec, 4)
    second_value = local(r.after_self, r.value)
    second_value.start()

    def share(which):
        copy = remote(r.low.at[which, :, its_half], r.cat_low.at[which, other], pair)
        copy.start()
        r.cat_low[which, own, :] = r.low[which, :, my_half]
        return copy

    shared = [share(0)]
    later[0].wait()
    output_copy.wait()
    r.mixed_grad[...] = matmul(r.low[0], r.first[0], (1, 1)).astype(bf16)
    point()
    lanes = min(128, depth)
    groups = lanes // width

    def cross(t, carry):
        at = pl.ds(pl.multiple_of(t * lanes, lanes), lanes)
        queries, keys, values, grads = r.cq[:, at], r.tk[:, at], r.tv[:, at], r.mixed_grad[:, at]
        query_sum = jnp.zeros((rows, lanes), f32)
        key_sum, value_sum = jnp.zeros((tokens, lanes), f32), jnp.zeros((tokens, lanes), f32)
        for h in range(lanes // HEAD):
            query_h, grad_h, key_h = head_only(queries, h), head_only(grads, h), head_only(keys, h)
            scores = matmul(keys, query_h, (1, 1)) * 0.125 + hidden_tokens
            scores = jnp.exp(scores - jnp.max(scores, axis=0, keepdims=True))
            prob = scores / jnp.sum(scores, axis=0, keepdims=True)
            dprob = matmul(values, grad_h, (1, 1))
            dscore = (prob * (dprob - jnp.sum(prob * dprob, axis=0, keepdims=True))).astype(bf16)
            query_sum = query_sum + matmul(dscore, key_h, (0, 0))
            key_sum = key_sum + matmul(dscore, query_h)
            value_sum = value_sum + matmul(prob.astype(bf16), grad_h)
        r.low[1, :, at] = (query_sum * 0.125).astype(bf16)
        for g in range(groups):
            r.kv_own[t * groups + g, :, :width] = (key_sum[:, g * width : (g + 1) * width] * 0.125).astype(bf16)
            r.kv_own[t * groups + g, :, width:] = value_sum[:, g * width : (g + 1) * width].astype(bf16)
        return carry

    turns = depth // lanes
    for quarter in range(4):
        lax.fori_loop(turns * quarter // 4, turns * (quarter + 1) // 4, cross, 0)
        point()
    text_load = local(r.text, r.tk)
    text_load.start()
    text_sum = Halving(blk_bits[::-1], blk_bits, [r.kv_own, *r.kv], r.kv_sems)
    text_sum.start()
    shared.append(share(1))
    point()
    later[1].wait()
    r.grad[...] = matmul(r.low[1], r.second[0], (1, 1))
    second_value.wait()
    shared[0].wait_send()

    def keep_one(at, value):
        r.total[at, :] = value
        r.low[0, at, :] = value.astype(bf16)

    norm_back(r.value, r.grad, r.gain_1[...], r.total, keep_one, vec, 2)
    point()
    for copy in (share_one := [remote(r.low.at[0, :, its_half], r.cat_low.at[2, other], pair)]):
        copy.start()
    r.cat_low[2, own, :] = r.low[0, :, my_half]
    later[2].wait()
    att_grad = matmul(r.low[0], r.first[1], (1, 1)).astype(bf16)
    for s in range(blks):
        r.grad_own[s] = att_grad[:, s * width : (s + 1) * width]

    block_sems = r.block_sems

    def fetch(peer, source):
        return pltpu.make_async_remote_copy(
            src_ref=r.grad_own.at[peer], dst_ref=r.grad_all.at[source], send_sem=block_sems.at[0, peer],
            recv_sem=block_sems.at[1, source], device_id={"blk": peer}, device_id_type=MESH,
        )

    def give(peer, source):
        return pltpu.make_async_remote_copy(
            src_ref=r.qkv_here.at[peer], dst_ref=r.sums_in.at[source], send_sem=block_sems.at[2, peer],
            recv_sem=block_sems.at[3, source], device_id={"blk": peer}, device_id_type=MESH,
        )

    for step in range(1, blks):
        fetch((me + step) % blks, me).start()
    r.grad_all[me] = r.grad_own[me]
    attention_inputs = [local(source, into) for source, into in ((r.qkv, r.qkv_here), (r.full, r.full_here), (r.lse, r.lse_rows))]
    for copy in attention_inputs:
        copy.start()
    projections = [
        local(source, into.at[slot])
        for source, into, slot in ((r.self_query, r.first, 0), (r.self_key, r.second, 0), (r.self_value, r.second, 1))
    ]
    text_weight = local(r.cross_key, r.first.at[1])
    for copy in (*projections, text_weight):
        copy.start()
    point()
    text_sum.turn(0)

    def last_pieces():
        for n, (name, cat, wait) in enumerate(((mixed, r.cat_mixed, shared[0]), (two, r.cat_two, shared[1]), (att, r.cat_att, share_one[0]))):
            for copy in exchanged[name]:
                copy.wait()
            wait.wait_recv() if n == 0 else wait.wait()
            if n < chunks:
                reach(0, n)
            outer(cat, r.cat_low.at[n], pieces[2 * chunks + n].bufs[0])
            point()

    last_pieces()
    text_done = text_sum.bufs[-1].at[0]
    text_rows = tokens // blks

    def swap_text(peer, source):
        return pltpu.make_async_remote_copy(
            src_ref=text_done.at[pl.ds(pl.multiple_of(peer * text_rows, text_rows), text_rows)], dst_ref=r.text_in.at[source],
            send_sem=block_sems.at[4, peer], recv_sem=block_sems.at[5, source], device_id={"blk": peer}, device_id_type=MESH,
        )

    clip_left = clip_bits[::-1] + blk_bits[::-1]
    text_w = Halving(clip_left, clip_bits[::-1], [r.text_w_own, *r.text_w], r.clip_sems.at[0])
    head_w = Halving(clip_left, clip_bits, [r.head_w_own, *r.head_w], r.clip_sems.at[1])

    def text_back(part):
        for s in range(blks):
            r.text_cat[:, s * width : (s + 1) * width] = r.text_in[s, :, part * width : (part + 1) * width]
        return matmul(r.text_cat[...], r.first[1], (1, 1))

    def text_ready():
        for step in range(1, blks):
            swap_text((me + step) % blks, me).start()
        r.text_in[me] = text_done[pl.ds(pl.multiple_of(me * text_rows, text_rows), text_rows), :]
        text_load.wait()
        outer(r.tk, text_done, r.text_w_own)
        text_w.start()

    for copy in attention_inputs:
        copy.wait()
    qkv, full = r.qkv_here, r.full_here
    for step in range(1, blks):
        fetch((me + step) % blks, (me + step) % blks).wait_recv()
    text_sum.turn(1)
    point()
    for i in range(blks):
        product = (r.grad_all[i].astype(f32) * full[i]).T
        for h in range(heads):
            r.delta_rows[i, h : h + 1, :] = jnp.sum(product[h * HEAD : (h + 1) * HEAD], axis=0, keepdims=True)

    full[...] = jnp.zeros_like(full)
    point()
    mask = causal(rows, True)

    def act_load(j):
        return pltpu.make_async_copy(r.act_all.at[j], r.low.at[j % 2], block_sems.at[6, j])

    act_load(0).start()
    act_load(1).start()

    def key_block(j):
        keys = qkv[j, :, width : 2 * width]
        values = qkv[j, :, 2 * width :]

        def update(i, state, masked):
            key_sum, value_sum = state
            queries = qkv[i, :, :width]
            grad = r.grad_all[i]
            summed = None
            for h in range(heads):
                query_h, grad_h, key_h = head_only(queries, h), head_only(grad, h), head_only(keys, h)
                scores = matmul(keys, query_h, (1, 1))
                probs = jnp.exp(scores - r.lse_rows[i, h : h + 1, :])
                if masked:
                    probs = jnp.where(mask, probs, 0.0)
                dprobs = matmul(values, grad_h, (1, 1))
                dscores = (probs * (dprobs - r.delta_rows[i, h : h + 1, :])).astype(bf16)
                value_sum = value_sum + matmul(probs.astype(bf16), grad_h)
                key_sum = key_sum + matmul(dscores, query_h)
                term = matmul(dscores, key_h, (0, 0))
                summed = term if summed is None else summed + term
            full[i] += summed
            return key_sum, value_sum

        zero = jnp.zeros((rows, width), f32)
        state = update(j, (zero, zero), True)
        if j + 1 < blks:
            state = lax.fori_loop(j + 1, blks, lambda i, held: update(i, held, False), state)
        r.qkv_here[j, :, :width] = (full[j] * 0.125).astype(bf16)
        r.qkv_here[j, :, width : 2 * width] = state[0].astype(bf16)
        r.qkv_here[j, :, 2 * width :] = state[1].astype(bf16)

        @pl.when(j != me)
        def _():
            give(j, me).start()

        act_load(j).wait()
        made = matmul(r.low[j % 2], r.qkv_here[j], (0, 0))
        if j == 0:
            r.head_sum[...] = made
        else:
            r.head_sum[...] += made
        if j + 2 < blks:
            act_load(j + 2).start()

    for j in range(blks):
        key_block(j)
        if j == 1:
            for stage in range(2, len(blk_bits)):
                text_sum.turn(stage)
            text_ready()
        if j == 4:
            text_w.turn(0)
        if j == 5:
            for step in range(1, blks):
                swap_text((me + step) % blks, (me + step) % blks).wait_recv()
            text_weight.wait()
            r.text_grad[...] = text_back(0)
            text_weight = local(r.cross_value, r.first.at[1])
            text_weight.start()
        point()
    for stage in range(1, len(clip_bits)):
        text_w.turn(stage)
    r.sums_in[me] = r.qkv_here[me]
    r.head_w_own[...] = r.head_sum[...].reshape(r.head_w_own.shape).astype(bf16)
    head_w.start()

    def swap_w(summed, out, base, peer, source):
        return pltpu.make_async_remote_copy(
            src_ref=summed.bufs[-1].at[peer], dst_ref=out.at[source], send_sem=block_sems.at[base, peer],
            recv_sem=block_sems.at[base + 1, source], device_id={"blk": peer}, device_id_type=MESH,
        )

    for step in range(1, blks):
        swap_w(text_w, r.text_w_out, 7, (me + step) % blks, me).start()
    r.text_w_out[me] = text_w.bufs[-1][me]
    for copy in projections:
        copy.wait()
    first_value = local(r.frames, r.mixed_grad)
    first_value.start()
    for step in range(1, blks):
        give((me + step) % blks, (me + step) % blks).wait_recv()
    grad_rows = [r.low.at[0], r.low.at[1], r.cq]
    for s in range(blks):
        for t in range(3):
            grad_rows[t][:, s * width : (s + 1) * width] = r.sums_in[s, :, t * width : (t + 1) * width]
    point()
    head_w.turn(0)
    r.grad[...] = matmul(grad_rows[0][...], r.first[0], (1, 1))
    r.grad[...] += matmul(grad_rows[1][...], r.second[0], (1, 1))
    r.grad[...] += matmul(grad_rows[2][...], r.second[1], (1, 1))
    first_value.wait()
    text_weight.wait()
    r.text_grad[...] += text_back(1)
    point()

    def keep_frames(at, value):
        r.value[at, :] = value

    norm_back(r.mixed_grad, r.grad, r.gain_0[...], r.total, keep_frames, vec, 0)
    frames_copy = local(r.value, r.frames_grad)
    frames_copy.start()
    vec[6:8, :] = jnp.zeros((2, depth), f32)
    part = depth // clips

    def swap_vec(peer, source):
        return pltpu.make_async_remote_copy(
            src_ref=vec.at[:, pl.ds(pl.multiple_of(peer * part, part), part)], dst_ref=r.vec_in.at[source],
            send_sem=r.vec_sems.at[0, peer], recv_sem=r.vec_sems.at[1, source], device_id={"clip": peer}, device_id_type=MESH,
        )

    for step in range(1, clips):
        swap_vec((clip + step) % clips, clip).start()
    r.vec_in[clip] = vec[:, pl.ds(pl.multiple_of(clip * part, part), part)]
    for stage in range(1, len(clip_bits)):
        head_w.turn(stage)
    for step in range(1, blks):
        swap_w(head_w, r.head_w_out, 9, (me + step) % blks, me).start()
    r.head_w_out[me] = head_w.bufs[-1][me]
    point()
    for step in range(1, clips):
        swap_vec((clip + step) % clips, (clip + step) % clips).wait_recv()
    r.vec_sum[me] = jnp.sum(r.vec_in[...], axis=0)

    def share_vec(peer, source):
        return pltpu.make_async_remote_copy(
            src_ref=r.vec_sum.at[me], dst_ref=r.vec_sum.at[source], send_sem=block_sems.at[11, peer],
            recv_sem=block_sems.at[12, source], device_id={"blk": peer}, device_id_type=MESH,
        )

    for step in range(1, blks):
        share_vec((me + step) % blks, me).start()
    for k in range(total + 2 * stages):
        for stage in range(stages):
            if 0 <= k - 2 * stage < total:
                reach(stage, k - 2 * stage)
    for step in range(1, blks):
        share_vec((me + step) % blks, (me + step) % blks).wait_recv()
    summed = jnp.sum(r.vec_sum[...], axis=0)
    share_own = depth // devices
    turned = pltpu.roll(summed, (summed.shape[-1] - me * share_own) % summed.shape[-1], 1)
    for n, out in enumerate((r.vec_0, r.vec_1, r.vec_2, r.vec_3, r.vec_4, r.vec_5)):
        out[...] = turned[n : n + 1, :share_own]
    for _, copy in fixes:
        copy.wait()
    frames_copy.wait()
    for step in range(1, clips):
        swap_vec((clip + step) % clips, clip).wait_send()
    for step in range(1, blks):
        peer = (me + step) % blks
        fetch(peer, me).wait_send()
        give(peer, me).wait_send()
        swap_text(peer, me).wait_send()
        for summed, out, base in ((text_w, r.text_w_out, 7), (head_w, r.head_w_out, 9)):
            swap_w(summed, out, base, peer, me).wait_send()
            swap_w(summed, out, base, peer, peer).wait_recv()
        share_vec(peer, me).wait_send()
    for parts, outs in ((r.head_w_out, (r.query_w, r.key_w, r.value_w)), (r.text_w_out, (r.text_key_w, r.text_value_w))):
        for s in range(blks):
            for t, out in enumerate(outs):
                out[:, s * width : (s + 1) * width] = parts[s, :, t * width : (t + 1) * width].astype(f32)


def backward(inputs, gains, lengths, clips, blks):
    rows, depth = inputs["frames"].shape
    tokens = inputs["text"].shape[0]
    hidden = inputs["hidden_in"].shape[1]
    devices, width, half = clips * blks, depth // blks, depth // 2
    chunk = min(1024, hidden)
    chunks = hidden // chunk
    own = depth // devices
    tall = half // chunks
    stages = bits_of(clips) + bits_of(blks) - 1
    bf16, f32 = jnp.bfloat16, jnp.float32
    hbm, vmem = pl.BlockSpec(memory_space=pltpu.MemorySpace.HBM), pl.BlockSpec(memory_space=pltpu.VMEM)
    dma = pltpu.SemaphoreType.DMA
    shape = jax.ShapeDtypeStruct
    row = shape((own, depth), f32)
    outs = dict(
        output=shape((rows, depth), bf16), frames_grad=shape((rows, depth), f32), text_grad=shape((tokens // blks, depth), f32),
        query_w=row, key_w=row, value_w=row, self_out_out=row, cross_query_out=row, text_key_w=row, text_value_w=row, cross_out_out=row,
        hidden_in_out=shape((own, hidden), f32), hidden_out_out=shape((hidden // devices, depth), f32),
        **{f"vec_{n}": shape((1, own), f32) for n in range(6)},
    )
    scratch = dict(
        first=((2, depth, chunk), bf16), second=((2, chunk, depth), bf16),
        cat_three=((2 * rows, depth), bf16), cat_mixed=((2 * rows, depth), bf16), cat_two=((2 * rows, depth), bf16),
        cat_att=((2 * rows, depth), bf16), cat_dy=((2 * rows, half), bf16), dy=((rows, depth), bf16),
        cat_hidden=((2 * rows, hidden), bf16), pre_low=((2, rows, chunk), bf16), cat_pre=((chunks, 2 * rows, chunk // 2), bf16),
        total=((rows, depth), f32), grad=((rows, depth), f32), value=((rows, depth), f32),
        low=((2, rows, depth), bf16), cat_low=((3, 2 * rows, half), bf16), mixed_grad=((rows, depth), bf16),
        cq=((rows, depth), bf16), tk=((tokens, depth), bf16), tv=((tokens, depth), bf16),
        vec=((8, depth), f32), vec_in=((clips, 8, depth // clips), f32), vec_sum=((blks, 8, depth // clips), f32),
        wide_own=((chunks, devices, own, half), bf16), tall_own=((chunks, devices, hidden // devices, tall), bf16),
        wide_fix=((chunks + 3, own, half), f32), tall_fix=((chunks, hidden // devices, tall), f32),
        text_in=((blks, tokens // blks, 2 * width), bf16), text_cat=((tokens // blks, depth), bf16),
        head_w_out=((blks, own, 3 * width), bf16), text_w_out=((blks, own, 2 * width), bf16),
        kv_own=((blks, tokens, 2 * width), bf16),
        head_w_own=((devices, own, 3 * width), bf16), text_w_own=((devices, own, 2 * width), bf16),
        grad_own=((blks, rows, width), bf16), grad_all=((blks, rows, width), bf16), sums_in=((blks, rows, 3 * width), bf16), qkv_here=((blks, rows, 3 * width), bf16), full_here=((blks, rows, width), f32),
        lse_rows=((blks, 8, rows), f32), delta_rows=((blks, 8, rows), f32),
        head_sum=((depth, 3 * width), f32),
    )
    levels = [((chunks + 3, devices >> (s + 1), own, half), bf16) for s in range(stages)]
    levels += [((chunks, devices >> (s + 1), hidden // devices, tall), bf16) for s in range(stages)]
    levels += [((blks >> (s + 1), tokens, 2 * width), bf16) for s in range(bits_of(blks))]
    for parts in (3, 2):
        levels += [((devices >> (s + 1), own, parts * width), bf16) for s in range(bits_of(clips))]
    sems = dict(
        sems=(160,), piece_sems=(2 * chunks + 3, 2, stages), kv_sems=(2, bits_of(blks)), block_sems=(13, blks),
        clip_sems=(2, 2, bits_of(clips)), vec_sems=(2, clips),
    )
    small = dict(lengths=lengths, gain_0=gains[0], gain_1=gains[1], gain_2=gains[2])
    names = [*inputs, *small, *outs, *scratch, *sems]
    made = pl.pallas_call(
        partial(tail_kernel, names, bits_of(clips), bits_of(blks)),
        out_shape=list(outs.values()),
        in_specs=[hbm] * len(inputs) + [pl.BlockSpec(memory_space=pltpu.SMEM)] + [vmem] * 3,
        out_specs=[hbm if i < 2 else vmem for i in range(len(outs))],
        scratch_shapes=[pltpu.VMEM(*v) for v in scratch.values()] + [dma(v) for v in sems.values()] + [pltpu.VMEM(*v) for v in levels],
        compiler_params=pltpu.CompilerParams(collective_id=3, has_side_effects=True, vmem_limit_bytes=63 << 20),
    )(*inputs.values(), *small.values())
    return SimpleNamespace(**dict(zip(outs, made)))


def collect_kernel(*refs):
    count = len(refs) // 2
    for n in range(count):
        refs[count + n][...] = refs[n][...]


def collect(*arrays):
    vmem = pl.BlockSpec(memory_space=pltpu.VMEM)
    return pl.pallas_call(
        collect_kernel,
        out_shape=[jax.ShapeDtypeStruct(a.shape, a.dtype) for a in arrays],
        in_specs=[vmem] * len(arrays),
        out_specs=[vmem] * len(arrays),
        compiler_params=pltpu.CompilerParams(vmem_limit_bytes=32 << 20),
    )(*arrays)


def body(
    frames,
    text_states,
    prompt_lengths,
    cotangent,
    self_query,
    self_key,
    self_value,
    self_out,
    cross_query,
    cross_key,
    cross_value,
    cross_out,
    hidden_in,
    hidden_out,
    first_gain,
    first_shift,
    second_gain,
    second_shift,
    third_gain,
    third_shift,
):
    block_total, clip_total = lax.axis_size("blk"), lax.axis_size("clip")
    block_rank = lax.axis_index("blk")
    own = D // (clip_total * block_total)
    head_width = D // block_total
    local_text = text_states[0]
    projections = (self_query, self_key, self_value)
    if head_width % 128:
        projections = [lax.dynamic_slice_in_dim(matrix, block_rank * head_width, head_width, 1) for matrix in projections]
    norms = [v.reshape(1, D) for v in (first_gain, second_gain, third_gain, first_shift, second_shift, third_shift)]
    weights = dict(
        text=local_text, cross_key=cross_key, cross_value=cross_value, self_out=self_out, cross_query=cross_query, cross_out=cross_out
    )
    kept = forward(frames[0], projections, norms, prompt_lengths, weights, block_total)
    inputs = dict(
        act_three=kept.act_three, cotangent=cotangent[0], hidden_in=hidden_in, hidden_out=hidden_out, mixed=kept.mixed, act_two=kept.act_two,
        att=kept.att, after_cross=kept.after_cross, after_self=kept.after_self, frames=frames[0], text=local_text, text_keys=kept.tk,
        text_values=kept.tv, cross_queries=kept.cross_queries, cross_out=cross_out, cross_query=cross_query, self_out=self_out,
        self_query=self_query, self_key=self_key, self_value=self_value, qkv=kept.qkv, full=kept.full, lse=kept.lse, act_all=kept.act_all,
        cross_key=cross_key, cross_value=cross_value,
    )
    made = backward(inputs, norms[:3], prompt_lengths, clip_total, block_total)
    frames_grad, text_grad = made.frames_grad[None], made.text_grad[None]
    sums = [
        made.query_w, made.key_w, made.value_w, made.self_out_out, made.cross_query_out, made.text_key_w, made.text_value_w,
        made.cross_out_out, made.hidden_in_out, made.hidden_out_out,
    ]
    vectors = [v.reshape(own) for v in (made.vec_0, made.vec_1, made.vec_2, made.vec_3, made.vec_4, made.vec_5)]
    return (*collect(made.output[None], frames_grad, text_grad, *sums, *vectors),)


def solution(mesh):
    in_specs = (
        P("clip", "blk", None),
        P("clip", None, None),
        P("clip"),
        P("clip", "blk", None),
        P(),
        P(),
        P(),
        P(),
        P(),
        P(),
        P(),
        P(),
        P(),
        P(),
        P(),
        P(),
        P(),
        P(),
        P(),
        P(),
    )
    out_specs = (
        P("clip", "blk", None),
        P("clip", "blk", None),
        P("clip", "blk", None),
        P(("clip", "blk"), None),
        P(("clip", "blk"), None),
        P(("clip", "blk"), None),
        P(("clip", "blk"), None),
        P(("clip", "blk"), None),
        P(("clip", "blk"), None),
        P(("clip", "blk"), None),
        P(("clip", "blk"), None),
        P(("clip", "blk"), None),
        P(("clip", "blk"), None),
        P(("clip", "blk")),
        P(("clip", "blk")),
        P(("clip", "blk")),
        P(("clip", "blk")),
        P(("clip", "blk")),
        P(("clip", "blk")),
    )
    return jax.shard_map(body, mesh=mesh, in_specs=in_specs, out_specs=out_specs, check_vma=False)
```

```python
from functools import partial
import math
from types import SimpleNamespace

import jax
import jax.numpy as jnp
from jax import lax
from jax.experimental import pallas as pl
from jax.experimental.pallas import tpu as pltpu
from jax.sharding import PartitionSpec as P

D = 1024
HEADS = 16
HEAD = 64
TEXT = 256
MESH = pl.DeviceIdType.MESH


def normed(block, gain, shift):
    values = block.astype(jnp.float32)
    centred = values - jnp.mean(values, axis=-1, keepdims=True)
    variance = jnp.mean(centred * centred, axis=-1, keepdims=True)
    return centred * lax.rsqrt(variance + 1e-05) * gain + shift


def matmul(left, right, over=(1, 0)):
    return lax.dot_general(left, right, (((over[0],), (over[1],)), ((), ())), preferred_element_type=jnp.float32)


def greet(axis, others):
    me, size = lax.axis_index(axis), lax.axis_size(axis)
    barrier = pltpu.get_barrier_semaphore()
    for step in range(1, size):
        pl.semaphore_signal(barrier, inc=1, device_id={axis: (me + step) % size}, device_id_type=MESH)
    pl.semaphore_wait(barrier, size - 1 + others)


def head_only(block, head):
    lanes = block.shape[-1]
    if lanes == HEAD:
        return block
    lane = lax.broadcasted_iota(jnp.int32, block.shape, 1)
    return jnp.where((lane // HEAD) == head, block, jnp.zeros_like(block))


def causal(rows, transposed):
    row = lax.broadcasted_iota(jnp.int32, (rows, rows), 0)
    column = lax.broadcasted_iota(jnp.int32, (rows, rows), 1)
    return (row <= column) if transposed else (column <= row)


def token_bias(lengths, tokens):
    token = lax.broadcasted_iota(jnp.int32, (tokens, 1), 0)
    return jnp.where(token < lengths[0], 0.0, -1e30)


def forward_kernel(names, *refs):
    r = SimpleNamespace(**dict(zip(names, refs)))
    blks = lax.axis_size("blk")
    chips = blks // 2
    me = lax.axis_index("blk")
    chip, core = me // 2, me % 2
    rows, width = r.low.shape[1:]
    depth = r.frames_here.shape[1]
    heads = width // HEAD
    bf16, f32 = jnp.bfloat16, jnp.float32
    gathered, qkv = r.gathered, r.qkv
    sem_at = [0]

    def local(source, target):
        sem_at[0] += 1
        return pltpu.make_async_copy(source, target, r.sems.at[sem_at[0] - 1])

    slices = []
    for n, source in enumerate((r.projection_0, r.projection_1, r.projection_2)):
        if source.shape[1] > width:
            source = source.at[:, pl.ds(pl.multiple_of(me * width, width), width)]
        slices.append(local(source, r.weight.at[n]))
    loads = [
        local(source, target)
        for source, target in (
            (r.text, r.text_here), (r.cross_key, r.key_here), (r.cross_value, r.value_here), (r.self_out, r.self_out_here),
            (r.cross_query, r.cross_query_here), (r.cross_out, r.cross_out_here),
        )
    ]
    for copy in slices:
        copy.start()
    greet("blk", 0)
    gathered[me] = r.frames_here[...]
    for copy in loads:
        copy.start()
    hidden_tokens = token_bias(r.lengths, r.tk.shape[0])

    def ring(slot, way):
        return pltpu.make_async_remote_copy(
            src_ref=gathered.at[slot], dst_ref=gathered.at[slot], send_sem=r.ring_send.at[0 if way > 0 else 1, slot],
            recv_sem=r.ring_recv.at[slot], device_id={"blk": me + 2 * way}, device_id_type=MESH,
        )

    def across(slot):
        return pltpu.make_async_remote_copy(
            src_ref=gathered.at[slot], dst_ref=gathered.at[slot], send_sem=r.core_send.at[slot],
            recv_sem=r.core_recv.at[slot], device_id={"blk": chip * 2 + 1 - core}, device_id_type=MESH,
        )

    def send(block):
        return pltpu.make_async_remote_copy(
            src_ref=r.low.at[block], dst_ref=r.att_parts.at[me], send_sem=r.out_send.at[block],
            recv_sem=r.out_recv.at[me], device_id={"blk": block}, device_id_type=MESH,
        )

    def project_block(slot):
        act = normed(gathered[slot], r.gain_0[...], r.shift_0[...]).astype(bf16)
        r.act_all[slot] = act
        qkv[slot, :, :width] = matmul(act, r.weight[0]).astype(bf16) * jnp.bfloat16(0.125)
        qkv[slot, :, width : 2 * width] = matmul(act, r.weight[1]).astype(bf16)
        values = matmul(act, r.weight[2]).astype(bf16)
        qkv[slot, :, 2 * width :] = values
        r.value_rows[slot] = values.T

    mask = causal(rows, True)
    r.peaks[...] = jnp.full_like(r.peaks, -1e30)
    r.totals[...] = jnp.zeros_like(r.totals)
    r.acc[...] = jnp.zeros_like(r.acc)

    def update(i, j):
        def pair(masked):
            keys, queries = qkv[j, :, width : 2 * width], qkv[i, :, :width]
            for h in range(heads):
                own = pl.ds(h * HEAD, HEAD)
                scores = matmul(keys, head_only(queries, h), (1, 1))
                if masked:
                    scores = jnp.where(mask, scores, -1e30)
                peak = r.peaks[i, h : h + 1, :]
                top = jnp.maximum(peak, jnp.max(scores, axis=0, keepdims=True))
                weights = jnp.exp(scores - top)
                rescale = jnp.exp(peak - top)
                r.peaks[i, h : h + 1, :] = top
                r.totals[i, h : h + 1, :] = r.totals[i, h : h + 1, :] * rescale + jnp.sum(weights, axis=0, keepdims=True)
                r.acc[i, own, :] = r.acc[i, own, :] * rescale + matmul(r.value_rows[j, own, :], weights.astype(bf16))

        pl.when(i == j)(lambda: pair(True))
        pl.when(i != j)(lambda: pair(False))

    def settle(i):
        for h in range(heads):
            own = pl.ds(h * HEAD, HEAD)
            r.acc[i, own, :] = r.acc[i, own, :] / r.totals[i, h : h + 1, :]
            r.lse[i, h : h + 1, :] = r.peaks[i, h : h + 1, :] + jnp.log(r.totals[i, h : h + 1, :])
        full = r.acc[i].T
        r.full[i] = full
        r.low[i] = full.astype(bf16)

        @pl.when(i != me)
        def _():
            send(i).start()

    def lower(first, stop):
        def one(i, carry):
            update(i, first)

            @pl.when(i > first)
            def _():
                update(i, first + 1)

            pl.when(first == 0)(lambda: settle(i))
            return carry

        lax.fori_loop(first, stop, one, 0)

    def upper(first, start):
        def one(i, carry):
            lax.fori_loop(start, i + 1, lambda j, held: (update(i, j), held)[1], 0)
            pl.when(start == 0)(lambda: settle(i))
            return carry

        lax.fori_loop(first, first + 2, one, 0)

    @pl.when(chip + 1 < chips)
    def _():
        ring(me, 1).start()

    @pl.when(chip > 0)
    def _():
        ring(me, -1).start()

    across(me).start()
    for copy in slices:
        copy.wait()
    project_block(me)
    other = chip * 2 + 1 - core
    across(other).wait_recv()
    project_block(other)
    upper(chip * 2, chip * 2)
    for copy in loads[:3]:
        copy.wait()
    r.tk[...] = matmul(r.text_here[...], r.key_here[...]).astype(bf16)
    r.tv[...] = matmul(r.text_here[...], r.value_here[...]).astype(bf16)

    for step in range(1, chips):
        for way in (1, -1):
            source = chip - way * step

            @pl.when((source >= 0) & (source < chips))
            def _():
                slot = source * 2 + core
                ring(slot, way).wait_recv()

                @pl.when((chip + way >= 0) & (chip + way < chips))
                def _():
                    ring(slot, way).start()

                across(slot).start()

        for way in (1, -1):
            source = chip - way * step

            @pl.when((source >= 0) & (source < chips))
            def _():
                project_block(source * 2 + core)
                across(source * 2 + 1 - core).wait_recv()
                project_block(source * 2 + 1 - core)
                if way > 0:
                    lower(source * 2, 2 * jnp.minimum(chip + step, chips))
                else:
                    upper(source * 2, 2 * jnp.maximum(chip - step, 0))

    stores = []

    def store(*pairs):
        for source, target in pairs:
            stores.append(local(source, target))
            stores[-1].start()

    store((r.act_all, r.act_all_out), (qkv, r.qkv_out), (r.full, r.full_out), (r.lse, r.lse_out), (r.tk, r.tk_out), (r.tv, r.tv_out))
    r.att_parts[me] = r.low[me]
    for copy in loads[3:]:
        copy.wait()
    for step in range(1, blks):
        peer = (me + step) % blks
        pltpu.make_async_remote_copy(
            src_ref=r.low.at[peer], dst_ref=r.att_parts.at[peer], send_sem=r.out_send.at[peer],
            recv_sem=r.out_recv.at[peer], device_id={"blk": peer}, device_id_type=MESH,
        ).wait_recv()
    for s in range(blks):
        r.att[:, s * width : (s + 1) * width] = r.att_parts[s]

    r.after_self[...] = r.frames_here[...].astype(f32) + matmul(r.att[...], r.self_out_here[...])
    r.act_two[...] = normed(r.after_self[...], r.gain_1[...], r.shift_1[...]).astype(bf16)
    r.cross_queries[...] = matmul(r.act_two[...], r.cross_query_here[...]).astype(bf16)
    lanes = min(128, depth)

    def cross(t, carry):
        at = pl.ds(pl.multiple_of(t * lanes, lanes), lanes)
        queries, keys, values = r.cross_queries[:, at], r.tk[:, at], r.tv[:, at]
        mixed = jnp.zeros((rows, lanes), f32)
        for h in range(lanes // HEAD):
            scores = matmul(keys, head_only(queries, h), (1, 1)) * 0.125 + hidden_tokens
            scores = jnp.exp(scores - jnp.max(scores, axis=0, keepdims=True))
            prob = scores / jnp.sum(scores, axis=0, keepdims=True)
            mixed = mixed + matmul(prob.astype(bf16), head_only(values, h), (0, 0))
        r.mixed[:, at] = mixed.astype(bf16)
        return carry

    lax.fori_loop(0, depth // lanes, cross, 0)
    store((r.att, r.att_out), (r.after_self, r.after_self_out), (r.act_two, r.act_two_out))
    store((r.cross_queries, r.cross_queries_out), (r.mixed, r.mixed_out))
    r.after_cross[...] = r.after_self[...] + matmul(r.mixed[...], r.cross_out_here[...])
    r.act_three[...] = normed(r.after_cross[...], r.gain_2[...], r.shift_2[...]).astype(bf16)

    store((r.after_cross, r.after_cross_out), (r.act_three, r.act_three_out))
    for step in range(1, blks):
        send((me + step) % blks).wait_send()

    @pl.when(chip + 1 < chips)
    def _():
        ring(me, 1).wait_send()

    @pl.when(chip > 0)
    def _():
        ring(me, -1).wait_send()

    across(me).wait_send()
    for step in range(1, chips):
        for way in (1, -1):
            source = chip - way * step

            @pl.when((source >= 0) & (source < chips))
            def _():
                slot = source * 2 + core

                @pl.when((chip + way >= 0) & (chip + way < chips))
                def _():
                    ring(slot, way).wait_send()

                across(slot).wait_send()

    for copy in stores:
        copy.wait()


def forward(frames, projections, norms, lengths, weights, blks):
    rows, depth = frames.shape
    width = depth // blks
    tokens = weights["text"].shape[0]
    bf16, f32 = jnp.bfloat16, jnp.float32
    hbm, vmem = pl.BlockSpec(memory_space=pltpu.MemorySpace.HBM), pl.BlockSpec(memory_space=pltpu.VMEM)
    dma = pltpu.SemaphoreType.DMA
    shape = jax.ShapeDtypeStruct
    small = dict(frames_here=frames)
    for n in range(3):
        small |= {f"gain_{n}": norms[n], f"shift_{n}": norms[3 + n]}
    weights = weights | {f"projection_{n}": projections[n] for n in range(3)}
    kept = dict(
        act_all=((blks, rows, depth), bf16), qkv=((blks, rows, 3 * width), bf16), full=((blks, rows, width), f32),
        lse=((blks, 8, rows), f32), att=((rows, depth), bf16), after_self=((rows, depth), f32), act_two=((rows, depth), bf16),
        cross_queries=((rows, depth), bf16), tk=((tokens, depth), bf16), tv=((tokens, depth), bf16),
        mixed=((rows, depth), bf16), after_cross=((rows, depth), f32), act_three=((rows, depth), bf16),
    )
    outs = {f"{name}_out": shape(*v) for name, v in kept.items()}
    scratch = dict(
        gathered=((blks, rows, depth), bf16), low=((blks, rows, width), bf16), att_parts=((blks, rows, width), bf16),
        value_rows=((blks, width, rows), bf16), peaks=((blks, 8, rows), f32), totals=((blks, 8, rows), f32), acc=((blks, width, rows), f32),
        text_here=((tokens, depth), bf16), key_here=((depth, depth), bf16), value_here=((depth, depth), bf16),
        self_out_here=((depth, depth), bf16), cross_query_here=((depth, depth), bf16), cross_out_here=((depth, depth), bf16),
        weight=((3, depth, width), bf16), **kept,
    )
    sems = dict(ring_send=(2, blks), ring_recv=(blks,), core_send=(blks,), core_recv=(blks,), out_send=(blks,), out_recv=(blks,), sems=(32,))
    names = ["lengths", *small, *weights, *outs, *scratch, *sems]
    made = pl.pallas_call(
        partial(forward_kernel, names),
        out_shape=list(outs.values()),
        in_specs=[pl.BlockSpec(memory_space=pltpu.SMEM)] + [vmem] * len(small) + [hbm] * len(weights),
        out_specs=[hbm] * len(outs),
        scratch_shapes=[pltpu.VMEM(*v) for v in scratch.values()] + [dma(v) for v in sems.values()],
        compiler_params=pltpu.CompilerParams(collective_id=1, has_side_effects=True, vmem_limit_bytes=60 << 20),
    )(lengths, *small.values(), *weights.values())
    return SimpleNamespace(**dict(zip(kept, made)))


EARLY = (0, 2)
PLAN = ((), (), ((-1, 0), ), (), ((-1, 1), ), (), ((-1, 2), ), ((-1, 3), ), ((0, 0), ), ((-1, 4), (-1, 5), (-1, 6), (-1, 7)), ((0, 1), ), (), (), ((0, 2), (0, 3)), ((1, 0), ), (), ((0, 4), ), (), ((0, 5), (-1, 8)), ((-1, 9), ), (), ((2, 0), (1, 2), (1, 3), (0, 6), (0, 7), (-1, 10)), ((1, 1), ), ((1, 4), (1, 5)), (), ((0, 8), ), ((3, 0), (1, 7), (0, 9), (2, 2)), (), ((1, 6), ), (), ((0, 10), ), ((3, 2), (1, 8), (1, 9), (1, 10)), (), ())


def bits_of(size):
    return size.bit_length() - 1


class Halving:
    def __init__(self, left, order, bufs, sems):
        self.order, self.bufs, self.sems = order, bufs, sems
        self.posts, held = [], list(left)
        for split in order:
            self.posts.append(1 << (len(held) - 1 - held.index(split)))
            held.remove(split)

    def parts(self, stage):
        axis, bit = self.order[stage]
        me = lax.axis_index(axis)
        mine = (me // (1 << bit)) % 2
        return {axis: me + (1 << bit) * (1 - 2 * mine)}, mine

    def half(self, stage, which):
        ref, post = self.bufs[stage], self.posts[stage]
        return ref.reshape(ref.shape[0] // (2 * post), 2, post, *ref.shape[1:]), which

    def copy(self, stage):
        partner, mine = self.parts(stage)
        into = self.bufs[stage + 1]
        view, which = self.half(stage, 1 - mine)
        return pltpu.make_async_remote_copy(
            src_ref=view.at[:, which],
            dst_ref=into.reshape(into.shape[0] // self.posts[stage], self.posts[stage], *into.shape[1:]),
            send_sem=self.sems.at[0, stage],
            recv_sem=self.sems.at[1, stage],
            device_id=partner,
            device_id_type=MESH,
        )

    def start(self, stage=0):
        self.copy(stage).start()

    def turn(self, stage):
        self.copy(stage).wait()
        _, mine = self.parts(stage)
        into, ref, post = self.bufs[stage + 1], self.bufs[stage], self.posts[stage]

        def one(i, carry):
            into[i] = into[i] + ref[((i // post) * 2 + mine) * post + i % post]
            return carry

        lax.fori_loop(0, into.shape[0], one, 0)
        if stage + 1 < len(self.order):
            self.start(stage + 1)


def columns(axis_sum):
    return jnp.sum(axis_sum.reshape(-1, 8, axis_sum.shape[-1]), axis=0)


def norm_back(value, grad, gain, base, write, vec, row):
    rows, width = grad.shape
    step = min(64, rows)

    def chunk(i, sums):
        at = pl.ds(pl.multiple_of(i * step, step), step)
        centred = value[at, :].astype(jnp.float32)
        centred = centred - jnp.mean(centred, axis=-1, keepdims=True)
        scale = lax.rsqrt(jnp.mean(centred * centred, axis=-1, keepdims=True) + 1e-05)
        unit = centred * scale
        error = grad[at, :]
        term = error * gain
        back = scale * (term - jnp.mean(term, axis=-1, keepdims=True) - unit * jnp.mean(term * unit, axis=-1, keepdims=True))
        write(at, base[at, :].astype(jnp.float32) + back)
        return sums[0] + columns(error * unit), sums[1] + columns(error)

    zero = jnp.zeros((8, width), jnp.float32)
    gain_sum, shift_sum = lax.fori_loop(0, rows // step, chunk, (zero, zero))
    vec[row : row + 1, :] = jnp.sum(gain_sum, axis=0, keepdims=True)
    vec[row + 1 : row + 2, :] = jnp.sum(shift_sum, axis=0, keepdims=True)


def tail_kernel(names, clip_stages, blk_stages, *refs):
    r = SimpleNamespace(**dict(zip(names, refs)))
    rest = list(refs[len(names) :])
    stages = clip_stages + blk_stages - 1
    r.wide, rest = rest[:stages], rest[stages:]
    r.tall, rest = rest[:stages], rest[stages:]
    r.kv, rest = rest[:blk_stages], rest[blk_stages:]
    r.head_w, r.text_w = rest[:clip_stages], rest[clip_stages:]
    clips, blks = lax.axis_size("clip"), lax.axis_size("blk")
    me, clip = lax.axis_index("blk"), lax.axis_index("clip")
    core = me % 2
    pair = {"blk": me + 1 - 2 * core}
    devices = clips * blks
    rows, depth = r.frames.shape
    half = depth // 2
    width = depth // blks
    heads = width // HEAD
    tokens = r.text.shape[0]
    chunk = r.first.shape[-1]
    chunks = r.hidden_in.shape[1] // chunk
    bf16, f32 = jnp.bfloat16, jnp.float32
    hidden_tokens = token_bias(r.lengths, tokens)
    vec = r.vec

    barrier = pltpu.get_barrier_semaphore()
    for step in range(1, clips):
        pl.semaphore_signal(barrier, inc=1, device_id={"clip": (clip + step) % clips}, device_id_type=MESH)
    greet("blk", clips - 1)

    sem_at = [0]

    def sem():
        sem_at[0] += 1
        return r.sems.at[sem_at[0] - 1]

    def local(source, target):
        return pltpu.make_async_copy(source, target, sem())

    def remote(source, target, where):
        return pltpu.make_async_remote_copy(
            src_ref=source, dst_ref=target, send_sem=sem(), recv_sem=sem(), device_id=where, device_id_type=MESH
        )

    own, other = pl.ds(0, rows), pl.ds(rows, rows)
    my_half = pl.ds(pl.multiple_of(core * half, half), half)
    its_half = pl.ds(pl.multiple_of((1 - core) * half, half), half)


    def hidden_loads(j):
        at = pl.ds(j * chunk, chunk)
        return (
            local(r.hidden_in.at[:, at], r.first.at[j % 2]),
            local(r.hidden_out.at[at, :], r.second.at[j % 2]),
        )

    act_here = local(r.act_three, r.cat_three.at[own])
    grad_here = local(r.cotangent, r.dy)
    act_here.start()
    grad_here.start()
    weights = {j: hidden_loads(j) for j in range(min(2, chunks))}
    for copies in weights.values():
        for copy in copies:
            copy.start()
    exchanged = {}
    three, mixed, two, att, grads = range(5)
    for name, (source, cat) in enumerate(((r.act_three, r.cat_three), (r.mixed, r.cat_mixed), (r.act_two, r.cat_two), (r.att, r.cat_att))):
        exchanged[name] = [remote(source, cat.at[other], pair)]
        if name != three:
            exchanged[name].append(local(source, cat.at[own]))
    exchanged[grads] = [
        remote(r.cotangent.at[:, its_half], r.cat_dy.at[other], pair),
        local(r.cotangent.at[:, my_half], r.cat_dy.at[own]),
    ]
    for name in (three, grads, mixed, two, att):
        for copy in exchanged[name]:
            copy.start()
    small = [
        local(source, into)
        for source, into in ((r.after_cross, r.value), (r.text_keys, r.tk), (r.text_values, r.tv), (r.cross_queries, r.cq))
    ]
    for copy in small:
        copy.start()
    act_here.wait()
    grad_here.wait()

    clip_bits = [("clip", k) for k in range(bits_of(clips))]
    blk_bits = [("blk", k) for k in range(bits_of(blks))]
    left = clip_bits[::-1] + blk_bits[::-1]
    orders = [clip_bits + blk_bits[1:], clip_bits[::-1] + blk_bits[1:]]
    early = [blk_bits[1:] + clip_bits, blk_bits[1:] + clip_bits[::-1]]
    pieces = []
    for p in range(2 * chunks + 3):
        wide = p < chunks or p >= 2 * chunks
        held = [r.wide_own, *r.wide] if wide else [r.tall_own, *r.tall]
        nth = (p if p < chunks else p - chunks) if wide else p - chunks
        order = early[EARLY.index(p) % 2] if p in EARLY else orders[(p - sum(q < p for q in EARLY)) % 2]
        pieces.append(
            Halving(left, order, [held[0].at[nth % chunks]] + [level.at[nth] for level in held[1:]], r.piece_sems.at[p])
        )

    def finish(p, out, column, rows_out):
        piece = pieces[p]
        size = piece.bufs[-1].shape[-1]
        base = core * half + column if p >= chunks and p < 2 * chunks else column + core * half
        at = pl.ds(pl.multiple_of(base, size), size)
        tall_piece = chunks <= p < 2 * chunks
        stage = r.tall_fix.at[p - chunks] if tall_piece else r.wide_fix.at[p if p < chunks else p - chunks]
        stage[...] = piece.bufs[-1][1 - core].astype(f32)
        copy = remote(stage, out.at[:, at], pair)
        copy.start()
        out[:, at] = piece.bufs[-1][core].astype(f32)
        return copy

    fixes = []

    def task(stage, p):
        if stage < stages:
            pieces[p].turn(stage)
        if stage == stages - 1:
            if p < chunks:
                fixes.append((p, finish(p, r.hidden_in_out, p * chunk, None)))
            elif p < 2 * chunks:
                fixes.append((p, finish(p, r.hidden_out_out, (p - chunks) * (half // chunks), None)))
            else:
                fixes.append((p, finish(p, (r.cross_out_out, r.cross_query_out, r.self_out_out)[p - 2 * chunks], 0, None)))

    total = len(pieces)
    at_point, reached = [0], [-2] * total

    def reach(stage, p):
        while reached[p] < stage:
            reached[p] += 1
            if reached[p] < 0:
                pieces[p].start()
            else:
                task(reached[p], p)

    def point():
        if at_point[0] < len(PLAN):
            for stage, p in PLAN[at_point[0]]:
                if p < total:
                    reach(stage, p)
        at_point[0] += 1

    def outer(cat_left, cat_right, into):
        entries, block = into.shape[:2]
        group = max(1, 256 // block)

        def part(m, carry):
            at = pl.ds(pl.multiple_of(m * group * block, group * block), group * block)
            made = matmul(cat_left[:, at], cat_right[...], (0, 0))
            into[pl.ds(m * group, group)] = made.reshape(group, block, made.shape[-1]).astype(bf16)
            return carry

        lax.fori_loop(0, entries // group, part, 0)

    swaps = {}
    sub = min(256, chunk)
    for j in range(chunks):
        for copy in weights[j]:
            copy.wait()
        first, second = r.first.at[j % 2], r.second.at[j % 2]
        pre_low = r.pre_low.at[j % 2]
        hidden = r.cat_hidden.at[own, pl.ds(j * chunk, chunk)]
        if j >= 2:
            swaps[j - 2][0].wait_send()

        def part(u, carry):
            at = pl.ds(pl.multiple_of(u * sub, sub), sub)
            pre = matmul(r.cat_three[own, :], first[:, at])
            grad = matmul(r.dy[...], second[at, :], (1, 1))
            phi = 0.5 * (1.0 + lax.erf(pre * math.sqrt(0.5)))
            slope = phi + pre * (jnp.exp(-0.5 * pre * pre) * (1.0 / math.sqrt(2.0 * math.pi)))
            hidden[:, at] = (pre * phi).astype(bf16)
            pre_low[:, at] = (grad * slope).astype(bf16)
            return carry

        lax.fori_loop(0, chunk // sub, part, 0)
        swaps[j] = (
            remote(pre_low.at[:, pl.ds(pl.multiple_of((1 - core) * (chunk // 2), chunk // 2), chunk // 2)], r.cat_pre.at[j, other], pair),
            remote(hidden, r.cat_hidden.at[other, pl.ds(j * chunk, chunk)], pair),
        )
        for copy in swaps[j]:
            copy.start()
        r.cat_pre[j, own, :] = pre_low[:, pl.ds(pl.multiple_of(core * (chunk // 2), chunk // 2), chunk // 2)]
        made = matmul(hidden[...], second[...])
        back = matmul(pre_low[...], first[...], (1, 1))
        if j == 0:
            r.total[...] = made
            r.grad[...] = back
        else:
            r.total[...] += made
            r.grad[...] += back
        if j + 2 < chunks:
            weights[j + 2] = hidden_loads(j + 2)
            for copy in weights[j + 2]:
                copy.start()
        point()
        if j == 0:
            for copy in exchanged[three]:
                copy.wait()
        else:
            swaps[j - 1][0].wait_recv()
            outer(r.cat_three, r.cat_pre.at[j - 1], pieces[j - 1].bufs[0])
            point()
    for j in (chunks - 2, chunks - 1):
        swaps[j][0].wait_send()
    later = [
        local(source, into.at[slot])
        for source, into, slot in ((r.cross_out, r.first, 0), (r.cross_query, r.second, 0), (r.self_out, r.first, 1))
    ]
    for copy in later:
        copy.start()
    swaps[chunks - 1][0].wait_recv()
    outer(r.cat_three, r.cat_pre.at[chunks - 1], pieces[chunks - 1].bufs[0])
    point()
    for copy in small:
        copy.wait()
    r.low[1] = (r.value[...] + r.total[...]).astype(bf16)
    output_copy = local(r.low.at[1], r.output)
    output_copy.start()
    for copy in exchanged[grads]:
        copy.wait()
    for j in range(chunks):
        swaps[j][1].wait()
    tall = half // chunks
    block = r.tall_own.shape[2]
    group = max(1, 512 // block)

    def tall_part(m, carry):
        at = pl.ds(pl.multiple_of(m * group * block, group * block), group * block)
        made = matmul(r.cat_hidden[:, at], r.cat_dy[...], (0, 0))
        for w in range(chunks):
            r.tall_own[w, pl.ds(m * group, group)] = made[:, w * tall : (w + 1) * tall].reshape(group, block, tall).astype(bf16)
        return carry

    turns = devices // group
    lax.fori_loop(0, turns // 2, tall_part, 0)
    point()
    lax.fori_loop(turns // 2, turns, tall_part, 0)
    point()

    def keep_two(at, value):
        r.total[at, :] = value
        r.low[0, at, :] = value.astype(bf16)

    norm_back(r.value, r.grad, r.gain_2[...], r.dy, keep_two, vec, 4)
    second_value = local(r.after_self, r.value)
    second_value.start()

    def share(which):
        copy = remote(r.low.at[which, :, its_half], r.cat_low.at[which, other], pair)
        copy.start()
        r.cat_low[which, own, :] = r.low[which, :, my_half]
        return copy

    shared = [share(0)]
    later[0].wait()
    output_copy.wait()
    r.dy[...] = matmul(r.low[0], r.first[0], (1, 1)).astype(bf16)
    point()
    lanes = min(128, depth)
    groups = lanes // width

    def cross(t, carry):
        at = pl.ds(pl.multiple_of(t * lanes, lanes), lanes)
        queries, keys, values, grads = r.cq[:, at], r.tk[:, at], r.tv[:, at], r.dy[:, at]
        query_sum = jnp.zeros((rows, lanes), f32)
        key_sum, value_sum = jnp.zeros((tokens, lanes), f32), jnp.zeros((tokens, lanes), f32)
        for h in range(lanes // HEAD):
            query_h, grad_h, key_h = head_only(queries, h), head_only(grads, h), head_only(keys, h)
            scores = matmul(keys, query_h, (1, 1)) * 0.125 + hidden_tokens
            scores = jnp.exp(scores - jnp.max(scores, axis=0, keepdims=True))
            prob = scores / jnp.sum(scores, axis=0, keepdims=True)
            dprob = matmul(values, grad_h, (1, 1))
            dscore = (prob * (dprob - jnp.sum(prob * dprob, axis=0, keepdims=True))).astype(bf16)
            query_sum = query_sum + matmul(dscore, key_h, (0, 0))
            key_sum = key_sum + matmul(dscore, query_h)
            value_sum = value_sum + matmul(prob.astype(bf16), grad_h)
        r.low[1, :, at] = (query_sum * 0.125).astype(bf16)
        for g in range(groups):
            r.kv_own[t * groups + g, :, :width] = (key_sum[:, g * width : (g + 1) * width] * 0.125).astype(bf16)
            r.kv_own[t * groups + g, :, width:] = value_sum[:, g * width : (g + 1) * width].astype(bf16)
        return carry

    turns = depth // lanes
    for quarter in range(4):
        lax.fori_loop(turns * quarter // 4, turns * (quarter + 1) // 4, cross, 0)
        point()
    text_load = local(r.text, r.tk)
    text_load.start()
    text_sum = Halving(blk_bits[::-1], blk_bits, [r.kv_own, *r.kv], r.kv_sems)
    text_sum.start()
    shared.append(share(1))
    point()
    later[1].wait()
    r.grad[...] = matmul(r.low[1], r.second[0], (1, 1))
    second_value.wait()
    shared[0].wait_send()

    def keep_one(at, value):
        r.total[at, :] = value
        r.low[0, at, :] = value.astype(bf16)

    norm_back(r.value, r.grad, r.gain_1[...], r.total, keep_one, vec, 2)
    point()
    for copy in (share_one := [remote(r.low.at[0, :, its_half], r.cat_low.at[2, other], pair)]):
        copy.start()
    r.cat_low[2, own, :] = r.low[0, :, my_half]
    later[2].wait()
    att_grad = matmul(r.low[0], r.first[1], (1, 1)).astype(bf16)
    for s in range(blks):
        r.grad_own[s] = att_grad[:, s * width : (s + 1) * width]

    block_sems = r.block_sems

    def fetch(peer, source):
        return pltpu.make_async_remote_copy(
            src_ref=r.grad_own.at[peer], dst_ref=r.grad_all.at[source], send_sem=block_sems.at[0, peer],
            recv_sem=block_sems.at[1, source], device_id={"blk": peer}, device_id_type=MESH,
        )

    def give(peer, source):
        return pltpu.make_async_remote_copy(
            src_ref=r.qkv_here.at[peer], dst_ref=r.sums_in.at[source], send_sem=block_sems.at[2, peer],
            recv_sem=block_sems.at[3, source], device_id={"blk": peer}, device_id_type=MESH,
        )

    for step in range(1, blks):
        fetch((me + step) % blks, me).start()
    r.grad_all[me] = r.grad_own[me]
    attention_inputs = [local(source, into) for source, into in ((r.qkv, r.qkv_here), (r.full, r.full_here), (r.lse, r.lse_rows))]
    for copy in attention_inputs:
        copy.start()
    projections = [
        local(source, into.at[slot])
        for source, into, slot in ((r.self_query, r.first, 0), (r.self_key, r.second, 0), (r.self_value, r.second, 1))
    ]
    text_weight = local(r.cross_key, r.first.at[1])
    for copy in (*projections, text_weight):
        copy.start()
    point()
    text_sum.turn(0)

    def last_pieces():
        for n, (name, cat, wait) in enumerate(((mixed, r.cat_mixed, shared[0]), (two, r.cat_two, shared[1]), (att, r.cat_att, share_one[0]))):
            for copy in exchanged[name]:
                copy.wait()
            wait.wait_recv() if n == 0 else wait.wait()
            if n < chunks:
                reach(0, n)
            outer(cat, r.cat_low.at[n], pieces[2 * chunks + n].bufs[0])
            point()

    last_pieces()
    text_done = text_sum.bufs[-1].at[0]
    text_rows = tokens // blks

    def swap_text(peer, source):
        return pltpu.make_async_remote_copy(
            src_ref=text_done.at[pl.ds(pl.multiple_of(peer * text_rows, text_rows), text_rows)], dst_ref=r.text_in.at[source],
            send_sem=block_sems.at[4, peer], recv_sem=block_sems.at[5, source], device_id={"blk": peer}, device_id_type=MESH,
        )

    clip_left = clip_bits[::-1] + blk_bits[::-1]
    text_w = Halving(clip_left, clip_bits[::-1], [r.text_w_own, *r.text_w], r.clip_sems.at[0])
    head_w = Halving(clip_left, clip_bits, [r.head_w_own, *r.head_w], r.clip_sems.at[1])

    def text_back(part):
        for s in range(blks):
            r.text_cat[:, s * width : (s + 1) * width] = r.text_in[s, :, part * width : (part + 1) * width]
        return matmul(r.text_cat[...], r.first[1], (1, 1))

    def text_ready():
        for step in range(1, blks):
            swap_text((me + step) % blks, me).start()
        r.text_in[me] = text_done[pl.ds(pl.multiple_of(me * text_rows, text_rows), text_rows), :]
        text_load.wait()
        outer(r.tk, text_done, r.text_w_own)
        text_w.start()

    for copy in attention_inputs:
        copy.wait()
    qkv, full = r.qkv_here, r.full_here
    for step in range(1, blks):
        fetch((me + step) % blks, (me + step) % blks).wait_recv()
    text_sum.turn(1)
    point()
    for i in range(blks):
        product = (r.grad_all[i].astype(f32) * full[i]).T
        for h in range(heads):
            r.delta_rows[i, h : h + 1, :] = jnp.sum(product[h * HEAD : (h + 1) * HEAD], axis=0, keepdims=True)

    full[...] = jnp.zeros_like(full)
    point()
    mask = causal(rows, True)

    r.pair_sum[...] = jnp.zeros_like(r.pair_sum)
    near = min(3 * width, rows)
    head_sums = [(r.value, 0, near)] + ([(r.grad, near, 3 * width - near)] if near < 3 * width else [])

    def update(i, j, masked):
        keys, values = qkv[j, :, width : 2 * width], qkv[j, :, 2 * width :]
        queries, grad = qkv[i, :, :width], r.grad_all[i]
        query_term = key_term = value_term = None
        for h in range(heads):
            query_h, grad_h, key_h = head_only(queries, h), head_only(grad, h), head_only(keys, h)
            scores = matmul(keys, query_h, (1, 1))
            probs = jnp.exp(scores - r.lse_rows[i, h : h + 1, :])
            if masked:
                probs = jnp.where(mask, probs, 0.0)
            dprobs = matmul(values, grad_h, (1, 1))
            dscores = (probs * (dprobs - r.delta_rows[i, h : h + 1, :])).astype(bf16)
            terms = matmul(dscores, key_h, (0, 0)), matmul(dscores, query_h), matmul(probs.astype(bf16), grad_h)
            query_term = terms[0] if h == 0 else query_term + terms[0]
            key_term = terms[1] if h == 0 else key_term + terms[1]
            value_term = terms[2] if h == 0 else value_term + terms[2]
        full[i] += query_term
        r.pair_sum[j, :, :width] += key_term
        r.pair_sum[j, :, width:] += value_term

    def block_of(turn):
        return turn + core * (blks - 1 - 2 * turn)

    def act_load(turn):
        return pltpu.make_async_copy(r.act_all.at[block_of(turn)], r.low.at[turn % 2], block_sems.at[6, turn])

    act_load(0).start()
    act_load(1).start()

    def attend_block(turn):
        block = block_of(turn)
        update(block, block, True)
        if turn + 1 < blks:
            lax.fori_loop(1, blks - turn, lambda n, held: (update(block + n * (1 - core), block - n * core, False), held)[1], 0)
        qkv[block, :, :width] = (full[block] * 0.125).astype(bf16)
        qkv[block, :, width:] = r.pair_sum[block].astype(bf16)

        @pl.when(block != me)
        def _():
            give(block, me).start()

        act_load(turn).wait()
        made = matmul(qkv[block], r.low[turn % 2], (0, 0))
        for ref, first, count in head_sums:
            if turn == 0:
                ref[:count] = made[first : first + count]
            else:
                ref[:count] += made[first : first + count]
        if turn + 2 < blks:
            act_load(turn + 2).start()

    for j in range(blks):
        attend_block(j)
        if j == 1:
            for stage in range(2, len(blk_bits)):
                text_sum.turn(stage)
            text_ready()
        if j == 4:
            text_w.turn(0)
        if j == 5:
            for step in range(1, blks):
                swap_text((me + step) % blks, (me + step) % blks).wait_recv()
            text_weight.wait()
            r.text_grad[...] = text_back(0)
            text_weight = local(r.cross_value, r.first.at[1])
            text_weight.start()
        point()
    for stage in range(1, len(clip_bits)):
        text_w.turn(stage)
    r.sums_in[me] = r.qkv_here[me]
    for ref, first, count in head_sums:
        turned = ref[:count].T
        r.head_w_own[:, :, first : first + count] = turned.reshape(devices, -1, count).astype(bf16)
    head_w.start()

    def swap_w(summed, out, base, peer, source):
        return pltpu.make_async_remote_copy(
            src_ref=summed.bufs[-1].at[peer], dst_ref=out.at[source], send_sem=block_sems.at[base, peer],
            recv_sem=block_sems.at[base + 1, source], device_id={"blk": peer}, device_id_type=MESH,
        )

    for step in range(1, blks):
        swap_w(text_w, r.text_w_out, 7, (me + step) % blks, me).start()
    r.text_w_out[me] = text_w.bufs[-1][me]
    for copy in projections:
        copy.wait()
    first_value = local(r.frames, r.dy)
    first_value.start()
    for step in range(1, blks):
        give((me + step) % blks, (me + step) % blks).wait_recv()
    grad_rows = [r.low.at[0], r.low.at[1], r.cq]
    for s in range(blks):
        for t in range(3):
            grad_rows[t][:, s * width : (s + 1) * width] = r.sums_in[s, :, t * width : (t + 1) * width]
    point()
    head_w.turn(0)
    r.grad[...] = matmul(grad_rows[0][...], r.first[0], (1, 1))
    r.grad[...] += matmul(grad_rows[1][...], r.second[0], (1, 1))
    r.grad[...] += matmul(grad_rows[2][...], r.second[1], (1, 1))
    first_value.wait()
    text_weight.wait()
    r.text_grad[...] += text_back(1)
    point()

    def keep_frames(at, value):
        r.value[at, :] = value

    norm_back(r.dy, r.grad, r.gain_0[...], r.total, keep_frames, vec, 0)
    frames_copy = local(r.value, r.frames_grad)
    frames_copy.start()
    vec[6:8, :] = jnp.zeros((2, depth), f32)
    part = depth // clips

    def swap_vec(peer, source):
        return pltpu.make_async_remote_copy(
            src_ref=vec.at[:, pl.ds(pl.multiple_of(peer * part, part), part)], dst_ref=r.vec_in.at[source],
            send_sem=r.vec_sems.at[0, peer], recv_sem=r.vec_sems.at[1, source], device_id={"clip": peer}, device_id_type=MESH,
        )

    for step in range(1, clips):
        swap_vec((clip + step) % clips, clip).start()
    r.vec_in[clip] = vec[:, pl.ds(pl.multiple_of(clip * part, part), part)]
    for stage in range(1, len(clip_bits)):
        head_w.turn(stage)
    for step in range(1, blks):
        swap_w(head_w, r.head_w_out, 9, (me + step) % blks, me).start()
    r.head_w_out[me] = head_w.bufs[-1][me]
    point()
    for step in range(1, clips):
        swap_vec((clip + step) % clips, (clip + step) % clips).wait_recv()
    r.vec_sum[me] = jnp.sum(r.vec_in[...], axis=0)

    def share_vec(peer, source):
        return pltpu.make_async_remote_copy(
            src_ref=r.vec_sum.at[me], dst_ref=r.vec_sum.at[source], send_sem=block_sems.at[11, peer],
            recv_sem=block_sems.at[12, source], device_id={"blk": peer}, device_id_type=MESH,
        )

    for step in range(1, blks):
        share_vec((me + step) % blks, me).start()
    for k in range(total + 2 * stages):
        for stage in range(stages):
            if 0 <= k - 2 * stage < total:
                reach(stage, k - 2 * stage)
    for step in range(1, blks):
        share_vec((me + step) % blks, (me + step) % blks).wait_recv()
    summed = jnp.sum(r.vec_sum[...], axis=0)
    share_own = depth // devices
    turned = pltpu.roll(summed, (summed.shape[-1] - me * share_own) % summed.shape[-1], 1)
    for n, out in enumerate((r.vec_0, r.vec_1, r.vec_2, r.vec_3, r.vec_4, r.vec_5)):
        out[...] = turned[n : n + 1, :share_own]
    for _, copy in fixes:
        copy.wait()
    frames_copy.wait()
    for step in range(1, clips):
        swap_vec((clip + step) % clips, clip).wait_send()
    for step in range(1, blks):
        peer = (me + step) % blks
        fetch(peer, me).wait_send()
        give(peer, me).wait_send()
        swap_text(peer, me).wait_send()
        for summed, out, base in ((text_w, r.text_w_out, 7), (head_w, r.head_w_out, 9)):
            swap_w(summed, out, base, peer, me).wait_send()
            swap_w(summed, out, base, peer, peer).wait_recv()
        share_vec(peer, me).wait_send()
    stored = []
    for parts, outs in ((r.head_w_out, (r.query_w, r.key_w, r.value_w)), (r.text_w_out, (r.text_key_w, r.text_value_w))):
        for t, out in enumerate(outs):
            stage = r.grad.at[pl.ds(len(stored) * share_own, share_own)]
            for s in range(blks):
                stage[:, s * width : (s + 1) * width] = parts[s, :, t * width : (t + 1) * width].astype(f32)
            stored.append(local(stage, out))
            stored[-1].start()
    for copy in stored:
        copy.wait()


def backward(inputs, gains, lengths, clips, blks):
    rows, depth = inputs["frames"].shape
    tokens = inputs["text"].shape[0]
    hidden = inputs["hidden_in"].shape[1]
    devices, width, half = clips * blks, depth // blks, depth // 2
    chunk = min(1024, hidden)
    chunks = hidden // chunk
    own = depth // devices
    tall = half // chunks
    stages = bits_of(clips) + bits_of(blks) - 1
    bf16, f32 = jnp.bfloat16, jnp.float32
    hbm, vmem = pl.BlockSpec(memory_space=pltpu.MemorySpace.HBM), pl.BlockSpec(memory_space=pltpu.VMEM)
    dma = pltpu.SemaphoreType.DMA
    shape = jax.ShapeDtypeStruct
    row = shape((own, depth), f32)
    outs = dict(
        output=shape((rows, depth), bf16), frames_grad=shape((rows, depth), f32), text_grad=shape((tokens // blks, depth), f32),
        query_w=row, key_w=row, value_w=row, self_out_out=row, cross_query_out=row, text_key_w=row, text_value_w=row, cross_out_out=row,
        hidden_in_out=shape((own, hidden), f32), hidden_out_out=shape((hidden // devices, depth), f32),
        **{f"vec_{n}": shape((1, own), f32) for n in range(6)},
    )
    scratch = dict(
        first=((2, depth, chunk), bf16), second=((2, chunk, depth), bf16),
        cat_three=((2 * rows, depth), bf16), cat_mixed=((2 * rows, depth), bf16), cat_two=((2 * rows, depth), bf16),
        cat_att=((2 * rows, depth), bf16), cat_dy=((2 * rows, half), bf16), dy=((rows, depth), bf16),
        cat_hidden=((2 * rows, hidden), bf16), pre_low=((2, rows, chunk), bf16), cat_pre=((chunks, 2 * rows, chunk // 2), bf16),
        total=((rows, depth), f32), grad=((rows, depth), f32), value=((rows, depth), f32),
        low=((2, rows, depth), bf16), cat_low=((3, 2 * rows, half), bf16),
        cq=((rows, depth), bf16), tk=((tokens, depth), bf16), tv=((tokens, depth), bf16),
        vec=((8, depth), f32), vec_in=((clips, 8, depth // clips), f32), vec_sum=((blks, 8, depth // clips), f32),
        wide_own=((chunks, devices, own, half), bf16), tall_own=((chunks, devices, hidden // devices, tall), bf16),
        wide_fix=((chunks + 3, own, half), f32), tall_fix=((chunks, hidden // devices, tall), f32),
        text_in=((blks, tokens // blks, 2 * width), bf16), text_cat=((tokens // blks, depth), bf16),
        head_w_out=((blks, own, 3 * width), bf16), text_w_out=((blks, own, 2 * width), bf16),
        pair_sum=((blks, rows, 2 * width), f32),
        kv_own=((blks, tokens, 2 * width), bf16),
        head_w_own=((devices, own, 3 * width), bf16), text_w_own=((devices, own, 2 * width), bf16),
        grad_own=((blks, rows, width), bf16), grad_all=((blks, rows, width), bf16), sums_in=((blks, rows, 3 * width), bf16), qkv_here=((blks, rows, 3 * width), bf16), full_here=((blks, rows, width), f32),
        lse_rows=((blks, 8, rows), f32), delta_rows=((blks, 8, rows), f32),

    )
    levels = [((chunks + 3, devices >> (s + 1), own, half), bf16) for s in range(stages)]
    levels += [((chunks, devices >> (s + 1), hidden // devices, tall), bf16) for s in range(stages)]
    levels += [((blks >> (s + 1), tokens, 2 * width), bf16) for s in range(bits_of(blks))]
    for parts in (3, 2):
        levels += [((devices >> (s + 1), own, parts * width), bf16) for s in range(bits_of(clips))]
    sems = dict(
        sems=(160,), piece_sems=(2 * chunks + 3, 2, stages), kv_sems=(2, bits_of(blks)), block_sems=(13, blks),
        clip_sems=(2, 2, bits_of(clips)), vec_sems=(2, clips),
    )
    small = dict(lengths=lengths, gain_0=gains[0], gain_1=gains[1], gain_2=gains[2])
    names = [*inputs, *small, *outs, *scratch, *sems]
    made = pl.pallas_call(
        partial(tail_kernel, names, bits_of(clips), bits_of(blks)),
        out_shape=list(outs.values()),
        in_specs=[hbm] * len(inputs) + [pl.BlockSpec(memory_space=pltpu.SMEM)] + [vmem] * 3,
        out_specs=[hbm if i in (0, 1, 3, 4, 5, 8, 9) else vmem for i in range(len(outs))],
        scratch_shapes=[pltpu.VMEM(*v) for v in scratch.values()] + [dma(v) for v in sems.values()] + [pltpu.VMEM(*v) for v in levels],
        compiler_params=pltpu.CompilerParams(collective_id=3, has_side_effects=True, vmem_limit_bytes=63 << 20),
    )(*inputs.values(), *small.values())
    return SimpleNamespace(**dict(zip(outs, made)))


def collect_kernel(*refs):
    count = len(refs) // 2
    for n in range(count):
        refs[count + n][...] = refs[n][...]


def collect(*arrays):
    vmem = pl.BlockSpec(memory_space=pltpu.VMEM)
    return pl.pallas_call(
        collect_kernel,
        out_shape=[jax.ShapeDtypeStruct(a.shape, a.dtype) for a in arrays],
        in_specs=[vmem] * len(arrays),
        out_specs=[vmem] * len(arrays),
        compiler_params=pltpu.CompilerParams(vmem_limit_bytes=32 << 20),
    )(*arrays)


def body(
    frames,
    text_states,
    prompt_lengths,
    cotangent,
    self_query,
    self_key,
    self_value,
    self_out,
    cross_query,
    cross_key,
    cross_value,
    cross_out,
    hidden_in,
    hidden_out,
    first_gain,
    first_shift,
    second_gain,
    second_shift,
    third_gain,
    third_shift,
):
    block_total, clip_total = lax.axis_size("blk"), lax.axis_size("clip")
    block_rank = lax.axis_index("blk")
    own = D // (clip_total * block_total)
    head_width = D // block_total
    local_text = text_states[0]
    projections = (self_query, self_key, self_value)
    if head_width % 128:
        projections = [lax.dynamic_slice_in_dim(matrix, block_rank * head_width, head_width, 1) for matrix in projections]
    norms = [v.reshape(1, D) for v in (first_gain, second_gain, third_gain, first_shift, second_shift, third_shift)]
    weights = dict(
        text=local_text, cross_key=cross_key, cross_value=cross_value, self_out=self_out, cross_query=cross_query, cross_out=cross_out
    )
    kept = forward(frames[0], projections, norms, prompt_lengths, weights, block_total)
    inputs = dict(
        act_three=kept.act_three, cotangent=cotangent[0], hidden_in=hidden_in, hidden_out=hidden_out, mixed=kept.mixed, act_two=kept.act_two,
        att=kept.att, after_cross=kept.after_cross, after_self=kept.after_self, frames=frames[0], text=local_text, text_keys=kept.tk,
        text_values=kept.tv, cross_queries=kept.cross_queries, cross_out=cross_out, cross_query=cross_query, self_out=self_out,
        self_query=self_query, self_key=self_key, self_value=self_value, qkv=kept.qkv, full=kept.full, lse=kept.lse, act_all=kept.act_all,
        cross_key=cross_key, cross_value=cross_value,
    )
    made = backward(inputs, norms[:3], prompt_lengths, clip_total, block_total)
    frames_grad, text_grad = made.frames_grad[None], made.text_grad[None]
    sums = [
        made.query_w, made.key_w, made.value_w, made.self_out_out, made.cross_query_out, made.text_key_w, made.text_value_w,
        made.cross_out_out, made.hidden_in_out, made.hidden_out_out,
    ]
    vectors = [v.reshape(own) for v in (made.vec_0, made.vec_1, made.vec_2, made.vec_3, made.vec_4, made.vec_5)]
    return (*collect(made.output[None], frames_grad, text_grad, *sums, *vectors),)


def solution(mesh):
    in_specs = (
        P("clip", "blk", None),
        P("clip", None, None),
        P("clip"),
        P("clip", "blk", None),
        P(),
        P(),
        P(),
        P(),
        P(),
        P(),
        P(),
        P(),
        P(),
        P(),
        P(),
        P(),
        P(),
        P(),
        P(),
        P(),
    )
    out_specs = (
        P("clip", "blk", None),
        P("clip", "blk", None),
        P("clip", "blk", None),
        P(("clip", "blk"), None),
        P(("clip", "blk"), None),
        P(("clip", "blk"), None),
        P(("clip", "blk"), None),
        P(("clip", "blk"), None),
        P(("clip", "blk"), None),
        P(("clip", "blk"), None),
        P(("clip", "blk"), None),
        P(("clip", "blk"), None),
        P(("clip", "blk"), None),
        P(("clip", "blk")),
        P(("clip", "blk")),
        P(("clip", "blk")),
        P(("clip", "blk")),
        P(("clip", "blk")),
        P(("clip", "blk")),
    )
    return jax.shard_map(body, mesh=mesh, in_specs=in_specs, out_specs=out_specs, check_vma=False)
```

```python
from functools import partial
import math
from types import SimpleNamespace

import jax
import jax.numpy as jnp
from jax import lax
from jax.experimental import pallas as pl
from jax.experimental.pallas import tpu as pltpu
from jax.sharding import PartitionSpec as P

D = 1024
HEADS = 16
HEAD = 64
TEXT = 256
MESH = pl.DeviceIdType.MESH


def normed(block, gain, shift):
    values = block.astype(jnp.float32)
    centred = values - jnp.mean(values, axis=-1, keepdims=True)
    variance = jnp.mean(centred * centred, axis=-1, keepdims=True)
    return centred * lax.rsqrt(variance + 1e-05) * gain + shift


def matmul(left, right, over=(1, 0)):
    return lax.dot_general(left, right, (((over[0],), (over[1],)), ((), ())), preferred_element_type=jnp.float32)


def greet(axis, others):
    me, size = lax.axis_index(axis), lax.axis_size(axis)
    barrier = pltpu.get_barrier_semaphore()
    for step in range(1, size):
        pl.semaphore_signal(barrier, inc=1, device_id={axis: (me + step) % size}, device_id_type=MESH)
    pl.semaphore_wait(barrier, size - 1 + others)


def head_only(block, head):
    lanes = block.shape[-1]
    if lanes == HEAD:
        return block
    lane = lax.broadcasted_iota(jnp.int32, block.shape, 1)
    return jnp.where((lane // HEAD) == head, block, jnp.zeros_like(block))


def causal(rows, transposed):
    row = lax.broadcasted_iota(jnp.int32, (rows, rows), 0)
    column = lax.broadcasted_iota(jnp.int32, (rows, rows), 1)
    return (row <= column) if transposed else (column <= row)


def token_bias(lengths, tokens):
    token = lax.broadcasted_iota(jnp.int32, (tokens, 1), 0)
    return jnp.where(token < lengths[0], 0.0, -1e30)


def forward_kernel(names, *refs):
    r = SimpleNamespace(**dict(zip(names, refs)))
    blks = lax.axis_size("blk")
    chips = blks // 2
    me = lax.axis_index("blk")
    chip, core = me // 2, me % 2
    rows, width = r.low.shape[1:]
    depth = r.frames_here.shape[1]
    heads = width // HEAD
    bf16, f32 = jnp.bfloat16, jnp.float32
    gathered, qkv = r.gathered, r.qkv
    sem_at = [0]

    def local(source, target):
        sem_at[0] += 1
        return pltpu.make_async_copy(source, target, r.sems.at[sem_at[0] - 1])

    slices = []
    for n, source in enumerate((r.projection_0, r.projection_1, r.projection_2)):
        if source.shape[1] > width:
            source = source.at[:, pl.ds(pl.multiple_of(me * width, width), width)]
        slices.append(local(source, r.weight.at[n]))
    loads = [
        local(source, target)
        for source, target in (
            (r.text, r.text_here), (r.cross_key, r.key_here), (r.cross_value, r.value_here), (r.self_out, r.self_out_here),
            (r.cross_query, r.cross_query_here), (r.cross_out, r.cross_out_here),
        )
    ]
    for copy in slices:
        copy.start()
    greet("blk", 0)
    gathered[me] = r.frames_here[...]
    for copy in loads:
        copy.start()
    hidden_tokens = token_bias(r.lengths, r.tk.shape[0])

    def ring(slot, way):
        return pltpu.make_async_remote_copy(
            src_ref=gathered.at[slot], dst_ref=gathered.at[slot], send_sem=r.ring_send.at[0 if way > 0 else 1, slot],
            recv_sem=r.ring_recv.at[slot], device_id={"blk": me + 2 * way}, device_id_type=MESH,
        )

    def across(slot):
        return pltpu.make_async_remote_copy(
            src_ref=gathered.at[slot], dst_ref=gathered.at[slot], send_sem=r.core_send.at[slot],
            recv_sem=r.core_recv.at[slot], device_id={"blk": chip * 2 + 1 - core}, device_id_type=MESH,
        )

    def send(block):
        return pltpu.make_async_remote_copy(
            src_ref=r.low.at[block], dst_ref=r.att_parts.at[me], send_sem=r.out_send.at[block],
            recv_sem=r.out_recv.at[me], device_id={"blk": block}, device_id_type=MESH,
        )

    def project_block(slot):
        act = normed(gathered[slot], r.gain_0[...], r.shift_0[...]).astype(bf16)
        r.act_all[slot] = act
        qkv[slot, :, :width] = matmul(act, r.weight[0]).astype(bf16) * jnp.bfloat16(0.125)
        qkv[slot, :, width : 2 * width] = matmul(act, r.weight[1]).astype(bf16)
        values = matmul(act, r.weight[2]).astype(bf16)
        qkv[slot, :, 2 * width :] = values
        r.value_rows[slot] = values.T

    mask = causal(rows, True)
    r.peaks[...] = jnp.full_like(r.peaks, -1e30)
    r.totals[...] = jnp.zeros_like(r.totals)
    r.acc[...] = jnp.zeros_like(r.acc)

    def update(i, j):
        def pair(masked):
            keys, queries = qkv[j, :, width : 2 * width], qkv[i, :, :width]
            for h in range(heads):
                own = pl.ds(h * HEAD, HEAD)
                scores = matmul(keys, head_only(queries, h), (1, 1))
                if masked:
                    scores = jnp.where(mask, scores, -1e30)
                peak = r.peaks[i, h : h + 1, :]
                top = jnp.maximum(peak, jnp.max(scores, axis=0, keepdims=True))
                weights = jnp.exp(scores - top)
                rescale = jnp.exp(peak - top)
                r.peaks[i, h : h + 1, :] = top
                r.totals[i, h : h + 1, :] = r.totals[i, h : h + 1, :] * rescale + jnp.sum(weights, axis=0, keepdims=True)
                r.acc[i, own, :] = r.acc[i, own, :] * rescale + matmul(r.value_rows[j, own, :], weights.astype(bf16))

        pl.when(i == j)(lambda: pair(True))
        pl.when(i != j)(lambda: pair(False))

    def settle(i):
        for h in range(heads):
            own = pl.ds(h * HEAD, HEAD)
            r.acc[i, own, :] = r.acc[i, own, :] / r.totals[i, h : h + 1, :]
            r.lse[i, h : h + 1, :] = r.peaks[i, h : h + 1, :] + jnp.log(r.totals[i, h : h + 1, :])
        full = r.acc[i].T
        r.full[i] = full
        r.low[i] = full.astype(bf16)

        @pl.when(i != me)
        def _():
            send(i).start()

    def lower(first, stop):
        def one(i, carry):
            update(i, first)

            @pl.when(i > first)
            def _():
                update(i, first + 1)

            pl.when(first == 0)(lambda: settle(i))
            return carry

        lax.fori_loop(first, stop, one, 0)

    def upper(first, start):
        def one(i, carry):
            lax.fori_loop(start, i + 1, lambda j, held: (update(i, j), held)[1], 0)
            pl.when(start == 0)(lambda: settle(i))
            return carry

        lax.fori_loop(first, first + 2, one, 0)

    @pl.when(chip + 1 < chips)
    def _():
        ring(me, 1).start()

    @pl.when(chip > 0)
    def _():
        ring(me, -1).start()

    across(me).start()
    for copy in slices:
        copy.wait()
    project_block(me)
    other = chip * 2 + 1 - core
    across(other).wait_recv()
    project_block(other)
    upper(chip * 2, chip * 2)
    for copy in loads[:3]:
        copy.wait()
    r.tk[...] = matmul(r.text_here[...], r.key_here[...]).astype(bf16)
    r.tv[...] = matmul(r.text_here[...], r.value_here[...]).astype(bf16)

    for step in range(1, chips):
        for way in (1, -1):
            source = chip - way * step

            @pl.when((source >= 0) & (source < chips))
            def _():
                slot = source * 2 + core
                ring(slot, way).wait_recv()

                @pl.when((chip + way >= 0) & (chip + way < chips))
                def _():
                    ring(slot, way).start()

                across(slot).start()

        for way in (1, -1):
            source = chip - way * step

            @pl.when((source >= 0) & (source < chips))
            def _():
                project_block(source * 2 + core)
                across(source * 2 + 1 - core).wait_recv()
                project_block(source * 2 + 1 - core)
                if way > 0:
                    lower(source * 2, 2 * jnp.minimum(chip + step, chips))
                else:
                    upper(source * 2, 2 * jnp.maximum(chip - step, 0))

    stores = []

    def store(*pairs):
        for source, target in pairs:
            stores.append(local(source, target))
            stores[-1].start()

    store((r.act_all, r.act_all_out), (qkv, r.qkv_out), (r.full, r.full_out), (r.lse, r.lse_out), (r.tk, r.tk_out), (r.tv, r.tv_out))
    r.att_parts[me] = r.low[me]
    for copy in loads[3:]:
        copy.wait()
    for step in range(1, blks):
        peer = (me + step) % blks
        pltpu.make_async_remote_copy(
            src_ref=r.low.at[peer], dst_ref=r.att_parts.at[peer], send_sem=r.out_send.at[peer],
            recv_sem=r.out_recv.at[peer], device_id={"blk": peer}, device_id_type=MESH,
        ).wait_recv()
    for s in range(blks):
        r.att[:, s * width : (s + 1) * width] = r.att_parts[s]

    r.after_self[...] = r.frames_here[...].astype(f32) + matmul(r.att[...], r.self_out_here[...])
    r.act_two[...] = normed(r.after_self[...], r.gain_1[...], r.shift_1[...]).astype(bf16)
    r.cross_queries[...] = matmul(r.act_two[...], r.cross_query_here[...]).astype(bf16)
    lanes = min(128, depth)

    def cross(t, carry):
        at = pl.ds(pl.multiple_of(t * lanes, lanes), lanes)
        queries, keys, values = r.cross_queries[:, at], r.tk[:, at], r.tv[:, at]
        mixed = jnp.zeros((rows, lanes), f32)
        for h in range(lanes // HEAD):
            scores = matmul(keys, head_only(queries, h), (1, 1)) * 0.125 + hidden_tokens
            scores = jnp.exp(scores - jnp.max(scores, axis=0, keepdims=True))
            prob = scores / jnp.sum(scores, axis=0, keepdims=True)
            mixed = mixed + matmul(prob.astype(bf16), head_only(values, h), (0, 0))
        r.mixed[:, at] = mixed.astype(bf16)
        return carry

    lax.fori_loop(0, depth // lanes, cross, 0)
    store((r.att, r.att_out), (r.after_self, r.after_self_out), (r.act_two, r.act_two_out))
    store((r.cross_queries, r.cross_queries_out), (r.mixed, r.mixed_out))
    r.after_cross[...] = r.after_self[...] + matmul(r.mixed[...], r.cross_out_here[...])
    r.act_three[...] = normed(r.after_cross[...], r.gain_2[...], r.shift_2[...]).astype(bf16)

    store((r.after_cross, r.after_cross_out), (r.act_three, r.act_three_out))
    for step in range(1, blks):
        send((me + step) % blks).wait_send()

    @pl.when(chip + 1 < chips)
    def _():
        ring(me, 1).wait_send()

    @pl.when(chip > 0)
    def _():
        ring(me, -1).wait_send()

    across(me).wait_send()
    for step in range(1, chips):
        for way in (1, -1):
            source = chip - way * step

            @pl.when((source >= 0) & (source < chips))
            def _():
                slot = source * 2 + core

                @pl.when((chip + way >= 0) & (chip + way < chips))
                def _():
                    ring(slot, way).wait_send()

                across(slot).wait_send()

    for copy in stores:
        copy.wait()


def forward(frames, projections, norms, lengths, weights, blks):
    rows, depth = frames.shape
    width = depth // blks
    tokens = weights["text"].shape[0]
    bf16, f32 = jnp.bfloat16, jnp.float32
    hbm, vmem = pl.BlockSpec(memory_space=pltpu.MemorySpace.HBM), pl.BlockSpec(memory_space=pltpu.VMEM)
    dma = pltpu.SemaphoreType.DMA
    shape = jax.ShapeDtypeStruct
    small = dict(frames_here=frames)
    for n in range(3):
        small |= {f"gain_{n}": norms[n], f"shift_{n}": norms[3 + n]}
    weights = weights | {f"projection_{n}": projections[n] for n in range(3)}
    kept = dict(
        act_all=((blks, rows, depth), bf16), qkv=((blks, rows, 3 * width), bf16), full=((blks, rows, width), f32),
        lse=((blks, 8, rows), f32), att=((rows, depth), bf16), after_self=((rows, depth), f32), act_two=((rows, depth), bf16),
        cross_queries=((rows, depth), bf16), tk=((tokens, depth), bf16), tv=((tokens, depth), bf16),
        mixed=((rows, depth), bf16), after_cross=((rows, depth), f32), act_three=((rows, depth), bf16),
    )
    outs = {f"{name}_out": shape(*v) for name, v in kept.items()}
    scratch = dict(
        gathered=((blks, rows, depth), bf16), low=((blks, rows, width), bf16), att_parts=((blks, rows, width), bf16),
        value_rows=((blks, width, rows), bf16), peaks=((blks, 8, rows), f32), totals=((blks, 8, rows), f32), acc=((blks, width, rows), f32),
        text_here=((tokens, depth), bf16), key_here=((depth, depth), bf16), value_here=((depth, depth), bf16),
        self_out_here=((depth, depth), bf16), cross_query_here=((depth, depth), bf16), cross_out_here=((depth, depth), bf16),
        weight=((3, depth, width), bf16), **kept,
    )
    sems = dict(ring_send=(2, blks), ring_recv=(blks,), core_send=(blks,), core_recv=(blks,), out_send=(blks,), out_recv=(blks,), sems=(32,))
    names = ["lengths", *small, *weights, *outs, *scratch, *sems]
    made = pl.pallas_call(
        partial(forward_kernel, names),
        out_shape=list(outs.values()),
        in_specs=[pl.BlockSpec(memory_space=pltpu.SMEM)] + [vmem] * len(small) + [hbm] * len(weights),
        out_specs=[hbm] * len(outs),
        scratch_shapes=[pltpu.VMEM(*v) for v in scratch.values()] + [dma(v) for v in sems.values()],
        compiler_params=pltpu.CompilerParams(collective_id=1, has_side_effects=True, vmem_limit_bytes=60 << 20),
    )(lengths, *small.values(), *weights.values())
    return SimpleNamespace(**dict(zip(kept, made)))


EARLY = (0, 2)
PLAN = ((), (), ((-1, 0), ), (), ((-1, 1), ), (), ((-1, 2), ), ((-1, 3), ), (), ((0, 0), (-1, 4), (-1, 5), (-1, 6), (-1, 7)), (), ((0, 1), ), (), ((0, 2), ), ((0, 3), ), (), ((1, 0), (0, 4)), (), ((-1, 8), ), ((0, 5), (-1, 9)), (), ((2, 0), (1, 2), (1, 3), (0, 6), (0, 7), (-1, 10)), ((1, 1), ), ((2, 3), (1, 4)), ((2, 1), (0, 8)), ((1, 5), (0, 9), (3, 3), (2, 4), (3, 0)), ((2, 2), (1, 7)), ((3, 1), ), ((2, 5), (1, 6)), ((0, 10), (3, 4)), ((1, 8), ), ((3, 2), (3, 5), (2, 6), (2, 7), (1, 9), (1, 10)), ((2, 8), ), ())


def bits_of(size):
    return size.bit_length() - 1


class Halving:
    def __init__(self, left, order, bufs, sems):
        self.order, self.bufs, self.sems = order, bufs, sems
        self.posts, held = [], list(left)
        for split in order:
            self.posts.append(1 << (len(held) - 1 - held.index(split)))
            held.remove(split)

    def parts(self, stage):
        axis, bit = self.order[stage]
        me = lax.axis_index(axis)
        mine = (me // (1 << bit)) % 2
        return {axis: me + (1 << bit) * (1 - 2 * mine)}, mine

    def half(self, stage, which):
        ref, post = self.bufs[stage], self.posts[stage]
        return ref.reshape(ref.shape[0] // (2 * post), 2, post, *ref.shape[1:]), which

    def copy(self, stage):
        partner, mine = self.parts(stage)
        into = self.bufs[stage + 1]
        view, which = self.half(stage, 1 - mine)
        return pltpu.make_async_remote_copy(
            src_ref=view.at[:, which],
            dst_ref=into.reshape(into.shape[0] // self.posts[stage], self.posts[stage], *into.shape[1:]),
            send_sem=self.sems.at[0, stage],
            recv_sem=self.sems.at[1, stage],
            device_id=partner,
            device_id_type=MESH,
        )

    def start(self, stage=0):
        self.copy(stage).start()

    def turn(self, stage):
        self.copy(stage).wait()
        _, mine = self.parts(stage)
        into, ref, post = self.bufs[stage + 1], self.bufs[stage], self.posts[stage]

        def one(i, carry):
            into[i] = into[i] + ref[((i // post) * 2 + mine) * post + i % post]
            return carry

        lax.fori_loop(0, into.shape[0], one, 0)
        if stage + 1 < len(self.order):
            self.start(stage + 1)


def columns(axis_sum):
    return jnp.sum(axis_sum.reshape(-1, 8, axis_sum.shape[-1]), axis=0)


def norm_back(value, grad, gain, base, write, vec, row):
    rows, width = grad.shape
    step = min(64, rows)

    def chunk(i, sums):
        at = pl.ds(pl.multiple_of(i * step, step), step)
        centred = value[at, :].astype(jnp.float32)
        centred = centred - jnp.mean(centred, axis=-1, keepdims=True)
        scale = lax.rsqrt(jnp.mean(centred * centred, axis=-1, keepdims=True) + 1e-05)
        unit = centred * scale
        error = grad[at, :]
        term = error * gain
        back = scale * (term - jnp.mean(term, axis=-1, keepdims=True) - unit * jnp.mean(term * unit, axis=-1, keepdims=True))
        write(at, base[at, :].astype(jnp.float32) + back)
        return sums[0] + columns(error * unit), sums[1] + columns(error)

    zero = jnp.zeros((8, width), jnp.float32)
    gain_sum, shift_sum = lax.fori_loop(0, rows // step, chunk, (zero, zero))
    vec[row : row + 1, :] = jnp.sum(gain_sum, axis=0, keepdims=True)
    vec[row + 1 : row + 2, :] = jnp.sum(shift_sum, axis=0, keepdims=True)


def tail_kernel(names, clip_stages, blk_stages, *refs):
    r = SimpleNamespace(**dict(zip(names, refs)))
    rest = list(refs[len(names) :])
    stages = clip_stages + blk_stages - 1
    r.wide, rest = rest[:stages], rest[stages:]
    r.tall, rest = rest[:stages], rest[stages:]
    r.kv, rest = rest[:blk_stages], rest[blk_stages:]
    r.head_w, r.text_w = rest[:clip_stages], rest[clip_stages:]
    clips, blks = lax.axis_size("clip"), lax.axis_size("blk")
    me, clip = lax.axis_index("blk"), lax.axis_index("clip")
    core = me % 2
    pair = {"blk": me + 1 - 2 * core}
    devices = clips * blks
    rows, depth = r.frames.shape
    half = depth // 2
    width = depth // blks
    heads = width // HEAD
    tokens = r.text.shape[0]
    chunk = r.first.shape[-1]
    chunks = r.hidden_in.shape[1] // chunk
    bf16, f32 = jnp.bfloat16, jnp.float32
    hidden_tokens = token_bias(r.lengths, tokens)
    vec = r.vec

    barrier = pltpu.get_barrier_semaphore()
    for step in range(1, clips):
        pl.semaphore_signal(barrier, inc=1, device_id={"clip": (clip + step) % clips}, device_id_type=MESH)
    greet("blk", clips - 1)

    sem_at = [0]

    def sem():
        sem_at[0] += 1
        return r.sems.at[sem_at[0] - 1]

    def local(source, target):
        return pltpu.make_async_copy(source, target, sem())

    def remote(source, target, where):
        return pltpu.make_async_remote_copy(
            src_ref=source, dst_ref=target, send_sem=sem(), recv_sem=sem(), device_id=where, device_id_type=MESH
        )

    own, other = pl.ds(0, rows), pl.ds(rows, rows)
    my_half = pl.ds(pl.multiple_of(core * half, half), half)
    its_half = pl.ds(pl.multiple_of((1 - core) * half, half), half)


    def hidden_loads(j):
        at = pl.ds(j * chunk, chunk)
        return (
            local(r.hidden_in.at[:, at], r.first.at[j % 2]),
            local(r.hidden_out.at[at, :], r.second.at[j % 2]),
        )

    act_here = local(r.act_three, r.cat_three.at[own])
    grad_here = local(r.cotangent, r.dy)
    act_here.start()
    grad_here.start()
    weights = {j: hidden_loads(j) for j in range(min(2, chunks))}
    for copies in weights.values():
        for copy in copies:
            copy.start()
    exchanged = {}
    three, mixed, two, att, grads = range(5)
    for name, (source, cat) in enumerate(((r.act_three, r.cat_three), (r.mixed, r.cat_mixed), (r.act_two, r.cat_two), (r.att, r.cat_att))):
        exchanged[name] = [remote(source, cat.at[other], pair)]
        if name != three:
            exchanged[name].append(local(source, cat.at[own]))
    exchanged[grads] = [
        remote(r.cotangent.at[:, its_half], r.cat_dy.at[other], pair),
        local(r.cotangent.at[:, my_half], r.cat_dy.at[own]),
    ]
    for name in (three, grads, mixed, two, att):
        for copy in exchanged[name]:
            copy.start()
    small = [
        local(source, into)
        for source, into in ((r.after_cross, r.value), (r.text_keys, r.tk), (r.text_values, r.tv), (r.cross_queries, r.cq))
    ]
    for copy in small:
        copy.start()
    act_here.wait()
    grad_here.wait()

    clip_bits = [("clip", k) for k in range(bits_of(clips))]
    blk_bits = [("blk", k) for k in range(bits_of(blks))]
    left = clip_bits[::-1] + blk_bits[::-1]
    orders = [clip_bits + blk_bits[1:], clip_bits[::-1] + blk_bits[1:]]
    early = [blk_bits[1:] + clip_bits, blk_bits[1:] + clip_bits[::-1]]
    pieces = []
    for p in range(2 * chunks + 3):
        wide = p < chunks or p >= 2 * chunks
        held = [r.wide_own, *r.wide] if wide else [r.tall_own, *r.tall]
        nth = (p if p < chunks else p - chunks) if wide else p - chunks
        order = early[EARLY.index(p) % 2] if p in EARLY else orders[(p - sum(q < p for q in EARLY)) % 2]
        pieces.append(
            Halving(left, order, [held[0].at[nth % chunks]] + [level.at[nth] for level in held[1:]], r.piece_sems.at[p])
        )

    def finish(p, out, column, rows_out):
        piece = pieces[p]
        size = piece.bufs[-1].shape[-1]
        base = core * half + column if p >= chunks and p < 2 * chunks else column + core * half
        at = pl.ds(pl.multiple_of(base, size), size)
        tall_piece = chunks <= p < 2 * chunks
        stage = r.tall_fix.at[p - chunks] if tall_piece else r.wide_fix.at[p if p < chunks else p - chunks]
        stage[...] = piece.bufs[-1][1 - core].astype(f32)
        copy = remote(stage, out.at[:, at], pair)
        copy.start()
        out[:, at] = piece.bufs[-1][core].astype(f32)
        return copy

    fixes = []

    def task(stage, p):
        if stage < stages:
            pieces[p].turn(stage)
        if stage == stages - 1:
            if p < chunks:
                fixes.append((p, finish(p, r.hidden_in_out, p * chunk, None)))
            elif p < 2 * chunks:
                fixes.append((p, finish(p, r.hidden_out_out, (p - chunks) * (half // chunks), None)))
            else:
                fixes.append((p, finish(p, (r.cross_out_out, r.cross_query_out, r.self_out_out)[p - 2 * chunks], 0, None)))

    total = len(pieces)
    at_point, reached = [0], [-2] * total

    def reach(stage, p):
        while reached[p] < stage:
            reached[p] += 1
            if reached[p] < 0:
                pieces[p].start()
            else:
                task(reached[p], p)

    def point():
        if at_point[0] < len(PLAN):
            for stage, p in PLAN[at_point[0]]:
                if p < total:
                    reach(stage, p)
        at_point[0] += 1

    def outer(cat_left, cat_right, into):
        entries, block = into.shape[:2]
        group = max(1, 256 // block)

        def part(m, carry):
            at = pl.ds(pl.multiple_of(m * group * block, group * block), group * block)
            made = matmul(cat_left[:, at], cat_right[...], (0, 0))
            into[pl.ds(m * group, group)] = made.reshape(group, block, made.shape[-1]).astype(bf16)
            return carry

        lax.fori_loop(0, entries // group, part, 0)

    swaps = {}
    sub = min(256, chunk)
    for j in range(chunks):
        for copy in weights[j]:
            copy.wait()
        first, second = r.first.at[j % 2], r.second.at[j % 2]
        pre_low = r.pre_low.at[j % 2]
        hidden = r.cat_hidden.at[own, pl.ds(j * chunk, chunk)]
        if j >= 2:
            swaps[j - 2][0].wait_send()

        def part(u, carry):
            at = pl.ds(pl.multiple_of(u * sub, sub), sub)
            pre = matmul(r.cat_three[own, :], first[:, at])
            grad = matmul(r.dy[...], second[at, :], (1, 1))
            phi = 0.5 * (1.0 + lax.erf(pre * math.sqrt(0.5)))
            slope = phi + pre * (jnp.exp(-0.5 * pre * pre) * (1.0 / math.sqrt(2.0 * math.pi)))
            hidden[:, at] = (pre * phi).astype(bf16)
            pre_low[:, at] = (grad * slope).astype(bf16)
            return carry

        lax.fori_loop(0, chunk // sub, part, 0)
        swaps[j] = (
            remote(pre_low.at[:, pl.ds(pl.multiple_of((1 - core) * (chunk // 2), chunk // 2), chunk // 2)], r.cat_pre.at[j, other], pair),
            remote(hidden, r.cat_hidden.at[other, pl.ds(j * chunk, chunk)], pair),
        )
        for copy in swaps[j]:
            copy.start()
        r.cat_pre[j, own, :] = pre_low[:, pl.ds(pl.multiple_of(core * (chunk // 2), chunk // 2), chunk // 2)]
        made = matmul(hidden[...], second[...])
        back = matmul(pre_low[...], first[...], (1, 1))
        if j == 0:
            r.total[...] = made
            r.grad[...] = back
        else:
            r.total[...] += made
            r.grad[...] += back
        if j + 2 < chunks:
            weights[j + 2] = hidden_loads(j + 2)
            for copy in weights[j + 2]:
                copy.start()
        point()
        if j == 0:
            for copy in exchanged[three]:
                copy.wait()
        else:
            swaps[j - 1][0].wait_recv()
            outer(r.cat_three, r.cat_pre.at[j - 1], pieces[j - 1].bufs[0])
            point()
    for j in (chunks - 2, chunks - 1):
        swaps[j][0].wait_send()
    later = [
        local(source, into.at[slot])
        for source, into, slot in ((r.cross_out, r.first, 0), (r.cross_query, r.second, 0), (r.self_out, r.first, 1))
    ]
    for copy in later:
        copy.start()
    swaps[chunks - 1][0].wait_recv()
    outer(r.cat_three, r.cat_pre.at[chunks - 1], pieces[chunks - 1].bufs[0])
    point()
    for copy in small:
        copy.wait()
    r.low[1] = (r.value[...] + r.total[...]).astype(bf16)
    output_copy = local(r.low.at[1], r.output)
    output_copy.start()
    for copy in exchanged[grads]:
        copy.wait()
    for j in range(chunks):
        swaps[j][1].wait()
    tall = half // chunks
    block = r.tall_own.shape[2]
    group = max(1, 512 // block)

    def tall_part(m, carry):
        at = pl.ds(pl.multiple_of(m * group * block, group * block), group * block)
        made = matmul(r.cat_hidden[:, at], r.cat_dy[...], (0, 0))
        for w in range(chunks):
            r.tall_own[w, pl.ds(m * group, group)] = made[:, w * tall : (w + 1) * tall].reshape(group, block, tall).astype(bf16)
        return carry

    turns = devices // group
    lax.fori_loop(0, turns // 2, tall_part, 0)
    point()
    lax.fori_loop(turns // 2, turns, tall_part, 0)
    point()

    def keep_two(at, value):
        r.total[at, :] = value
        r.low[0, at, :] = value.astype(bf16)

    norm_back(r.value, r.grad, r.gain_2[...], r.dy, keep_two, vec, 4)
    second_value = local(r.after_self, r.value)
    second_value.start()

    def share(which):
        copy = remote(r.low.at[which, :, its_half], r.cat_low.at[which, other], pair)
        copy.start()
        r.cat_low[which, own, :] = r.low[which, :, my_half]
        return copy

    shared = [share(0)]
    later[0].wait()
    output_copy.wait()
    r.dy[...] = matmul(r.low[0], r.first[0], (1, 1)).astype(bf16)
    point()
    lanes = min(128, depth)
    groups = lanes // width

    def cross(t, carry):
        at = pl.ds(pl.multiple_of(t * lanes, lanes), lanes)
        queries, keys, values, grads = r.cq[:, at], r.tk[:, at], r.tv[:, at], r.dy[:, at]
        query_sum = jnp.zeros((rows, lanes), f32)
        key_sum, value_sum = jnp.zeros((tokens, lanes), f32), jnp.zeros((tokens, lanes), f32)
        for h in range(lanes // HEAD):
            query_h, grad_h, key_h = head_only(queries, h), head_only(grads, h), head_only(keys, h)
            scores = matmul(keys, query_h, (1, 1)) * 0.125 + hidden_tokens
            scores = jnp.exp(scores - jnp.max(scores, axis=0, keepdims=True))
            prob = scores / jnp.sum(scores, axis=0, keepdims=True)
            dprob = matmul(values, grad_h, (1, 1))
            dscore = (prob * (dprob - jnp.sum(prob * dprob, axis=0, keepdims=True))).astype(bf16)
            query_sum = query_sum + matmul(dscore, key_h, (0, 0))
            key_sum = key_sum + matmul(dscore, query_h)
            value_sum = value_sum + matmul(prob.astype(bf16), grad_h)
        r.low[1, :, at] = (query_sum * 0.125).astype(bf16)
        for g in range(groups):
            r.kv_own[t * groups + g, :, :width] = (key_sum[:, g * width : (g + 1) * width] * 0.125).astype(bf16)
            r.kv_own[t * groups + g, :, width:] = value_sum[:, g * width : (g + 1) * width].astype(bf16)
        return carry

    turns = depth // lanes
    for quarter in range(4):
        lax.fori_loop(turns * quarter // 4, turns * (quarter + 1) // 4, cross, 0)
        point()
    text_load = local(r.text, r.tk)
    text_load.start()
    text_sum = Halving(blk_bits[::-1], blk_bits, [r.kv_own, *r.kv], r.kv_sems)
    text_sum.start()
    shared.append(share(1))
    point()
    later[1].wait()
    r.grad[...] = matmul(r.low[1], r.second[0], (1, 1))
    second_value.wait()
    shared[0].wait_send()

    def keep_one(at, value):
        r.total[at, :] = value
        r.low[0, at, :] = value.astype(bf16)

    norm_back(r.value, r.grad, r.gain_1[...], r.total, keep_one, vec, 2)
    point()
    for copy in (share_one := [remote(r.low.at[0, :, its_half], r.cat_low.at[2, other], pair)]):
        copy.start()
    r.cat_low[2, own, :] = r.low[0, :, my_half]
    later[2].wait()
    att_grad = matmul(r.low[0], r.first[1], (1, 1)).astype(bf16)
    for s in range(blks):
        r.grad_own[s] = att_grad[:, s * width : (s + 1) * width]

    block_sems = r.block_sems

    def fetch(peer, source):
        return pltpu.make_async_remote_copy(
            src_ref=r.grad_own.at[peer], dst_ref=r.grad_all.at[source], send_sem=block_sems.at[0, peer],
            recv_sem=block_sems.at[1, source], device_id={"blk": peer}, device_id_type=MESH,
        )

    def give(peer, source):
        return pltpu.make_async_remote_copy(
            src_ref=r.qkv_here.at[peer], dst_ref=r.sums_in.at[source], send_sem=block_sems.at[2, peer],
            recv_sem=block_sems.at[3, source], device_id={"blk": peer}, device_id_type=MESH,
        )

    for step in range(1, blks):
        fetch((me + step) % blks, me).start()
    r.grad_all[me] = r.grad_own[me]
    attention_inputs = [local(source, into) for source, into in ((r.qkv, r.qkv_here), (r.full, r.full_here), (r.lse, r.lse_rows))]
    for copy in attention_inputs:
        copy.start()
    projections = [
        local(source, into.at[slot])
        for source, into, slot in ((r.self_query, r.first, 0), (r.self_key, r.second, 0), (r.self_value, r.second, 1))
    ]
    text_weight = local(r.cross_key, r.first.at[1])
    for copy in (*projections, text_weight):
        copy.start()
    point()
    text_sum.turn(0)

    def last_pieces():
        for n, (name, cat, wait) in enumerate(((mixed, r.cat_mixed, shared[0]), (two, r.cat_two, shared[1]), (att, r.cat_att, share_one[0]))):
            for copy in exchanged[name]:
                copy.wait()
            wait.wait_recv() if n == 0 else wait.wait()
            if n < chunks:
                reach(0, n)
            outer(cat, r.cat_low.at[n], pieces[2 * chunks + n].bufs[0])
            point()

    last_pieces()
    text_done = text_sum.bufs[-1].at[0]
    text_rows = tokens // blks

    def swap_text(peer, source):
        return pltpu.make_async_remote_copy(
            src_ref=text_done.at[pl.ds(pl.multiple_of(peer * text_rows, text_rows), text_rows)], dst_ref=r.text_in.at[source],
            send_sem=block_sems.at[4, peer], recv_sem=block_sems.at[5, source], device_id={"blk": peer}, device_id_type=MESH,
        )

    clip_left = clip_bits[::-1] + blk_bits[::-1]
    text_w = Halving(clip_left, clip_bits[::-1], [r.text_w_own, *r.text_w], r.clip_sems.at[0])
    head_w = Halving(clip_left, clip_bits, [r.head_w_own, *r.head_w], r.clip_sems.at[1])

    def text_back(part):
        for s in range(blks):
            r.text_cat[:, s * width : (s + 1) * width] = r.text_in[s, :, part * width : (part + 1) * width]
        return matmul(r.text_cat[...], r.first[1], (1, 1))

    def text_ready():
        for step in range(1, blks):
            swap_text((me + step) % blks, me).start()
        r.text_in[me] = text_done[pl.ds(pl.multiple_of(me * text_rows, text_rows), text_rows), :]
        text_load.wait()
        outer(r.tk, text_done, r.text_w_own)
        text_w.start()

    for copy in attention_inputs:
        copy.wait()
    qkv, full = r.qkv_here, r.full_here
    for step in range(1, blks):
        fetch((me + step) % blks, (me + step) % blks).wait_recv()
    text_sum.turn(1)
    point()
    for i in range(blks):
        product = (r.grad_all[i].astype(f32) * full[i]).T
        for h in range(heads):
            r.delta_rows[i, h : h + 1, :] = jnp.sum(product[h * HEAD : (h + 1) * HEAD], axis=0, keepdims=True)

    full[...] = jnp.zeros_like(full)
    point()
    mask = causal(rows, True)

    r.pair_sum[...] = jnp.zeros_like(r.pair_sum)
    near = min(3 * width, rows)
    head_sums = [(r.value, 0, near)] + ([(r.grad, near, 3 * width - near)] if near < 3 * width else [])

    def update(i, j, masked):
        keys, values = qkv[j, :, width : 2 * width], qkv[j, :, 2 * width :]
        queries, grad = qkv[i, :, :width], r.grad_all[i]
        query_term = key_term = value_term = None
        for h in range(heads):
            query_h, grad_h, key_h = head_only(queries, h), head_only(grad, h), head_only(keys, h)
            scores = matmul(keys, query_h, (1, 1))
            probs = jnp.exp(scores - r.lse_rows[i, h : h + 1, :])
            if masked:
                probs = jnp.where(mask, probs, 0.0)
            dprobs = matmul(values, grad_h, (1, 1))
            dscores = (probs * (dprobs - r.delta_rows[i, h : h + 1, :])).astype(bf16)
            terms = matmul(dscores, key_h, (0, 0)), matmul(dscores, query_h), matmul(probs.astype(bf16), grad_h)
            query_term = terms[0] if h == 0 else query_term + terms[0]
            key_term = terms[1] if h == 0 else key_term + terms[1]
            value_term = terms[2] if h == 0 else value_term + terms[2]
        full[i] += query_term
        r.pair_sum[j, :, :width] += key_term
        r.pair_sum[j, :, width:] += value_term

    def block_of(turn):
        return turn + core * (blks - 1 - 2 * turn)

    def act_load(turn):
        return pltpu.make_async_copy(r.act_all.at[block_of(turn)], r.low.at[turn % 2], block_sems.at[6, turn])

    act_load(0).start()
    act_load(1).start()

    def attend_block(turn):
        block = block_of(turn)
        update(block, block, True)
        if turn + 1 < blks:
            lax.fori_loop(1, blks - turn, lambda n, held: (update(block + n * (1 - core), block - n * core, False), held)[1], 0)
        qkv[block, :, :width] = (full[block] * 0.125).astype(bf16)
        qkv[block, :, width:] = r.pair_sum[block].astype(bf16)

        @pl.when(block != me)
        def _():
            give(block, me).start()

        act_load(turn).wait()
        made = matmul(qkv[block], r.low[turn % 2], (0, 0))
        for ref, first, count in head_sums:
            if turn == 0:
                ref[:count] = made[first : first + count]
            else:
                ref[:count] += made[first : first + count]
        if turn + 2 < blks:
            act_load(turn + 2).start()

    for j in range(blks):
        attend_block(j)
        if j == 1:
            for stage in range(2, len(blk_bits)):
                text_sum.turn(stage)
            text_ready()
        if j == 4:
            text_w.turn(0)
        if j == 5:
            for step in range(1, blks):
                swap_text((me + step) % blks, (me + step) % blks).wait_recv()
            text_weight.wait()
            r.text_grad[...] = text_back(0)
            text_weight = local(r.cross_value, r.first.at[1])
            text_weight.start()
        point()
    for stage in range(1, len(clip_bits)):
        text_w.turn(stage)
    r.sums_in[me] = r.qkv_here[me]
    for ref, first, count in head_sums:
        turned = ref[:count].T
        r.head_w_own[:, :, first : first + count] = turned.reshape(devices, -1, count).astype(bf16)
    head_w.start()

    def swap_w(summed, out, base, peer, source):
        return pltpu.make_async_remote_copy(
            src_ref=summed.bufs[-1].at[peer], dst_ref=out.at[source], send_sem=block_sems.at[base, peer],
            recv_sem=block_sems.at[base + 1, source], device_id={"blk": peer}, device_id_type=MESH,
        )

    for step in range(1, blks):
        swap_w(text_w, r.text_w_out, 7, (me + step) % blks, me).start()
    r.text_w_out[me] = text_w.bufs[-1][me]
    for copy in projections:
        copy.wait()
    first_value = local(r.frames, r.dy)
    first_value.start()
    for step in range(1, blks):
        give((me + step) % blks, (me + step) % blks).wait_recv()
    grad_rows = [r.low.at[0], r.low.at[1], r.cq]
    for s in range(blks):
        for t in range(3):
            grad_rows[t][:, s * width : (s + 1) * width] = r.sums_in[s, :, t * width : (t + 1) * width]
    point()
    head_w.turn(0)
    r.grad[...] = matmul(grad_rows[0][...], r.first[0], (1, 1))
    r.grad[...] += matmul(grad_rows[1][...], r.second[0], (1, 1))
    r.grad[...] += matmul(grad_rows[2][...], r.second[1], (1, 1))
    first_value.wait()
    text_weight.wait()
    r.text_grad[...] += text_back(1)
    point()

    def keep_frames(at, value):
        r.value[at, :] = value

    norm_back(r.dy, r.grad, r.gain_0[...], r.total, keep_frames, vec, 0)
    frames_copy = local(r.value, r.frames_grad)
    frames_copy.start()
    vec[6:8, :] = jnp.zeros((2, depth), f32)
    part = depth // clips

    def swap_vec(peer, source):
        return pltpu.make_async_remote_copy(
            src_ref=vec.at[:, pl.ds(pl.multiple_of(peer * part, part), part)], dst_ref=r.vec_in.at[source],
            send_sem=r.vec_sems.at[0, peer], recv_sem=r.vec_sems.at[1, source], device_id={"clip": peer}, device_id_type=MESH,
        )

    for step in range(1, clips):
        swap_vec((clip + step) % clips, clip).start()
    r.vec_in[clip] = vec[:, pl.ds(pl.multiple_of(clip * part, part), part)]
    for stage in range(1, len(clip_bits)):
        head_w.turn(stage)
    for step in range(1, blks):
        swap_w(head_w, r.head_w_out, 9, (me + step) % blks, me).start()
    r.head_w_out[me] = head_w.bufs[-1][me]
    point()
    for step in range(1, clips):
        swap_vec((clip + step) % clips, (clip + step) % clips).wait_recv()
    r.vec_sum[me] = jnp.sum(r.vec_in[...], axis=0)

    def share_vec(peer, source):
        return pltpu.make_async_remote_copy(
            src_ref=r.vec_sum.at[me], dst_ref=r.vec_sum.at[source], send_sem=block_sems.at[11, peer],
            recv_sem=block_sems.at[12, source], device_id={"blk": peer}, device_id_type=MESH,
        )

    for step in range(1, blks):
        share_vec((me + step) % blks, me).start()
    for stage in range(stages):
        for p in range(total):
            reach(stage, p)
    for step in range(1, blks):
        share_vec((me + step) % blks, (me + step) % blks).wait_recv()
    summed = jnp.sum(r.vec_sum[...], axis=0)
    share_own = depth // devices
    turned = pltpu.roll(summed, (summed.shape[-1] - me * share_own) % summed.shape[-1], 1)
    for n, out in enumerate((r.vec_0, r.vec_1, r.vec_2, r.vec_3, r.vec_4, r.vec_5)):
        out[...] = turned[n : n + 1, :share_own]
    for _, copy in fixes:
        copy.wait()
    frames_copy.wait()
    for step in range(1, clips):
        swap_vec((clip + step) % clips, clip).wait_send()
    for step in range(1, blks):
        peer = (me + step) % blks
        fetch(peer, me).wait_send()
        give(peer, me).wait_send()
        swap_text(peer, me).wait_send()
        for summed, out, base in ((text_w, r.text_w_out, 7), (head_w, r.head_w_out, 9)):
            swap_w(summed, out, base, peer, me).wait_send()
            swap_w(summed, out, base, peer, peer).wait_recv()
        share_vec(peer, me).wait_send()
    stored = []
    for parts, outs in ((r.head_w_out, (r.query_w, r.key_w, r.value_w)), (r.text_w_out, (r.text_key_w, r.text_value_w))):
        for t, out in enumerate(outs):
            stage = r.grad.at[pl.ds(len(stored) * share_own, share_own)]
            for s in range(blks):
                stage[:, s * width : (s + 1) * width] = parts[s, :, t * width : (t + 1) * width].astype(f32)
            stored.append(local(stage, out))
            stored[-1].start()
    for copy in stored:
        copy.wait()


def backward(inputs, gains, lengths, clips, blks):
    rows, depth = inputs["frames"].shape
    tokens = inputs["text"].shape[0]
    hidden = inputs["hidden_in"].shape[1]
    devices, width, half = clips * blks, depth // blks, depth // 2
    chunk = min(1024, hidden)
    chunks = hidden // chunk
    own = depth // devices
    tall = half // chunks
    stages = bits_of(clips) + bits_of(blks) - 1
    bf16, f32 = jnp.bfloat16, jnp.float32
    hbm, vmem = pl.BlockSpec(memory_space=pltpu.MemorySpace.HBM), pl.BlockSpec(memory_space=pltpu.VMEM)
    dma = pltpu.SemaphoreType.DMA
    shape = jax.ShapeDtypeStruct
    row = shape((own, depth), f32)
    outs = dict(
        output=shape((rows, depth), bf16), frames_grad=shape((rows, depth), f32), text_grad=shape((tokens // blks, depth), f32),
        query_w=row, key_w=row, value_w=row, self_out_out=row, cross_query_out=row, text_key_w=row, text_value_w=row, cross_out_out=row,
        hidden_in_out=shape((own, hidden), f32), hidden_out_out=shape((hidden // devices, depth), f32),
        **{f"vec_{n}": shape((1, own), f32) for n in range(6)},
    )
    scratch = dict(
        first=((2, depth, chunk), bf16), second=((2, chunk, depth), bf16),
        cat_three=((2 * rows, depth), bf16), cat_mixed=((2 * rows, depth), bf16), cat_two=((2 * rows, depth), bf16),
        cat_att=((2 * rows, depth), bf16), cat_dy=((2 * rows, half), bf16), dy=((rows, depth), bf16),
        cat_hidden=((2 * rows, hidden), bf16), pre_low=((2, rows, chunk), bf16), cat_pre=((chunks, 2 * rows, chunk // 2), bf16),
        total=((rows, depth), f32), grad=((rows, depth), f32), value=((rows, depth), f32),
        low=((2, rows, depth), bf16), cat_low=((3, 2 * rows, half), bf16),
        cq=((rows, depth), bf16), tk=((tokens, depth), bf16), tv=((tokens, depth), bf16),
        vec=((8, depth), f32), vec_in=((clips, 8, depth // clips), f32), vec_sum=((blks, 8, depth // clips), f32),
        wide_own=((chunks, devices, own, half), bf16), tall_own=((chunks, devices, hidden // devices, tall), bf16),
        wide_fix=((chunks + 3, own, half), f32), tall_fix=((chunks, hidden // devices, tall), f32),
        text_in=((blks, tokens // blks, 2 * width), bf16), text_cat=((tokens // blks, depth), bf16),
        head_w_out=((blks, own, 3 * width), bf16), text_w_out=((blks, own, 2 * width), bf16),
        pair_sum=((blks, rows, 2 * width), f32),
        kv_own=((blks, tokens, 2 * width), bf16),
        head_w_own=((devices, own, 3 * width), bf16), text_w_own=((devices, own, 2 * width), bf16),
        grad_own=((blks, rows, width), bf16), grad_all=((blks, rows, width), bf16), sums_in=((blks, rows, 3 * width), bf16), qkv_here=((blks, rows, 3 * width), bf16), full_here=((blks, rows, width), f32),
        lse_rows=((blks, 8, rows), f32), delta_rows=((blks, 8, rows), f32),

    )
    levels = [((chunks + 3, devices >> (s + 1), own, half), bf16) for s in range(stages)]
    levels += [((chunks, devices >> (s + 1), hidden // devices, tall), bf16) for s in range(stages)]
    levels += [((blks >> (s + 1), tokens, 2 * width), bf16) for s in range(bits_of(blks))]
    for parts in (3, 2):
        levels += [((devices >> (s + 1), own, parts * width), bf16) for s in range(bits_of(clips))]
    sems = dict(
        sems=(160,), piece_sems=(2 * chunks + 3, 2, stages), kv_sems=(2, bits_of(blks)), block_sems=(13, blks),
        clip_sems=(2, 2, bits_of(clips)), vec_sems=(2, clips),
    )
    small = dict(lengths=lengths, gain_0=gains[0], gain_1=gains[1], gain_2=gains[2])
    names = [*inputs, *small, *outs, *scratch, *sems]
    made = pl.pallas_call(
        partial(tail_kernel, names, bits_of(clips), bits_of(blks)),
        out_shape=list(outs.values()),
        in_specs=[hbm] * len(inputs) + [pl.BlockSpec(memory_space=pltpu.SMEM)] + [vmem] * 3,
        out_specs=[hbm if i in (0, 1, 3, 4, 5, 8, 9) else vmem for i in range(len(outs))],
        scratch_shapes=[pltpu.VMEM(*v) for v in scratch.values()] + [dma(v) for v in sems.values()] + [pltpu.VMEM(*v) for v in levels],
        compiler_params=pltpu.CompilerParams(collective_id=3, has_side_effects=True, vmem_limit_bytes=63 << 20),
    )(*inputs.values(), *small.values())
    return SimpleNamespace(**dict(zip(outs, made)))


def collect_kernel(*refs):
    count = len(refs) // 2
    for n in range(count):
        refs[count + n][...] = refs[n][...]


def collect(*arrays):
    vmem = pl.BlockSpec(memory_space=pltpu.VMEM)
    return pl.pallas_call(
        collect_kernel,
        out_shape=[jax.ShapeDtypeStruct(a.shape, a.dtype) for a in arrays],
        in_specs=[vmem] * len(arrays),
        out_specs=[vmem] * len(arrays),
        compiler_params=pltpu.CompilerParams(vmem_limit_bytes=32 << 20),
    )(*arrays)


def body(
    frames,
    text_states,
    prompt_lengths,
    cotangent,
    self_query,
    self_key,
    self_value,
    self_out,
    cross_query,
    cross_key,
    cross_value,
    cross_out,
    hidden_in,
    hidden_out,
    first_gain,
    first_shift,
    second_gain,
    second_shift,
    third_gain,
    third_shift,
):
    block_total, clip_total = lax.axis_size("blk"), lax.axis_size("clip")
    block_rank = lax.axis_index("blk")
    own = D // (clip_total * block_total)
    head_width = D // block_total
    local_text = text_states[0]
    projections = (self_query, self_key, self_value)
    if head_width % 128:
        projections = [lax.dynamic_slice_in_dim(matrix, block_rank * head_width, head_width, 1) for matrix in projections]
    norms = [v.reshape(1, D) for v in (first_gain, second_gain, third_gain, first_shift, second_shift, third_shift)]
    weights = dict(
        text=local_text, cross_key=cross_key, cross_value=cross_value, self_out=self_out, cross_query=cross_query, cross_out=cross_out
    )
    kept = forward(frames[0], projections, norms, prompt_lengths, weights, block_total)
    inputs = dict(
        act_three=kept.act_three, cotangent=cotangent[0], hidden_in=hidden_in, hidden_out=hidden_out, mixed=kept.mixed, act_two=kept.act_two,
        att=kept.att, after_cross=kept.after_cross, after_self=kept.after_self, frames=frames[0], text=local_text, text_keys=kept.tk,
        text_values=kept.tv, cross_queries=kept.cross_queries, cross_out=cross_out, cross_query=cross_query, self_out=self_out,
        self_query=self_query, self_key=self_key, self_value=self_value, qkv=kept.qkv, full=kept.full, lse=kept.lse, act_all=kept.act_all,
        cross_key=cross_key, cross_value=cross_value,
    )
    made = backward(inputs, norms[:3], prompt_lengths, clip_total, block_total)
    frames_grad, text_grad = made.frames_grad[None], made.text_grad[None]
    sums = [
        made.query_w, made.key_w, made.value_w, made.self_out_out, made.cross_query_out, made.text_key_w, made.text_value_w,
        made.cross_out_out, made.hidden_in_out, made.hidden_out_out,
    ]
    vectors = [v.reshape(own) for v in (made.vec_0, made.vec_1, made.vec_2, made.vec_3, made.vec_4, made.vec_5)]
    return (*collect(made.output[None], frames_grad, text_grad, *sums, *vectors),)


def solution(mesh):
    in_specs = (
        P("clip", "blk", None),
        P("clip", None, None),
        P("clip"),
        P("clip", "blk", None),
        P(),
        P(),
        P(),
        P(),
        P(),
        P(),
        P(),
        P(),
        P(),
        P(),
        P(),
        P(),
        P(),
        P(),
        P(),
        P(),
    )
    out_specs = (
        P("clip", "blk", None),
        P("clip", "blk", None),
        P("clip", "blk", None),
        P(("clip", "blk"), None),
        P(("clip", "blk"), None),
        P(("clip", "blk"), None),
        P(("clip", "blk"), None),
        P(("clip", "blk"), None),
        P(("clip", "blk"), None),
        P(("clip", "blk"), None),
        P(("clip", "blk"), None),
        P(("clip", "blk"), None),
        P(("clip", "blk"), None),
        P(("clip", "blk")),
        P(("clip", "blk")),
        P(("clip", "blk")),
        P(("clip", "blk")),
        P(("clip", "blk")),
        P(("clip", "blk")),
    )
    return jax.shard_map(body, mesh=mesh, in_specs=in_specs, out_specs=out_specs, check_vma=False)
```
